128 devices in a mesh: strip: 128 (over x, y, z, core).
Axes of the slice: x: 4, y: 4, z: 4, core: 2. Of those that a mesh axis runs over, the one named last changes fastest.
Arguments:
- params: float32 [59, 655360], P(None, 'strip'), may hold values from -26 to 26, as said below
- camera: float32 [4, 12], replicated, may hold values from -2 to 2, as said below
- send_index: int32 [16384, 80], P('strip'), may hold values from 0 to 5119, as said below
- send_count: int32 [16384], P('strip'), may hold values from 0 to 80, as said below
- tile_list: int32 [5120, 128], P('strip'), may hold values from 0 to 5119, as said below
- target: float32 [3, 2048, 640], P(None, 'strip'), may hold values from 0 to 1
Outputs:
- param_grads: float32 [59, 655360], P(None, 'strip')
The draws below stay inside these ranges and needn't reach their ends.
Inputs may be any that keep to these rules, and one draw needn't show every extreme that they name: `send_index`: in row s * 128 + r the first send_count[s * 128 + r] entries are distinct local Gaussian numbers of device s; over all r these live entries name each of device s's 5120 Gaussians exactly once. Later entries are local Gaussian numbers that name nothing sent. `send_count`: for every sender, and for every strip, the counts sum to 5120; the largest count equals 80. `tile_list`: each row holds 128 distinct received numbers of its strip; every number 0 to 5119 of a strip stands in exactly one of the strip's lists. `params`: each Gaussian lies 2 to 6 in front of the camera of the view of the strip that receives it and projects inside the tile whose list holds it; entry 6 of every Gaussian is 1 or more. `camera`: the first nine entries of each row form a rotation matrix.
All inputs are finite; a program needn't handle non-finite values.
Results may differ from the reference program's by a relative error of at most 0.0003.
Values sent between devices are 32-bit elements; how exact they have to be, the bound alone decides.
No kernel may reach another device: no remote copies, remote signals or barrier semaphores. Data moves between devices by JAX's collectives and lax.ppermute only.
A program may use at most 64 MiB of HBM per device.

```python
import math
import jax
import jax.numpy as jnp
from jax import lax

TILE_ROWS = 1
IMG_W = 640
VIEWS = 4
LIST = 128
PARAMS = 59
TILES_DEV = 40
G_DEV = 5120
CAP = 80
GAUSS = 655360
TILES = 5120
ROWS = 2048
VIEW_ROWS = 512
N_STRIP = 128


def camera_table(key):
    first, second = jax.random.split(jax.random.fold_in(key, 202))
    raw = jax.random.uniform(first, (VIEWS, 4), jnp.float32, -1.0, 1.0)
    raw = raw.at[:, 0].add(2.0)
    versor = raw / jnp.sqrt(jnp.sum(raw * raw, axis=1, keepdims=True))
    real, imag_x, imag_y, imag_z = (versor[:, 0], versor[:, 1], versor[:, 2], versor[:, 3])
    rows = jnp.stack([1.0 - 2.0 * (imag_y * imag_y + imag_z * imag_z), 2.0 * (imag_x * imag_y - real * imag_z), 2.0 * (imag_x * imag_z + real * imag_y), 2.0 * (imag_x * imag_y + real * imag_z), 1.0 - 2.0 * (imag_x * imag_x + imag_z * imag_z), 2.0 * (imag_y * imag_z - real * imag_x), 2.0 * (imag_x * imag_z - real * imag_y), 2.0 * (imag_y * imag_z + real * imag_x), 1.0 - 2.0 * (imag_x * imag_x + imag_y * imag_y)], axis=1)
    shift = jax.random.uniform(second, (VIEWS, 3), jnp.float32, -1.0, 1.0)
    return jnp.concatenate([rows, shift], axis=1)


def routing(key):
    strips = N_STRIP
    mean_load = G_DEV // strips
    quarter = mean_load // 4
    keys = jax.random.split(jax.random.fold_in(key, 101), 6)

    def wave(subkey):
        heights = jax.random.randint(subkey, (strips,), -quarter, quarter + 1, dtype=jnp.int32)
        heights = heights.at[0].set(quarter).at[1].set(-quarter)
        return heights - jnp.roll(heights, -1)
    rise = wave(keys[0])
    fall = wave(keys[1])
    source = jnp.arange(strips, dtype=jnp.int32)[:, None]
    dest_strip = jnp.arange(strips, dtype=jnp.int32)[None, :]
    base = mean_load + rise[(dest_strip - source) % strips] + fall[(dest_strip + source) % strips]
    row_order = jax.random.permutation(keys[2], strips)
    col_order = jax.random.permutation(keys[3], strips)
    loads = base[row_order][:, col_order].astype(jnp.int32)
    orders = jax.vmap(lambda subkey: jax.random.permutation(subkey, G_DEV))(jax.random.split(keys[4], strips)).astype(jnp.int32)
    starts = jnp.cumsum(loads, axis=1) - loads
    slot = jnp.arange(CAP, dtype=jnp.int32)
    position = (starts[:, :, None] + slot[None, None, :]) % G_DEV
    sends = jax.vmap(lambda order, place: order[place])(orders, position)
    inverse = jax.vmap(lambda order: jnp.zeros((G_DEV,), jnp.int32).at[order].set(jnp.arange(G_DEV, dtype=jnp.int32)))(orders)
    ends = starts + loads
    dest = jax.vmap(lambda edge, place: jnp.searchsorted(edge, place, side='right'))(ends, inverse).astype(jnp.int32)
    within = inverse - jnp.take_along_axis(starts, dest, axis=1)
    in_starts = jnp.cumsum(loads, axis=0) - loads
    compact = jnp.take_along_axis(in_starts, dest, axis=1) + within
    arrange = jax.vmap(lambda subkey: jax.random.permutation(subkey, G_DEV))(jax.random.split(keys[5], strips)).astype(jnp.int32)
    place_of = jax.vmap(lambda order: jnp.zeros((G_DEV,), jnp.int32).at[order].set(jnp.arange(G_DEV, dtype=jnp.int32)))(arrange)
    tile = place_of[dest, compact] // LIST
    return (loads, sends, arrange, dest, tile)


def draw_send_index(key, part):
    return routing(key)[1].reshape(N_STRIP * N_STRIP, CAP)


def draw_send_count(key, part):
    return routing(key)[0].reshape(N_STRIP * N_STRIP)


def draw_tile_list(key, part):
    return routing(key)[2].reshape(TILES, LIST)


def draw_camera(key, part):
    return camera_table(key)


def draw_params(key, part):
    loads, sends, arrange, dest, tile = routing(key)
    camera = camera_table(key)
    per_view = N_STRIP // VIEWS
    tile_cols = IMG_W // 16
    noise = jax.random.split(jax.random.fold_in(key, 303), 8)
    shape = (N_STRIP, G_DEV)
    logical = (dest + per_view // 2) % N_STRIP
    view = logical // per_view
    pixel_x = (tile % tile_cols * 16).astype(jnp.float32) + jax.random.uniform(noise[0], shape, jnp.float32, 2.0, 14.0)
    pixel_y = ((logical % per_view * TILE_ROWS + tile // tile_cols) * 16).astype(jnp.float32) + jax.random.uniform(noise[1], shape, jnp.float32, 2.0, 14.0)
    depth = jax.random.uniform(noise[2], shape, jnp.float32, 2.0, 6.0)
    focal = 0.5 * IMG_W
    placed = [(pixel_x - 0.5 * IMG_W) / focal * depth, (pixel_y - 0.5 * VIEW_ROWS) / focal * depth, depth]
    rows = camera[view]
    relative = [placed[axis] - rows[:, :, 9 + axis] for axis in range(3)]
    mean = [rows[:, :, col] * relative[0] + rows[:, :, 3 + col] * relative[1] + rows[:, :, 6 + col] * relative[2] for col in range(3)]
    sigma = jax.random.uniform(noise[3], (3,) + shape, jnp.float32, 1.5, 4.0)
    logit = jax.random.uniform(noise[4], shape, jnp.float32, -5.0, -1.5)
    first_band = jax.random.uniform(noise[5], (3,) + shape, jnp.float32, -1.0, 1.0)
    higher = jax.random.uniform(noise[6], (45,) + shape, jnp.float32, -0.4, 0.4)
    log_scale = jnp.log(sigma * depth[None] / focal)
    quaternion = jax.random.uniform(noise[7], (4,) + shape, jnp.float32, -1.0, 1.0)
    quaternion = quaternion.at[0].set(jnp.abs(quaternion[0]) + 1.0)
    stacked = jnp.concatenate([jnp.stack(mean), log_scale, quaternion, logit[None], first_band, higher], axis=0)
    return stacked.reshape(PARAMS, GAUSS).astype(jnp.float32)


def shard_levels(key, dims, cuts, smallest, high):
    factor_of = 1.0
    for dim, parts in cuts:
        steps = jax.random.uniform(jax.random.fold_in(jax.random.fold_in(key, 6), dim), (parts,), jnp.float32, smallest / len(cuts), high / len(cuts))
        factor_of = factor_of * jnp.repeat(jnp.exp(steps), dims[dim] // parts).reshape((-1,) + (1,) * (len(dims) - 1 - dim))
    return factor_of


def setup_inputs(seed: int = 0) -> dict:
    seeds = jax.random.split(jax.random.key(seed), 7)
    params = draw_params(jax.random.fold_in(seeds[6], 71), 0)
    camera = draw_camera(jax.random.fold_in(seeds[6], 71), 0)
    send_index = draw_send_index(jax.random.fold_in(seeds[6], 71), 0)
    send_count = draw_send_count(jax.random.fold_in(seeds[6], 71), 0)
    tile_list = draw_tile_list(jax.random.fold_in(seeds[6], 71), 0)
    target = jnp.clip(1.0 * jax.random.uniform(seeds[5], (3, ROWS, IMG_W), jnp.float32) ** shard_levels(seeds[5], (3, ROWS, IMG_W), ((1, 128),), -0.2, 0.2), 0.0, 1.0)
    return {"params": params, "camera": camera, "send_index": send_index, "send_count": send_count, "tile_list": tile_list, "target": target}


exact_dot = lax.Precision.HIGHEST
harmonic_zero = 0.28209479177387814
harmonic_one = 0.4886025119029199
harmonic_two = (1.0925484305920792, -1.0925484305920792, 0.31539156525252005, -1.0925484305920792, 0.5462742152960396)
harmonic_three = (-0.5900435899266435, 2.890611442640554, -0.4570457994644658, 0.3731763325901154, -0.4570457994644658, 1.445305721320277, -0.5900435899266435)
light_term = 0.0001
contrast_term = 0.0009

def harmonics(along_x, along_y, along_z):
    square_x = along_x * along_x
    square_y = along_y * along_y
    square_z = along_z * along_z
    return [harmonic_zero + 0.0 * along_x, -harmonic_one * along_y, harmonic_one * along_z, -harmonic_one * along_x, harmonic_two[0] * along_x * along_y, harmonic_two[1] * along_y * along_z, harmonic_two[2] * (2.0 * square_z - square_x - square_y), harmonic_two[3] * along_x * along_z, harmonic_two[4] * (square_x - square_y), harmonic_three[0] * along_y * (3.0 * square_x - square_y), harmonic_three[1] * along_x * along_y * along_z, harmonic_three[2] * along_y * (4.0 * square_z - square_x - square_y), harmonic_three[3] * along_z * (2.0 * square_z - 3.0 * square_x - 3.0 * square_y), harmonic_three[4] * along_x * (4.0 * square_z - square_x - square_y), harmonic_three[5] * along_z * (square_x - square_y), harmonic_three[6] * along_x * (square_x - 3.0 * square_y)]

def project(params, camera, focal, centre_x, centre_y, alive):
    rotation = [[camera[3 * row + col] for col in range(3)] for row in range(3)]
    mean = [params[axis] for axis in range(3)]
    placed = [rotation[row][0] * mean[0] + rotation[row][1] * mean[1] + rotation[row][2] * mean[2] + camera[9 + row] for row in range(3)]
    depth = placed[2]
    if alive is not None:
        depth = jnp.where(alive, depth, 1.0)
    inverse = 1.0 / depth
    screen_x = focal * placed[0] * inverse + centre_x
    screen_y = focal * placed[1] * inverse + centre_y
    quaternion = params[6:10]
    versor = quaternion * lax.rsqrt(lax.optimization_barrier(jnp.sum(quaternion * quaternion, axis=0)))
    real, imag_x, imag_y, imag_z = (versor[0], versor[1], versor[2], versor[3])
    turn = [[1.0 - 2.0 * (imag_y * imag_y + imag_z * imag_z), 2.0 * (imag_x * imag_y - real * imag_z), 2.0 * (imag_x * imag_z + real * imag_y)], [2.0 * (imag_x * imag_y + real * imag_z), 1.0 - 2.0 * (imag_x * imag_x + imag_z * imag_z), 2.0 * (imag_y * imag_z - real * imag_x)], [2.0 * (imag_x * imag_z - real * imag_y), 2.0 * (imag_y * imag_z + real * imag_x), 1.0 - 2.0 * (imag_x * imag_x + imag_y * imag_y)]]
    scales = jnp.exp(params[3:6])
    jacobian = [[focal * inverse, 0.0 * inverse, -focal * placed[0] * inverse * inverse], [0.0 * inverse, focal * inverse, -focal * placed[1] * inverse * inverse]]
    facing = [[jacobian[row][0] * rotation[0][col] + jacobian[row][1] * rotation[1][col] + jacobian[row][2] * rotation[2][col] for col in range(3)] for row in range(2)]
    stretch = [[(facing[row][0] * turn[0][col] + facing[row][1] * turn[1][col] + facing[row][2] * turn[2][col]) * scales[col] for col in range(3)] for row in range(2)]
    cov_xx = stretch[0][0] * stretch[0][0] + stretch[0][1] * stretch[0][1] + stretch[0][2] * stretch[0][2] + 0.3
    cov_xy = stretch[0][0] * stretch[1][0] + stretch[0][1] * stretch[1][1] + stretch[0][2] * stretch[1][2]
    cov_yy = stretch[1][0] * stretch[1][0] + stretch[1][1] * stretch[1][1] + stretch[1][2] * stretch[1][2] + 0.3
    determinant = cov_xx * cov_yy - cov_xy * cov_xy
    safe = [placed[0], placed[1], depth]
    length = jnp.sqrt(safe[0] * safe[0] + safe[1] * safe[1] + safe[2] * safe[2])
    heading = [(rotation[0][col] * safe[0] + rotation[1][col] * safe[1] + rotation[2][col] * safe[2]) / length for col in range(3)]
    basis = jnp.stack(harmonics(heading[0], heading[1], heading[2]))
    coefficients = params[11:59].reshape(16, 3, -1)
    colour = 0.5 + lax.optimization_barrier(jnp.sum(basis[:, None, :] * coefficients, axis=0))
    opacity = jax.nn.sigmoid(params[10])
    return jnp.stack([screen_x, screen_y, cov_yy / determinant, -cov_xy / determinant, cov_xx / determinant, colour[0], colour[1], colour[2], opacity])

def blend_tiles(footprint, anchor_x, anchor_y):
    pixel = jnp.arange(256, dtype=jnp.int32)
    inside_x = (pixel % 16).astype(jnp.float32) + 0.5
    inside_y = (pixel // 16).astype(jnp.float32) + 0.5
    apart_x = anchor_x[:, None, None] + inside_x[None, :, None] - footprint[0][:, None, :]
    apart_y = anchor_y[:, None, None] + inside_y[None, :, None] - footprint[1][:, None, :]
    power = -0.5 * (footprint[2][:, None, :] * apart_x * apart_x + footprint[4][:, None, :] * apart_y * apart_y) - footprint[3][:, None, :] * apart_x * apart_y
    alpha = footprint[8][:, None, :] * jnp.exp(power)
    passed = jnp.log1p(-alpha)
    before = jnp.cumsum(passed, axis=2) - passed
    weight = alpha * jnp.exp(before)
    return jnp.einsum('tpl,ctl->ctp', weight, footprint[5:8], precision=exact_dot)

def window_weights():
    offsets = jnp.arange(11, dtype=jnp.float32) - 5.0
    raw = jnp.exp(-offsets * offsets / 4.5)
    return raw / jnp.sum(raw)

def smooth(field, weights, out_rows):
    width = field.shape[2]
    total = weights[0] * field[:, 0:out_rows, :]
    for shift in range(1, 11):
        total = total + weights[shift] * field[:, shift:shift + out_rows, :]
    padded = jnp.pad(total, ((0, 0), (0, 0), (5, 5)))
    result = weights[0] * padded[:, :, 0:width]
    for shift in range(1, 11):
        result = result + weights[shift] * padded[:, :, shift:shift + width]
    return result

def similarity(mean_x, mean_y, power_x, power_y, cross):
    var_x = power_x - mean_x * mean_x
    var_y = power_y - mean_y * mean_y
    covar = cross - mean_x * mean_y
    upper = (2.0 * mean_x * mean_y + light_term) * (2.0 * covar + contrast_term)
    lower = (mean_x * mean_x + mean_y * mean_y + light_term) * (var_x + var_y + contrast_term)
    return upper / lower

def pad_rows(field):
    return jnp.pad(field, ((0, 0), (5, 5), (0, 0)))

def reference(params, camera, send_index, send_count, tile_list, target):
    strips = N_STRIP
    per_view = strips // VIEWS
    offset = per_view // 2
    width = IMG_W
    focal = 0.5 * width
    counts = send_count.reshape(strips, strips)
    sends = send_index.reshape(strips, strips, CAP)
    lists = tile_list.reshape(strips, TILES_DEV * LIST)
    tile_cols = width // 16
    tile_num = jnp.arange(TILES_DEV, dtype=jnp.int32)
    anchor_x = (tile_num % tile_cols * 16).astype(jnp.float32)
    block = math.gcd(16, TILES_DEV)
    groups = TILES_DEV // block
    weights = window_weights()

    def render_strip(values, strip):
        counts_in = counts[:, strip]
        keys = lists[strip]
        ends = jnp.cumsum(counts_in)
        before = ends[None, :] <= keys[:, None]
        source = lax.optimization_barrier(jnp.sum(before.astype(jnp.int32), axis=1))
        start = lax.optimization_barrier(jnp.sum(jnp.where(before, counts_in[None, :], 0), axis=1))
        local = sends[source, strip, keys - start]
        entries = values[:, source * G_DEV + local]
        position = (strip + offset) % strips
        camera_row = lax.dynamic_index_in_dim(camera, position // per_view, 0, keepdims=False)[:, None]
        footprint = project(entries, camera_row, focal, 0.5 * width, 0.5 * VIEW_ROWS, None)
        anchor_y = ((position % per_view * TILE_ROWS + tile_num // tile_cols) * 16).astype(jnp.float32)
        feet = footprint.reshape(9, groups, block, LIST).transpose(1, 0, 2, 3)
        colours = lax.map(lambda item: jax.checkpoint(blend_tiles)(item[0], item[1], item[2]), (feet, anchor_x.reshape(groups, block), anchor_y.reshape(groups, block)))
        flat = colours.transpose(1, 0, 2, 3).reshape(3, TILE_ROWS, tile_cols, 16, 16)
        return flat.transpose(0, 1, 3, 2, 4).reshape(3, 16 * TILE_ROWS, width)

    def total_loss(values):
        images = lax.map(lambda strip: jax.checkpoint(render_strip)(values, strip), jnp.arange(strips, dtype=jnp.int32))
        images = jnp.roll(images, offset, axis=0)
        rendered = images.transpose(1, 0, 2, 3).reshape(3 * VIEWS, VIEW_ROWS, width)
        seen = jnp.roll(target, offset * 16 * TILE_ROWS, axis=1).reshape(3 * VIEWS, VIEW_ROWS, width)
        whole = pad_rows(rendered)
        truth = pad_rows(seen)
        score = similarity(smooth(whole, weights, VIEW_ROWS), smooth(truth, weights, VIEW_ROWS), smooth(whole * whole, weights, VIEW_ROWS), smooth(truth * truth, weights, VIEW_ROWS), smooth(whole * truth, weights, VIEW_ROWS))
        return jnp.sum(1.0 - score)
    return jax.grad(total_loss)(params)
```

```python
import numpy as np

import jax
import jax.numpy as jnp
from jax import lax
from jax.experimental import pallas as pl
from jax.experimental.pallas import tpu as pltpu
from jax.sharding import PartitionSpec as P

VIEWS = 4
ROWS = 40
FEATS = 9
LOG2E = 1.4426950408889634
harmonic_zero = 0.28209479177387814
harmonic_one = 0.4886025119029199
harmonic_two = (
    1.0925484305920792,
    -1.0925484305920792,
    0.31539156525252005,
    -1.0925484305920792,
    0.5462742152960396,
)
harmonic_three = (
    -0.5900435899266435,
    2.890611442640554,
    -0.4570457994644658,
    0.3731763325901154,
    -0.4570457994644658,
    1.445305721320277,
    -0.5900435899266435,
)
light_term = 0.0001
contrast_term = 0.0009
F32 = jnp.float32
BF16 = jnp.bfloat16
SMEM = pl.BlockSpec(memory_space=pltpu.SMEM)
VMEM = pl.BlockSpec(memory_space=pltpu.VMEM)


def iota(shape, axis):
    return lax.broadcasted_iota(jnp.int32, shape, axis)


def dot_nt(a, b):
    return lax.dot_general(a, b, (((1,), (1,)), ((), ())), preferred_element_type=F32)


def rounded(x):
    return x.astype(BF16).astype(F32)


def pick(row, lanes):
    return jnp.take_along_axis(
        jnp.broadcast_to(row, lanes.shape), lanes, axis=1, mode="promise_in_bounds"
    )


def harmonics(along_x, along_y, along_z):
    square_x = along_x * along_x
    square_y = along_y * along_y
    square_z = along_z * along_z
    return [
        harmonic_zero + 0.0 * along_x,
        -harmonic_one * along_y,
        harmonic_one * along_z,
        -harmonic_one * along_x,
        harmonic_two[0] * along_x * along_y,
        harmonic_two[1] * along_y * along_z,
        harmonic_two[2] * (2.0 * square_z - square_x - square_y),
        harmonic_two[3] * along_x * along_z,
        harmonic_two[4] * (square_x - square_y),
        harmonic_three[0] * along_y * (3.0 * square_x - square_y),
        harmonic_three[1] * along_x * along_y * along_z,
        harmonic_three[2] * along_y * (4.0 * square_z - square_x - square_y),
        harmonic_three[3] * along_z * (2.0 * square_z - 3.0 * square_x - 3.0 * square_y),
        harmonic_three[4] * along_x * (4.0 * square_z - square_x - square_y),
        harmonic_three[5] * along_z * (square_x - square_y),
        harmonic_three[6] * along_x * (square_x - 3.0 * square_y),
    ]


def project(params, camera, focal, centre_x, centre_y):
    rotation = [[camera[3 * row + col] for col in range(3)] for row in range(3)]
    mean = [params[axis] for axis in range(3)]
    placed = [
        rotation[row][0] * mean[0]
        + rotation[row][1] * mean[1]
        + rotation[row][2] * mean[2]
        + camera[9 + row]
        for row in range(3)
    ]
    depth = placed[2]
    inverse = 1.0 / depth
    screen_x = focal * placed[0] * inverse + centre_x
    screen_y = focal * placed[1] * inverse + centre_y
    quaternion = params[6:10]
    scale = lax.rsqrt(
        quaternion[0] * quaternion[0]
        + quaternion[1] * quaternion[1]
        + quaternion[2] * quaternion[2]
        + quaternion[3] * quaternion[3]
    )
    real, imag_x, imag_y, imag_z = [part * scale for part in quaternion]
    turn = [
        [
            1.0 - 2.0 * (imag_y * imag_y + imag_z * imag_z),
            2.0 * (imag_x * imag_y - real * imag_z),
            2.0 * (imag_x * imag_z + real * imag_y),
        ],
        [
            2.0 * (imag_x * imag_y + real * imag_z),
            1.0 - 2.0 * (imag_x * imag_x + imag_z * imag_z),
            2.0 * (imag_y * imag_z - real * imag_x),
        ],
        [
            2.0 * (imag_x * imag_z - real * imag_y),
            2.0 * (imag_y * imag_z + real * imag_x),
            1.0 - 2.0 * (imag_x * imag_x + imag_y * imag_y),
        ],
    ]
    scales = [jnp.exp(part) for part in params[3:6]]
    near = focal * inverse
    slant = [-near * placed[0] * inverse, -near * placed[1] * inverse]
    facing = [
        [near * rotation[row][col] + slant[row] * rotation[2][col] for col in range(3)]
        for row in range(2)
    ]
    stretch = [
        [
            (
                facing[row][0] * turn[0][col]
                + facing[row][1] * turn[1][col]
                + facing[row][2] * turn[2][col]
            )
            * scales[col]
            for col in range(3)
        ]
        for row in range(2)
    ]
    cov_xx = (
        stretch[0][0] * stretch[0][0]
        + stretch[0][1] * stretch[0][1]
        + stretch[0][2] * stretch[0][2]
        + 0.3
    )
    cov_xy = (
        stretch[0][0] * stretch[1][0]
        + stretch[0][1] * stretch[1][1]
        + stretch[0][2] * stretch[1][2]
    )
    cov_yy = (
        stretch[1][0] * stretch[1][0]
        + stretch[1][1] * stretch[1][1]
        + stretch[1][2] * stretch[1][2]
        + 0.3
    )
    over = 1.0 / (cov_xx * cov_yy - cov_xy * cov_xy)
    shrink = 1.0 / jnp.sqrt(placed[0] * placed[0] + placed[1] * placed[1] + depth * depth)
    heading = [
        (
            rotation[0][col] * placed[0]
            + rotation[1][col] * placed[1]
            + rotation[2][col] * placed[2]
        )
        * shrink
        for col in range(3)
    ]
    basis = harmonics(heading[0], heading[1], heading[2])
    colour = []
    for channel in range(3):
        total = 0.5 + basis[0] * params[11 + channel]
        for k in range(1, 16):
            total = total + basis[k] * params[11 + 3 * k + channel]
        colour.append(total)
    return [
        screen_x,
        screen_y,
        cov_yy * over,
        -cov_xy * over,
        cov_xx * over,
        colour[0],
        colour[1],
        colour[2],
    ]


def log_sigmoid(logit):
    return jnp.minimum(logit, 0.0) - jnp.log(1.0 + jnp.exp(-jnp.abs(logit)))


def send_views(count_ref, strips):
    per_view = strips // VIEWS
    offset = per_view // 2
    runs = []
    for strip in range(strips):
        view = (strip + offset) % strips // per_view
        if not runs or runs[-1][1] != view:
            runs.append([strip, view])
    return runs


def compact_ints(chunk_ref, count_ref, out_ref, steps):
    lane = iota((1, 128), 1)

    def step(number, carry):
        start, held = carry
        live = count_ref[number]
        shift = start & 127
        row = start >> 7
        chunk = pltpu.roll(chunk_ref[pl.ds(number, 1), :], shift, axis=1)
        held = jnp.where(lane >= shift, chunk, held)
        out_ref[pl.ds(row, 1), :] = held
        held = jnp.where(shift + live >= 128, chunk, held)
        return start + live, held

    lax.fori_loop(0, steps, step, (jnp.int32(0), jnp.zeros((1, 128), jnp.int32)), unroll=4)


def compact_feats(chunk_ref, count_ref, table_ref, steps):
    lane = iota((8, 128), 1)

    def step(number, carry):
        start, held, last = carry
        live = count_ref[number]
        shift = start & 127
        row = start >> 7
        chunk = chunk_ref[number]
        first = pltpu.roll(chunk, 48, axis=1)
        second = pltpu.roll(pltpu.roll(chunk, 96, axis=1), 7, axis=0)
        ninth = jnp.where(lane < 48, first, second)
        chunk = pltpu.roll(chunk, shift, axis=1)
        ninth = pltpu.roll(ninth, shift, axis=1)
        fresh = lane >= shift
        held = jnp.where(fresh, chunk, held)
        last = jnp.where(fresh, ninth, last)
        base = pl.multiple_of(row * 16, 16)
        table_ref[pl.ds(base, 8), :] = held
        table_ref[pl.ds(base + 8, 8), :] = last
        crossed = shift + live >= 128
        held = jnp.where(crossed, chunk, held)
        last = jnp.where(crossed, ninth, last)
        return start + live, held, last

    zero = jnp.zeros((8, 128), F32)
    lax.fori_loop(0, steps, step, (jnp.int32(0), zero, zero), unroll=4)


def expand_feats(table_ref, count_ref, out_ref, steps):
    lane = iota((8, 128), 1)
    sub = iota((8, 128), 0)

    def step(number, start):
        live = count_ref[number]
        shift = start & 127
        base = pl.multiple_of((start >> 7) * 16, 16)
        back = (128 - shift) & 127
        here = lane < 128 - shift
        main = jnp.where(
            here,
            pltpu.roll(table_ref[pl.ds(base, 8), :], back, axis=1),
            pltpu.roll(table_ref[pl.ds(base + 16, 8), :], back, axis=1),
        )
        ninth = jnp.where(
            here,
            pltpu.roll(table_ref[pl.ds(base + 8, 8), :], back, axis=1),
            pltpu.roll(table_ref[pl.ds(base + 24, 8), :], back, axis=1),
        )
        tail = jnp.where(sub == 0, pltpu.roll(ninth, 80, axis=1), pltpu.roll(ninth, 32, axis=1))
        tail = jnp.where(sub < 2, tail, live.astype(F32))
        out_ref[number] = jnp.where(lane < 80, main, tail)
        return start + live

    lax.fori_loop(0, steps, step, jnp.int32(0), unroll=4)


def put_feature(table_ref, block, feature, value):
    table_ref[pl.ds(block * 128 + feature, 8, stride=16), :] = value
    if feature == 8:
        table_ref[pl.ds(block * 128 + 9, 8, stride=16), :] = value


def invert(rows_ref, out_ref):
    high = iota((ROWS, 128), 0)
    low = iota((128, 128), 0)
    lane = iota((ROWS, 128), 1).astype(F32)
    total = jnp.zeros((2 * ROWS, 128), F32)
    for pair in range(ROWS // 2):
        lefts = []
        rights = []
        for row in (2 * pair, 2 * pair + 1):
            number = rows_ref[row : row + 1, :]
            same = high == (number >> 7)
            lefts.append(
                jnp.concatenate([jnp.where(same, float(row), 0.0), jnp.where(same, lane, 0.0)], 0)
            )
            rights.append(jnp.where(low == (number & 127), 1.0, 0.0))
        total = total + dot_nt(
            jnp.concatenate(lefts, 1).astype(BF16), jnp.concatenate(rights, 1).astype(BF16)
        )
    out_ref[...] = (total[:ROWS] * 128.0 + total[ROWS:]).astype(jnp.int32)


def select_camera(camera_ref, place, run_starts):
    values = []
    for entry in range(12):
        value = jnp.full(place.shape, camera_ref[run_starts[0][1], entry], F32)
        for start, view in run_starts[1:]:
            value = jnp.where(place >= start, camera_ref[view, entry], value)
        values.append(value)
    return values


def run_bounds(count_ref, strips):
    runs = send_views(count_ref, strips)
    bounds = [(jnp.int32(0), runs[0][1])]
    for (first, _), (last, view) in zip(runs[:-1], runs[1:]):
        begin = bounds[-1][0]
        total = lax.fori_loop(
            first, last, lambda number, sum_: sum_ + count_ref[number], begin, unroll=True
        )
        bounds.append((total, view))
    return bounds


def owner_kernel(focal, centre_x, centre_y):
    def kernel(
        camera_ref, count_ref, params_ref, index_ref, out_ref, place_ref,
        wide_ref, rows_ref, feats_ref, table_ref,
    ):
        strips = index_ref.shape[0]
        wide_ref[:, 0:80] = index_ref[...]
        compact_ints(wide_ref, count_ref, rows_ref, strips)
        invert(rows_ref, place_ref)
        bounds = run_bounds(count_ref, strips)

        def project_block(block, carry):
            rows = pl.ds(block * 8, 8)
            camera = select_camera(camera_ref, place_ref[rows, :], bounds)
            params = [params_ref[number, rows, :] for number in range(59)]
            feats = project(params, camera, focal, centre_x, centre_y)
            feats.append(log_sigmoid(params[10]))
            for feature in range(FEATS):
                feats_ref[feature, rows, :] = feats[feature]
            return carry

        lax.fori_loop(0, 5, project_block, 0)

        def gather_block(block, carry):
            number = rows_ref[pl.ds(block * 8, 8), :]
            high = number >> 7
            low = number & 127
            got = [jnp.zeros((8, 128), F32)] * FEATS
            for row in range(ROWS):
                same = high == row
                for feature in range(FEATS):
                    value = pick(feats_ref[feature, row : row + 1, :], low)
                    got[feature] = jnp.where(same, value, got[feature])
            for feature in range(FEATS):
                put_feature(table_ref, block, feature, got[feature])
            return carry

        lax.fori_loop(0, 5, gather_block, 0)
        expand_feats(table_ref, count_ref, out_ref, strips)

    return kernel


def entry_basis():
    pixel = np.arange(256)
    x = pixel % 16 - 7.5
    y = pixel // 16 - 7.5
    return np.stack([np.ones(256), x, y, x * x, x * y, y * y]).astype(np.float32)


def swap_tiles(x):
    sub = iota((8, 128), 0)
    group = iota((8, 128), 1) >> 4
    for k in (1, 2, 4):
        up = pltpu.roll(pltpu.roll(x, 8 - k, axis=0), 16 * k, axis=1)
        down = pltpu.roll(pltpu.roll(x, k, axis=0), 128 - 16 * k, axis=1)
        s = (sub & k) != 0
        g = (group & k) != 0
        x = jnp.where(s == g, x, jnp.where(g, up, down))
    return x


def expand_block(lines_ref, row, basis):
    lines = lines_ref[pl.ds(pl.multiple_of(row * 24, 8), 24), :]
    columns = lines.T
    return columns, jnp.dot(columns.astype(BF16), basis, preferred_element_type=F32)


def render_kernel(
    count_ref, top_ref, chunks_ref, list_ref, across_ref, basis_ref,
    image_ref, first_ref, last_ref, lines_ref, entries_ref,
    table_ref, power_ref, column_ref,
):
    compact_feats(chunks_ref, count_ref, table_ref, chunks_ref.shape[0])
    top = top_ref[0]

    def entry_block(block, carry):
        rows = pl.ds(block * 8, 8)
        number = list_ref[rows, :]
        high = number >> 7
        low = number & 127
        got = [jnp.zeros((8, 128), F32)] * FEATS
        for row in range(ROWS):
            same = high == row
            for feature in range(FEATS):
                value = pick(table_ref[row * 16 + feature : row * 16 + feature + 1, :], low)
                got[feature] = jnp.where(same, value, got[feature])
        x = got[0] - across_ref[rows, :]
        y = got[1] - top
        a, b, c = got[2:5]
        for slot, value in enumerate((x, y, a, b, c)):
            entries_ref[slot, rows, :] = value
        terms = [
            got[8] - 0.5 * (a * x * x + c * y * y) - b * x * y,
            a * x + b * y,
            c * y + b * x,
            -0.5 * a,
            -b,
            -0.5 * c,
        ]
        for slot, term in enumerate(terms):
            term = term * LOG2E
            for part in range(3):
                piece = rounded(term)
                lines_ref[pl.ds(block * 192 + slot * 3 + part, 8, stride=24), :] = piece
                term = term - piece
        for channel in range(3):
            lines_ref[pl.ds(block * 192 + 18 + channel, 8, stride=24), :] = got[5 + channel]
            lines_ref[pl.ds(block * 192 + 21 + channel, 8, stride=24), :] = jnp.zeros((8, 128), F32)
        return carry

    lax.fori_loop(0, 5, entry_block, 0)
    basis = basis_ref[...]

    def blend(turn, carry):
        through = list(carry[0:10])
        shown = list(carry[10:40])
        for part in range(5):
            columns, power = expand_block(lines_ref, turn * 5 + part, basis)
            power_ref[part * 128 : part * 128 + 128, :] = power
            column_ref[part * 128 : part * 128 + 128, 0:24] = columns
        for entry in range(16):
            for group in range(5):
                at = (entry * 5 + group) * 8
                columns = column_ref[at : at + 8, :]
                colour = [
                    jnp.broadcast_to(columns[:, 18 + channel : 19 + channel], (8, 128))
                    for channel in range(3)
                ]
                for half in range(2):
                    slot = group * 2 + half
                    alpha = jnp.exp2(power_ref[at : at + 8, half * 128 : half * 128 + 128])
                    weight = alpha * through[slot]
                    through[slot] = through[slot] - weight
                    for channel in range(3):
                        shown[slot * 3 + channel] = (
                            shown[slot * 3 + channel] + weight * colour[channel]
                        )
        return tuple(through + shown)

    one = jnp.ones((8, 128), F32)
    zero = jnp.zeros((8, 128), F32)
    final = lax.fori_loop(0, 8, blend, (one,) * 10 + (zero,) * 30)
    for group in range(5):
        for channel in range(3):
            for half in range(2):
                image_ref[channel, group, half * 8 : half * 8 + 8, :] = swap_tiles(
                    final[10 + (group * 2 + half) * 3 + channel]
                )
            at = (channel * 5 + group) * 10
            first_ref[at : at + 10, :] = image_ref[channel, group, 0:10, :]
            last_ref[at : at + 10, :] = image_ref[channel, group, 6:16, :]


def window_weights():
    offsets = np.arange(11, dtype=np.float64) - 5.0
    raw = np.exp(-offsets * offsets / 4.5)
    return [float(value) for value in raw / raw.sum()]


WINDOW = window_weights()


def tap_sum(load):
    total = WINDOW[5] * load(5)
    for k in range(5):
        total = total + WINDOW[k] * (load(k) + load(10 - k))
    return total


def down_rows(field_ref, slot, out_ref):
    for tile in range(5):
        for channel in range(3):
            base = channel * 40
            out_ref[base : base + 32, :] = tap_sum(
                lambda k: field_ref[tile, base + k : base + k + 32, :]
            )
        yield tile, out_ref[...].T


def extend(ext_ref, own, above, below, keep_above, keep_below):
    for tile in range(5):
        for channel in range(3):
            base = channel * 40
            ext_ref[tile, base : base + 10, :] = above(channel, tile) * keep_above
            ext_ref[tile, base + 10 : base + 26, :] = own(channel, tile)
            ext_ref[tile, base + 26 : base + 36, :] = below(channel, tile) * keep_below
            ext_ref[tile, base + 36 : base + 40, :] = jnp.zeros((4, 128), F32)
        ext_ref[tile, 120:128, :] = jnp.zeros((8, 128), F32)


def clear_ends(ref, slot):
    ref[slot, 0:8, :] = jnp.zeros((8, 128), F32)
    ref[slot, 648:656, :] = jnp.zeros((8, 128), F32)


def truth_kernel(
    keep_ref, own_ref, above_ref, below_ref, ext_ref, mean_ref, power_ref,
    field_ref, rows_ref, cols_ref,
):
    lanes = lambda tile: slice(tile * 128, tile * 128 + 128)
    extend(
        ext_ref,
        lambda channel, tile: own_ref[channel, :, lanes(tile)],
        lambda channel, tile: above_ref[channel, :, lanes(tile)],
        lambda channel, tile: below_ref[channel, :, lanes(tile)],
        keep_ref[0],
        keep_ref[1],
    )
    rows_ref[...] = jnp.zeros((128, 128), F32)
    for tile in range(5):
        field_ref[tile] = ext_ref[tile] * ext_ref[tile]
    for slot, (source, out_ref) in enumerate(((ext_ref, mean_ref), (field_ref, power_ref))):
        clear_ends(cols_ref, slot)
        for tile, turned in down_rows(source, slot, rows_ref):
            cols_ref[slot, 8 + tile * 128 : 136 + tile * 128, :] = turned

        def columns(step, carry, slot=slot, out_ref=out_ref):
            base = step * 64
            out_ref[pl.ds(base, 64), :] = tap_sum(
                lambda k: cols_ref[slot, pl.ds(base + 3 + k, 64), :]
            )
            return carry

        lax.fori_loop(0, 10, columns, 0)


def invert_kernel(list_ref, out_ref):
    invert(list_ref, out_ref)


def gradient_kernel(
    count_ref, keep_ref, image_ref, above_ref, below_ref, truth_ref, mean_y_ref, power_y_ref,
    lines_ref, entries_ref, place_ref, basis_ref, moment_ref,
    out_ref,
    ext_ref, square_ref, cross_ref, rows_ref, cols_ref, parts_ref,
    alpha_ref, weight_ref, column_ref, power_ref, light_ref, split_ref,
    sums_ref, tint_ref, feats_ref, table_ref,
):
    keep_above = keep_ref[0]
    keep_below = keep_ref[1]
    extend(
        ext_ref,
        lambda channel, tile: image_ref[channel, tile],
        lambda channel, tile: above_ref[(channel * 5 + tile) * 10 : (channel * 5 + tile) * 10 + 10, :],
        lambda channel, tile: below_ref[(channel * 5 + tile) * 10 : (channel * 5 + tile) * 10 + 10, :],
        keep_above,
        keep_below,
    )
    for tile in range(5):
        square_ref[tile] = ext_ref[tile] * ext_ref[tile]
        cross_ref[tile] = ext_ref[tile] * truth_ref[tile]
    rows_ref[...] = jnp.zeros((128, 128), F32)
    for slot, source in enumerate((ext_ref, square_ref, cross_ref)):
        clear_ends(cols_ref, slot)
        clear_ends(parts_ref, slot)
        for tile, turned in down_rows(source, slot, rows_ref):
            cols_ref[slot, 8 + tile * 128 : 136 + tile * 128, :] = turned
    lane = iota((8, 128), 1)
    row = lane - jnp.where(lane >= 80, 80, jnp.where(lane >= 40, 40, 0))
    live = jnp.where(row < 5, keep_above, jnp.where(row >= 21, keep_below, 1.0))
    live = jnp.where((row < 26) & (lane < 120), live, 0.0)[0:1, :]

    def similarity(step, carry):
        base = step * 32
        mean_x, power_x, cross = [
            tap_sum(lambda k: cols_ref[slot, pl.ds(base + 3 + k, 32), :]) for slot in range(3)
        ]
        mean_y = mean_y_ref[pl.ds(base, 32), :]
        power_y = power_y_ref[pl.ds(base, 32), :]
        both = mean_x * mean_y
        squares = mean_x * mean_x + mean_y * mean_y
        light_up = 2.0 * both + light_term
        light_down = squares + light_term
        sharp_up = 2.0 * (cross - both) + contrast_term
        sharp_down = power_x + power_y - squares + contrast_term
        over = 1.0 / (light_down * sharp_down)
        score = light_up * sharp_up * over
        scale = live * over
        cross_grad = -2.0 * light_up * scale
        power_grad = score * light_down * scale
        mean_grad = (
            -2.0 * mean_y * (sharp_up - light_up) + 2.0 * mean_x * score * (sharp_down - light_down)
        ) * scale
        at = pl.ds(base + 8, 32)
        parts_ref[0, at, :] = mean_grad
        parts_ref[1, at, :] = power_grad
        parts_ref[2, at, :] = cross_grad
        return carry

    lax.fori_loop(0, 20, similarity, 0)
    for tile in range(5):
        for slot in range(3):
            turned = tap_sum(
                lambda k: parts_ref[slot, tile * 128 + 3 + k : tile * 128 + 131 + k, :]
            ).T
            (square_ref, cross_ref, cols_ref)[slot][0, 0:128, :] = turned
        for channel in range(3):
            base = channel * 40
            down = [
                tap_sum(lambda k: (square_ref, cross_ref, cols_ref)[slot][0, base + k : base + k + 16, :])
                for slot in range(3)
            ]
            own = image_ref[channel, tile]
            truth = truth_ref[tile, base + 10 : base + 26, :]
            pull = down[0] + 2.0 * own * down[1] + truth * down[2]
            for half in range(2):
                value = swap_tiles(pull[half * 8 : half * 8 + 8])
                light_ref[tile * 6 + half * 3 + channel] = value
                for part in range(3):
                    piece = rounded(value)
                    split_ref[half, pl.ds(tile * 128 + channel * 3 + part, 8, stride=16), :] = piece
                    value = value - piece
    basis = basis_ref[...]

    def forward(turn, carry):
        through = list(carry)
        for part in range(5):
            columns, power = expand_block(lines_ref, turn * 5 + part, basis)
            power_ref[part * 128 : part * 128 + 128, :] = power
            at = pl.multiple_of(turn * 640 + part * 128, 128)
            column_ref[pl.ds(at, 128), 0:24] = columns
        for entry in range(16):
            for group in range(5):
                at = (entry * 5 + group) * 8
                for half in range(2):
                    slot = group * 2 + half
                    lanes = slice(half * 128, half * 128 + 128)
                    alpha = jnp.exp2(power_ref[at : at + 8, lanes])
                    weight = alpha * through[slot]
                    through[slot] = through[slot] - weight
                    alpha_ref[half, pl.ds(turn * 640 + at, 8), :] = alpha
                    weight_ref[half, pl.ds(turn * 640 + at, 8), :] = weight
        return tuple(through)

    lax.fori_loop(0, 8, forward, (jnp.ones((8, 128), F32),) * 10)
    moments = moment_ref[...]

    def backward(count, carry):
        turn = 7 - count
        behind = list(carry)
        for entry in range(15, -1, -1):
            for group in range(5):
                at = (entry * 5 + group) * 8
                columns = column_ref[pl.ds(turn * 640 + at, 8), :]
                colour = [
                    jnp.broadcast_to(columns[:, 18 + channel : 19 + channel], (8, 128))
                    for channel in range(3)
                ]
                for half in range(2):
                    slot = group * 2 + half
                    lanes = slice(half * 128, half * 128 + 128)
                    light = group * 6 + half * 3
                    value = (
                        colour[0] * light_ref[light]
                        + colour[1] * light_ref[light + 1]
                        + colour[2] * light_ref[light + 2]
                    )
                    delta = value - behind[slot]
                    alpha = alpha_ref[half, pl.ds(turn * 640 + at, 8), :]
                    behind[slot] = behind[slot] + alpha * delta
                    power_ref[at : at + 8, lanes] = (
                        weight_ref[half, pl.ds(turn * 640 + at, 8), :] * delta
                    )
        for part in range(5):
            pull = power_ref[part * 128 : part * 128 + 128, :]
            coarse = pull.astype(BF16)
            fine = (pull - coarse.astype(F32)).astype(BF16)
            total = dot_nt(moments, coarse) + dot_nt(moments, fine)
            sums_ref[pl.ds(pl.multiple_of((turn * 5 + part) * 8, 8), 8), :] = total[0:8]
        return tuple(behind)

    lax.fori_loop(0, 8, backward, (jnp.zeros((8, 128), F32),) * 10)

    def tints(tile, carry):
        at = pl.ds(pl.multiple_of(tile * 16, 16), 16)
        total = jnp.zeros((16, 128), F32)
        for half in range(2):
            weight = weight_ref[half, pl.ds(tile, 128, stride=ROWS), :]
            coarse = weight.astype(BF16)
            fine = (weight - coarse.astype(F32)).astype(BF16)
            light = split_ref[half, at, :].astype(BF16)
            total = total + dot_nt(light, coarse) + dot_nt(light, fine)
        tint_ref[at, :] = total
        return carry

    split_rows(split_ref)
    lax.fori_loop(0, ROWS, tints, 0)

    def entry_grads(block, carry):
        rows = pl.ds(block * 8, 8)
        zeroth, by_x, by_y, by_xx, by_xy, by_yy = [
            sums_ref[pl.ds(block * 64 + slot, 8, stride=8), :] for slot in range(6)
        ]
        x, y, a, b, c = [entries_ref[slot, rows, :] for slot in range(5)]
        off_x = by_x - x * zeroth
        off_y = by_y - y * zeroth
        feats_ref[0, rows, :] = a * off_x + b * off_y
        feats_ref[1, rows, :] = c * off_y + b * off_x
        feats_ref[2, rows, :] = -0.5 * (by_xx - x * (by_x + off_x))
        feats_ref[3, rows, :] = x * by_y + y * off_x - by_xy
        feats_ref[4, rows, :] = -0.5 * (by_yy - y * (by_y + off_y))
        feats_ref[8, rows, :] = zeroth
        for channel in range(3):
            feats_ref[5 + channel, rows, :] = (
                tint_ref[pl.ds(block * 128 + channel * 3, 8, stride=16), :]
                + tint_ref[pl.ds(block * 128 + channel * 3 + 1, 8, stride=16), :]
                + tint_ref[pl.ds(block * 128 + channel * 3 + 2, 8, stride=16), :]
            )
        return carry

    lax.fori_loop(0, 5, entry_grads, 0)

    def gather_block(block, carry):
        place = place_ref[pl.ds(block * 8, 8), :]
        tile = place >> 7
        entry = place & 127
        other = entry * ROWS + tile
        high = other >> 7
        low = other & 127
        got = [jnp.zeros((8, 128), F32)] * FEATS
        for row in range(ROWS):
            same = high == row
            match = tile == row
            for feature in range(FEATS):
                line = feats_ref[feature, row : row + 1, :]
                if 5 <= feature < 8:
                    got[feature] = jnp.where(match, pick(line, entry), got[feature])
                else:
                    got[feature] = jnp.where(same, pick(line, low), got[feature])
        for feature in range(FEATS):
            put_feature(table_ref, block, feature, got[feature])
        return carry

    lax.fori_loop(0, 5, gather_block, 0)
    expand_feats(table_ref, count_ref, out_ref, out_ref.shape[0])


def split_rows(split_ref):
    for row in range(9, 16):
        for half in range(2):
            split_ref[half, pl.ds(row, ROWS, stride=16), :] = jnp.zeros((ROWS, 128), F32)


def pull_kernel(focal, centre_x, centre_y):
    def kernel(camera_ref, count_ref, params_ref, place_ref, chunks_ref, out_ref, table_ref):
        strips = chunks_ref.shape[0]
        compact_feats(chunks_ref, count_ref, table_ref, strips)
        bounds = run_bounds(count_ref, strips)

        def block_grads(block, carry):
            rows = pl.ds(block * 8, 8)
            place = place_ref[rows, :]
            high = place >> 7
            low = place & 127
            got = [jnp.zeros((8, 128), F32)] * FEATS
            for row in range(ROWS):
                same = high == row
                for feature in range(FEATS):
                    value = pick(table_ref[row * 16 + feature : row * 16 + feature + 1, :], low)
                    got[feature] = jnp.where(same, value, got[feature])
            camera = select_camera(camera_ref, place, bounds)
            params = [params_ref[number, rows, :] for number in range(59)]
            ignored, pull = jax.vjp(
                lambda values: project(values, camera, focal, centre_x, centre_y), params
            )
            for number, grad in enumerate(pull(got[:8])[0]):
                if number == 10:
                    grad = got[8] / (1.0 + jnp.exp(params[10]))
                out_ref[number, rows, :] = grad
            return carry

        lax.fori_loop(0, 5, block_grads, 0)

    return kernel


def shape(*dims, dtype=F32):
    return jax.ShapeDtypeStruct(dims, dtype)


def per_device(params, camera, send_index, send_count, tile_list, target):
    strips = lax.axis_size("strip")
    index = lax.axis_index("strip")
    per_view = strips // VIEWS
    offset = per_view // 2
    position = (index + offset) % strips
    rows_strip = target.shape[1]
    width = target.shape[2]
    focal = 0.5 * width
    centre_y = 0.5 * rows_strip * per_view
    top = ((position % per_view) * rows_strip + rows_strip // 2).astype(F32).reshape(1)
    keep = jnp.stack([position % per_view != 0, position % per_view != per_view - 1]).astype(F32)
    ahead = [(i, (i + 1) % strips) for i in range(strips)]
    behind = [((i + 1) % strips, i) for i in range(strips)]
    blocks = params.reshape(59, ROWS, 128)

    chunks, place = pl.pallas_call(
        owner_kernel(focal, 0.5 * width, centre_y),
        out_shape=(shape(strips, 8, 128), shape(ROWS, 128, dtype=jnp.int32)),
        in_specs=[SMEM, SMEM, VMEM, VMEM],
        scratch_shapes=[
            pltpu.VMEM((strips, 128), jnp.int32),
            pltpu.VMEM((ROWS + 8, 128), jnp.int32),
            pltpu.VMEM((FEATS, ROWS, 128), F32),
            pltpu.VMEM(((ROWS + 2) * 16, 128), F32),
        ],
        name="owner",
    )(camera, send_count, blocks, send_index)
    arrived = lax.all_to_all(chunks, "strip", split_axis=0, concat_axis=0, tiled=True)
    counts = arrived[:, 2, 80].astype(jnp.int32)

    truth_above = lax.ppermute(target[:, 6:16, :], "strip", ahead)
    truth_below = lax.ppermute(target[:, 0:10, :], "strip", behind)
    truth, mean_y, power_y = pl.pallas_call(
        truth_kernel,
        out_shape=(shape(5, 128, 128), shape(640, 128), shape(640, 128)),
        in_specs=[SMEM, VMEM, VMEM, VMEM],
        scratch_shapes=[
            pltpu.VMEM((5, 128, 128), F32),
            pltpu.VMEM((128, 128), F32),
            pltpu.VMEM((2, 656, 128), F32),
        ],
        name="truth",
    )(keep, target, truth_above, truth_below)
    listed = pl.pallas_call(
        invert_kernel, out_shape=shape(ROWS, 128, dtype=jnp.int32), name="listed"
    )(tile_list)

    flat_list = tile_list.T.reshape(ROWS, 128)
    across = jnp.asarray(
        (np.arange(ROWS * 128) % ROWS * 16 + 8).astype(np.float32).reshape(ROWS, 128)
    )
    rows = entry_basis()
    basis = np.zeros((24, 256), np.float32)
    basis[0:18] = np.repeat(rows, 3, axis=0)
    moment = np.zeros((16, 256), np.float32)
    moment[0:6] = rows
    basis = jnp.asarray(basis, BF16)
    moment = jnp.asarray(moment, BF16)
    image, first, last, lines, entries = pl.pallas_call(
        render_kernel,
        out_shape=(
            shape(3, 5, 16, 128),
            shape(150, 128),
            shape(150, 128),
            shape(ROWS * 24, 128),
            shape(5, ROWS, 128),
        ),
        in_specs=[SMEM, SMEM, VMEM, VMEM, VMEM, VMEM],
        scratch_shapes=[
            pltpu.VMEM(((ROWS + 2) * 16, 128), F32),
            pltpu.VMEM((640, 256), F32),
            pltpu.VMEM((640, 128), F32),
        ],
        name="render",
    )(counts, top, arrived, flat_list, across, basis)
    above = lax.ppermute(last, "strip", ahead)
    below = lax.ppermute(first, "strip", behind)
    grads = pl.pallas_call(
        gradient_kernel,
        out_shape=shape(strips, 8, 128),
        in_specs=[SMEM, SMEM] + [VMEM] * 11,
        scratch_shapes=[
            pltpu.VMEM((5, 128, 128), F32),
            pltpu.VMEM((5, 128, 128), F32),
            pltpu.VMEM((5, 128, 128), F32),
            pltpu.VMEM((128, 128), F32),
            pltpu.VMEM((3, 656, 128), F32),
            pltpu.VMEM((3, 656, 128), F32),
            pltpu.VMEM((2, 5120, 128), F32),
            pltpu.VMEM((2, 5120, 128), F32),
            pltpu.VMEM((5120, 128), F32),
            pltpu.VMEM((640, 256), F32),
            pltpu.VMEM((30, 8, 128), F32),
            pltpu.VMEM((2, ROWS * 16, 128), F32),
            pltpu.VMEM((ROWS * 8, 128), F32),
            pltpu.VMEM((ROWS * 16, 128), F32),
            pltpu.VMEM((FEATS, ROWS, 128), F32),
            pltpu.VMEM(((ROWS + 2) * 16, 128), F32),
        ],
        name="gradient",
    )(
        counts, keep, image, above, below, truth, mean_y, power_y,
        lines, entries, listed, basis, moment,
    )
    returned = lax.all_to_all(grads, "strip", split_axis=0, concat_axis=0, tiled=True)
    result = pl.pallas_call(
        pull_kernel(focal, 0.5 * width, centre_y),
        out_shape=shape(59, ROWS, 128),
        in_specs=[SMEM, SMEM, VMEM, VMEM, VMEM],
        scratch_shapes=[pltpu.VMEM(((ROWS + 2) * 16, 128), F32)],
        name="pull",
    )(camera, send_count, blocks, place, returned)
    return result.reshape(59, ROWS * 128)


def solution(mesh):
    return jax.shard_map(
        per_device,
        mesh=mesh,
        in_specs=(
            P(None, "strip"),
            P(),
            P("strip", None),
            P("strip"),
            P("strip", None),
            P(None, "strip", None),
        ),
        out_specs=P(None, "strip"),
        check_vma=False,
    )
```

```python
import numpy as np

import jax
import jax.numpy as jnp
from jax import lax
from jax.experimental import pallas as pl
from jax.experimental.pallas import tpu as pltpu
from jax.sharding import PartitionSpec as P

VIEWS = 4
ROWS = 40
FEATS = 9
LOG2E = 1.4426950408889634
harmonic_zero = 0.28209479177387814
harmonic_one = 0.4886025119029199
harmonic_two = (
    1.0925484305920792,
    -1.0925484305920792,
    0.31539156525252005,
    -1.0925484305920792,
    0.5462742152960396,
)
harmonic_three = (
    -0.5900435899266435,
    2.890611442640554,
    -0.4570457994644658,
    0.3731763325901154,
    -0.4570457994644658,
    1.445305721320277,
    -0.5900435899266435,
)
light_term = 0.0001
contrast_term = 0.0009
F32 = jnp.float32
BF16 = jnp.bfloat16
SMEM = pl.BlockSpec(memory_space=pltpu.SMEM)
VMEM = pl.BlockSpec(memory_space=pltpu.VMEM)
ANY = pl.BlockSpec(memory_space=pl.ANY)


def iota(shape, axis):
    return lax.broadcasted_iota(jnp.int32, shape, axis)


def dot_nt(a, b):
    return lax.dot_general(a, b, (((1,), (1,)), ((), ())), preferred_element_type=F32)


def rounded(x):
    return x.astype(BF16).astype(F32)


def pick(row, lanes):
    return jnp.take_along_axis(
        jnp.broadcast_to(row, lanes.shape), lanes, axis=1, mode="promise_in_bounds"
    )


def harmonics(along_x, along_y, along_z):
    square_x = along_x * along_x
    square_y = along_y * along_y
    square_z = along_z * along_z
    return [
        harmonic_zero + 0.0 * along_x,
        -harmonic_one * along_y,
        harmonic_one * along_z,
        -harmonic_one * along_x,
        harmonic_two[0] * along_x * along_y,
        harmonic_two[1] * along_y * along_z,
        harmonic_two[2] * (2.0 * square_z - square_x - square_y),
        harmonic_two[3] * along_x * along_z,
        harmonic_two[4] * (square_x - square_y),
        harmonic_three[0] * along_y * (3.0 * square_x - square_y),
        harmonic_three[1] * along_x * along_y * along_z,
        harmonic_three[2] * along_y * (4.0 * square_z - square_x - square_y),
        harmonic_three[3] * along_z * (2.0 * square_z - 3.0 * square_x - 3.0 * square_y),
        harmonic_three[4] * along_x * (4.0 * square_z - square_x - square_y),
        harmonic_three[5] * along_z * (square_x - square_y),
        harmonic_three[6] * along_x * (square_x - 3.0 * square_y),
    ]


def project(params, camera, focal, centre_x, centre_y):
    rotation = [[camera[3 * row + col] for col in range(3)] for row in range(3)]
    mean = [params[axis] for axis in range(3)]
    placed = [
        rotation[row][0] * mean[0]
        + rotation[row][1] * mean[1]
        + rotation[row][2] * mean[2]
        + camera[9 + row]
        for row in range(3)
    ]
    depth = placed[2]
    inverse = 1.0 / depth
    screen_x = focal * placed[0] * inverse + centre_x
    screen_y = focal * placed[1] * inverse + centre_y
    quaternion = params[6:10]
    scale = lax.rsqrt(
        quaternion[0] * quaternion[0]
        + quaternion[1] * quaternion[1]
        + quaternion[2] * quaternion[2]
        + quaternion[3] * quaternion[3]
    )
    real, imag_x, imag_y, imag_z = [part * scale for part in quaternion]
    turn = [
        [
            1.0 - 2.0 * (imag_y * imag_y + imag_z * imag_z),
            2.0 * (imag_x * imag_y - real * imag_z),
            2.0 * (imag_x * imag_z + real * imag_y),
        ],
        [
            2.0 * (imag_x * imag_y + real * imag_z),
            1.0 - 2.0 * (imag_x * imag_x + imag_z * imag_z),
            2.0 * (imag_y * imag_z - real * imag_x),
        ],
        [
            2.0 * (imag_x * imag_z - real * imag_y),
            2.0 * (imag_y * imag_z + real * imag_x),
            1.0 - 2.0 * (imag_x * imag_x + imag_y * imag_y),
        ],
    ]
    scales = [jnp.exp(part) for part in params[3:6]]
    near = focal * inverse
    slant = [-near * placed[0] * inverse, -near * placed[1] * inverse]
    facing = [
        [near * rotation[row][col] + slant[row] * rotation[2][col] for col in range(3)]
        for row in range(2)
    ]
    stretch = [
        [
            (
                facing[row][0] * turn[0][col]
                + facing[row][1] * turn[1][col]
                + facing[row][2] * turn[2][col]
            )
            * scales[col]
            for col in range(3)
        ]
        for row in range(2)
    ]
    cov_xx = (
        stretch[0][0] * stretch[0][0]
        + stretch[0][1] * stretch[0][1]
        + stretch[0][2] * stretch[0][2]
        + 0.3
    )
    cov_xy = (
        stretch[0][0] * stretch[1][0]
        + stretch[0][1] * stretch[1][1]
        + stretch[0][2] * stretch[1][2]
    )
    cov_yy = (
        stretch[1][0] * stretch[1][0]
        + stretch[1][1] * stretch[1][1]
        + stretch[1][2] * stretch[1][2]
        + 0.3
    )
    over = 1.0 / (cov_xx * cov_yy - cov_xy * cov_xy)
    shrink = 1.0 / jnp.sqrt(placed[0] * placed[0] + placed[1] * placed[1] + depth * depth)
    heading = [
        (
            rotation[0][col] * placed[0]
            + rotation[1][col] * placed[1]
            + rotation[2][col] * placed[2]
        )
        * shrink
        for col in range(3)
    ]
    basis = harmonics(heading[0], heading[1], heading[2])
    colour = []
    for channel in range(3):
        total = 0.5 + basis[0] * params[11 + channel]
        for k in range(1, 16):
            total = total + basis[k] * params[11 + 3 * k + channel]
        colour.append(total)
    return [
        screen_x,
        screen_y,
        cov_yy * over,
        -cov_xy * over,
        cov_xx * over,
        colour[0],
        colour[1],
        colour[2],
    ]


def log_sigmoid(logit):
    return jnp.minimum(logit, 0.0) - jnp.log(1.0 + jnp.exp(-jnp.abs(logit)))


def send_views(count_ref, strips):
    per_view = strips // VIEWS
    offset = per_view // 2
    runs = []
    for strip in range(strips):
        view = (strip + offset) % strips // per_view
        if not runs or runs[-1][1] != view:
            runs.append([strip, view])
    return runs


def compact_ints(chunk_ref, count_ref, out_ref, steps):
    lane = iota((1, 128), 1)

    def step(number, carry):
        start, held = carry
        live = count_ref[number]
        shift = start & 127
        row = start >> 7
        chunk = pltpu.roll(chunk_ref[pl.ds(number, 1), :], shift, axis=1)
        held = jnp.where(lane >= shift, chunk, held)
        out_ref[pl.ds(row, 1), :] = held
        held = jnp.where(shift + live >= 128, chunk, held)
        return start + live, held

    lax.fori_loop(0, steps, step, (jnp.int32(0), jnp.zeros((1, 128), jnp.int32)), unroll=16)


def compact_feats(chunk_ref, count_of, table_ref, steps):
    lane = iota((8, 128), 1)

    def step(number, carry):
        start, held, last = carry
        if isinstance(number, int) and number == steps - 1:
            chunk = pltpu.roll(chunk_ref[number * 6 - 2 : number * 6 + 6, :], 6, axis=0)
        else:
            chunk = chunk_ref[pl.ds(number * 6, 8), :]
        live = count_of(number, chunk)
        shift = start & 127
        row = start >> 7
        first = pltpu.roll(chunk, 48, axis=1)
        second = pltpu.roll(pltpu.roll(chunk, 96, axis=1), 7, axis=0)
        rest = jnp.where(lane < 48, first, second)
        chunk = pltpu.roll(chunk, shift, axis=1)
        rest = pltpu.roll(rest, shift, axis=1)
        fresh = lane >= shift
        held = jnp.where(fresh, chunk, held)
        last = jnp.where(fresh, rest, last)
        base = pl.multiple_of(row * 16, 16)
        table_ref[pl.ds(base, 8), :] = held
        table_ref[pl.ds(base + 8, 8), :] = last
        crossed = shift + live >= 128
        held = jnp.where(crossed, chunk, held)
        last = jnp.where(crossed, rest, last)
        return start + live, held, last

    zero = jnp.zeros((8, 128), F32)
    carry = lax.fori_loop(0, steps - 16, step, (jnp.int32(0), zero, zero), unroll=16)
    for number in range(steps - 16, steps):
        carry = step(number, carry)


def expand_feats(table_ref, count_ref, out_ref, steps):
    lane = iota((8, 128), 1)
    sub = iota((8, 128), 0)

    def step(number, start):
        live = count_ref[number]
        shift = start & 127
        base = pl.multiple_of((start >> 7) * 16, 16)
        back = (128 - shift) & 127
        here = lane < 128 - shift
        main = jnp.where(
            here,
            pltpu.roll(table_ref[pl.ds(base, 8), :], back, axis=1),
            pltpu.roll(table_ref[pl.ds(base + 16, 8), :], back, axis=1),
        )
        rest = jnp.where(
            here,
            pltpu.roll(table_ref[pl.ds(base + 8, 8), :], back, axis=1),
            pltpu.roll(table_ref[pl.ds(base + 24, 8), :], back, axis=1),
        )
        tail = jnp.where(
            (sub & 1) == 0, pltpu.roll(rest, 80, axis=1), pltpu.roll(rest, 32, axis=1)
        )
        tail = jnp.where((sub == 1) & (lane == 127), live.astype(F32), tail)
        out_ref[pl.ds(number * 6, 6), :] = jnp.where(lane < 80, main, tail)[0:6]
        return start + live

    lax.fori_loop(0, steps, step, jnp.int32(0), unroll=16)


def line_of(feature):
    return feature if feature < 6 else 8 + 2 * (feature - 6)


def put_feature(table_ref, block, feature, value):
    line = line_of(feature)
    table_ref[pl.ds(block * 128 + line, 8, stride=16), :] = value
    if feature >= 6:
        table_ref[pl.ds(block * 128 + line + 1, 8, stride=16), :] = value


def table_line(table_ref, row, feature):
    line = row * 16 + line_of(feature)
    return table_ref[line : line + 1, :]


def fetch_params(params_ref, local_ref, sems):
    copies = [
        pltpu.make_async_copy(
            params_ref.at[:, pl.ds(tile * 128, 128)],
            local_ref.at[pl.ds(tile * 64, 59), :],
            sems.at[tile],
        )
        for tile in range(ROWS)
    ]
    for copy in copies:
        copy.start()
    return copies


def invert(rows_ref, out_ref):
    high = iota((ROWS, 128), 0)
    low = iota((128, 128), 0)
    lane = iota((ROWS, 128), 1).astype(F32)
    total = jnp.zeros((2 * ROWS, 128), F32)
    for pair in range(ROWS // 2):
        lefts = []
        rights = []
        for row in (2 * pair, 2 * pair + 1):
            number = rows_ref[row : row + 1, :]
            same = high == (number >> 7)
            lefts.append(
                jnp.concatenate([jnp.where(same, float(row), 0.0), jnp.where(same, lane, 0.0)], 0)
            )
            rights.append(jnp.where(low == (number & 127), 1.0, 0.0))
        total = total + dot_nt(
            jnp.concatenate(lefts, 1).astype(BF16), jnp.concatenate(rights, 1).astype(BF16)
        )
    out_ref[...] = (total[:ROWS] * 128.0 + total[ROWS:]).astype(jnp.int32)


def select_camera(camera_ref, place, run_starts):
    values = []
    for entry in range(12):
        value = jnp.full(place.shape, camera_ref[run_starts[0][1], entry], F32)
        for start, view in run_starts[1:]:
            value = jnp.where(place >= start, camera_ref[view, entry], value)
        values.append(value)
    return values


def run_bounds(count_ref, strips):
    runs = send_views(count_ref, strips)
    bounds = [(jnp.int32(0), runs[0][1])]
    for (first, _), (last, view) in zip(runs[:-1], runs[1:]):
        begin = bounds[-1][0]
        total = lax.fori_loop(
            first, last, lambda number, sum_: sum_ + count_ref[number], begin, unroll=True
        )
        bounds.append((total, view))
    return bounds


def owner_kernel(focal, centre_x, centre_y):
    def kernel(
        camera_ref, count_ref, params_ref, index_ref, out_ref, place_ref,
        wide_ref, rows_ref, feats_ref, table_ref, local_ref, sems,
    ):
        copies = fetch_params(params_ref, local_ref, sems)
        strips = index_ref.shape[1]
        wide_ref[...] = jnp.concatenate(
            [index_ref[...], jnp.zeros((128 - index_ref.shape[0], strips), jnp.int32)], 0
        ).T
        compact_ints(wide_ref, count_ref, rows_ref, strips)
        invert(rows_ref, place_ref)
        bounds = run_bounds(count_ref, strips)
        for copy in copies:
            copy.wait()

        def project_block(block, carry):
            rows = pl.ds(block * 8, 8)
            camera = select_camera(camera_ref, place_ref[rows, :], bounds)
            params = [
                local_ref[pl.ds(block * 512 + number, 8, stride=64), :] for number in range(59)
            ]
            feats = project(params, camera, focal, centre_x, centre_y)
            feats.append(log_sigmoid(params[10]))
            for feature in range(FEATS):
                feats_ref[feature, rows, :] = feats[feature]
            return carry

        lax.fori_loop(0, 5, project_block, 0)

        def gather_block(block, carry):
            number = rows_ref[pl.ds(block * 8, 8), :]
            high = number >> 7
            low = number & 127
            got = [jnp.zeros((8, 128), F32)] * FEATS
            for row in range(ROWS):
                same = high == row
                for feature in range(FEATS):
                    value = pick(feats_ref[feature, row : row + 1, :], low)
                    got[feature] = jnp.where(same, value, got[feature])
            for feature in range(FEATS):
                put_feature(table_ref, block, feature, got[feature])
            return carry

        lax.fori_loop(0, 5, gather_block, 0)
        expand_feats(table_ref, count_ref, out_ref, strips)

    return kernel


def entry_basis():
    pixel = np.arange(256)
    x = pixel % 16 - 7.5
    y = pixel // 16 - 7.5
    return np.stack([np.ones(256), x, y, x * x, x * y, y * y]).astype(np.float32)


def swap_tiles(x):
    sub = iota((8, 128), 0)
    group = iota((8, 128), 1) >> 4
    for k in (1, 2, 4):
        up = pltpu.roll(pltpu.roll(x, 8 - k, axis=0), 16 * k, axis=1)
        down = pltpu.roll(pltpu.roll(x, k, axis=0), 128 - 16 * k, axis=1)
        s = (sub & k) != 0
        g = (group & k) != 0
        x = jnp.where(s == g, x, jnp.where(g, up, down))
    return x


def coarse_fine(x):
    coarse = x.astype(BF16)
    return coarse, (x - coarse.astype(F32)).astype(BF16)


def render_kernel(
    top_ref, chunks_ref, list_ref, tiles_ref, across_ref, basis_ref,
    image_ref, first_ref, last_ref, entries_ref, colour_ref, count_ref, alphas_ref, weights_ref,
    table_ref, lines_ref, power_a, power_b, alpha_ref, weight_ref, tint_ref, shown_ref, sems,
):
    strips = chunks_ref.shape[0] // 6

    def count_of(number, chunk):
        live = chunk[1, 127].astype(jnp.int32)
        count_ref[number] = live
        return live

    compact_feats(chunks_ref, count_of, table_ref, strips)
    top = top_ref[0]

    def entry_block(block, carry):
        rows = pl.ds(block * 8, 8)
        number = list_ref[rows, :]
        high = number >> 7
        low = number & 127
        other = tiles_ref[rows, :]
        other_high = other >> 7
        other_low = other & 127
        got = [jnp.zeros((8, 128), F32)] * FEATS
        for row in range(ROWS):
            same = high == row
            match = other_high == row
            for feature in range(FEATS):
                line = table_line(table_ref, row, feature)
                if 5 <= feature < 8:
                    got[feature] = jnp.where(match, pick(line, other_low), got[feature])
                else:
                    got[feature] = jnp.where(same, pick(line, low), got[feature])
        x = got[0] - across_ref[rows, :]
        y = got[1] - top
        a, b, c = got[2:5]
        for slot, value in enumerate((x, y, a, b, c)):
            entries_ref[slot, rows, :] = value
        terms = [
            got[8] - 0.5 * (a * x * x + c * y * y) - b * x * y,
            a * x + b * y,
            c * y + b * x,
            -0.5 * a,
            -b,
            -0.5 * c,
        ]
        for slot, term in enumerate(terms):
            term = term * LOG2E
            for part in range(3):
                piece = rounded(term)
                lines_ref[pl.ds(block * 192 + slot * 3 + part, 8, stride=24), :] = piece
                term = term - piece
        for slot in range(18, 24):
            lines_ref[pl.ds(block * 192 + slot, 8, stride=24), :] = jnp.zeros((8, 128), F32)
        for channel in range(3):
            value = got[5 + channel]
            colour_ref[channel, rows, :] = value
            for part in range(3):
                piece = rounded(value)
                tint_ref[pl.ds(block * 128 + channel * 3 + part, 8, stride=16), :] = piece
                value = value - piece
        return carry

    lax.fori_loop(0, 5, entry_block, 0)
    basis = basis_ref[...]

    def powers(turn, power_ref):
        for part in range(5):
            lines = lines_ref[pl.ds(pl.multiple_of((turn * 5 + part) * 24, 8), 24), :]
            power_ref[part * 128 : part * 128 + 128, :] = jnp.dot(
                lines.T.astype(BF16), basis, preferred_element_type=F32
            )

    def copies(turn):
        rows = pl.ds(turn * 640, 640)
        found = []
        for half in range(2):
            for slot, (near, far) in enumerate(((alpha_ref, alphas_ref), (weight_ref, weights_ref))):
                found.append(
                    pltpu.make_async_copy(
                        near.at[half, rows, :],
                        far.at[half, rows, :],
                        sems.at[turn * 4 + slot * 2 + half],
                    )
                )
        return found

    def scan(turn, power_ref, through):
        through = list(through)
        for entry in range(16):
            for group in range(5):
                at = (entry * 5 + group) * 8
                for half in range(2):
                    slot = group * 2 + half
                    alpha = jnp.exp2(power_ref[at : at + 8, half * 128 : half * 128 + 128])
                    weight = alpha * through[slot]
                    through[slot] = through[slot] - weight
                    alpha_ref[half, pl.ds(turn * 640 + at, 8), :] = alpha
                    weight_ref[half, pl.ds(turn * 640 + at, 8), :] = weight
        return tuple(through)

    def blend(pair, through):
        powers(2 * pair + 1, power_b)
        through = scan(2 * pair, power_a, through)
        powers(jnp.minimum(2 * pair + 2, 7), power_a)
        through = scan(2 * pair + 1, power_b, through)
        for turn in (2 * pair, 2 * pair + 1):
            for copy in copies(turn):
                copy.start()
        return through

    powers(0, power_a)
    lax.fori_loop(0, 4, blend, (jnp.ones((8, 128), F32),) * 10)

    def tints(tile, carry):
        tint = tint_ref[pl.ds(pl.multiple_of(tile * 16, 16), 16), :].astype(BF16)
        for half in range(2):
            coarse, fine = coarse_fine(weight_ref[half, pl.ds(tile, 128, stride=ROWS), :])
            total = jnp.dot(tint, coarse, preferred_element_type=F32) + jnp.dot(
                tint, fine, preferred_element_type=F32
            )
            shown_ref[half, pl.ds(pl.multiple_of(tile * 16, 16), 16), :] = total
        return carry

    lax.fori_loop(0, ROWS, tints, 0, unroll=4)
    for group in range(5):
        for channel in range(3):
            for half in range(2):
                parts = [
                    shown_ref[half, pl.ds(group * 128 + channel * 3 + part, 8, stride=16), :]
                    for part in range(3)
                ]
                image_ref[channel, group, half * 8 : half * 8 + 8, :] = swap_tiles(
                    parts[0] + parts[1] + parts[2]
                )
            at = (channel * 5 + group) * 10
            first_ref[at : at + 10, :] = image_ref[channel, group, 0:10, :]
            last_ref[at : at + 10, :] = image_ref[channel, group, 6:16, :]
    for turn in range(8):
        for copy in copies(turn):
            copy.wait()


def window_weights():
    offsets = np.arange(11, dtype=np.float64) - 5.0
    raw = np.exp(-offsets * offsets / 4.5)
    return [float(value) for value in raw / raw.sum()]


WINDOW = window_weights()


def tap_sum(load):
    total = WINDOW[5] * load(5)
    for k in range(5):
        total = total + WINDOW[k] * (load(k) + load(10 - k))
    return total


def down_rows(field_ref, slot, out_ref):
    for tile in range(5):
        for channel in range(3):
            base = channel * 40
            out_ref[base : base + 32, :] = tap_sum(
                lambda k: field_ref[tile, base + k : base + k + 32, :]
            )
        yield tile, out_ref[...].T


def extend(ext_ref, own, above, below, keep_above, keep_below):
    for tile in range(5):
        for channel in range(3):
            base = channel * 40
            ext_ref[tile, base : base + 10, :] = above(channel, tile) * keep_above
            ext_ref[tile, base + 10 : base + 26, :] = own(channel, tile)
            ext_ref[tile, base + 26 : base + 36, :] = below(channel, tile) * keep_below
            ext_ref[tile, base + 36 : base + 40, :] = jnp.zeros((4, 128), F32)
        ext_ref[tile, 120:128, :] = jnp.zeros((8, 128), F32)


def clear_ends(ref, slot):
    ref[slot, 0:8, :] = jnp.zeros((8, 128), F32)
    ref[slot, 648:656, :] = jnp.zeros((8, 128), F32)


def truth_kernel(
    keep_ref, own_ref, above_ref, below_ref, ext_ref, mean_ref, power_ref,
    field_ref, rows_ref, cols_ref,
):
    lanes = lambda tile: slice(tile * 128, tile * 128 + 128)
    extend(
        ext_ref,
        lambda channel, tile: own_ref[channel, :, lanes(tile)],
        lambda channel, tile: above_ref[channel, :, lanes(tile)],
        lambda channel, tile: below_ref[channel, :, lanes(tile)],
        keep_ref[0],
        keep_ref[1],
    )
    rows_ref[...] = jnp.zeros((128, 128), F32)
    for tile in range(5):
        field_ref[tile] = ext_ref[tile] * ext_ref[tile]
    for slot, (source, out_ref) in enumerate(((ext_ref, mean_ref), (field_ref, power_ref))):
        clear_ends(cols_ref, slot)
        for tile, turned in down_rows(source, slot, rows_ref):
            cols_ref[slot, 8 + tile * 128 : 136 + tile * 128, :] = turned

        def columns(step, carry, slot=slot, out_ref=out_ref):
            base = step * 64
            out_ref[pl.ds(base, 64), :] = tap_sum(
                lambda k: cols_ref[slot, pl.ds(base + 3 + k, 64), :]
            )
            return carry

        lax.fori_loop(0, 10, columns, 0)


def invert_kernel(list_ref, out_ref):
    invert(list_ref, out_ref)


def gradient_kernel(
    count_ref, keep_ref, image_ref, above_ref, below_ref, truth_ref, mean_y_ref, power_y_ref,
    entries_ref, colour_ref, place_ref, moment_ref, alphas_ref, weights_ref,
    out_ref,
    ext_ref, square_ref, cross_ref, rows_ref, cols_ref, parts_ref,
    alpha_ref, weight_ref, pull_a, pull_b, light_ref, split_ref,
    sums_ref, tint_ref, feats_ref, table_ref, sems,
):
    copies = [
        pltpu.make_async_copy(far.at[half], near.at[half], sems.at[slot * 2 + half])
        for slot, (far, near) in enumerate(((alphas_ref, alpha_ref), (weights_ref, weight_ref)))
        for half in range(2)
    ]
    for copy in copies:
        copy.start()
    keep_above = keep_ref[0]
    keep_below = keep_ref[1]
    extend(
        ext_ref,
        lambda channel, tile: image_ref[channel, tile],
        lambda channel, tile: above_ref[(channel * 5 + tile) * 10 : (channel * 5 + tile) * 10 + 10, :],
        lambda channel, tile: below_ref[(channel * 5 + tile) * 10 : (channel * 5 + tile) * 10 + 10, :],
        keep_above,
        keep_below,
    )
    for tile in range(5):
        square_ref[tile] = ext_ref[tile] * ext_ref[tile]
        cross_ref[tile] = ext_ref[tile] * truth_ref[tile]
    rows_ref[...] = jnp.zeros((128, 128), F32)
    for slot, source in enumerate((ext_ref, square_ref, cross_ref)):
        clear_ends(cols_ref, slot)
        clear_ends(parts_ref, slot)
        for tile, turned in down_rows(source, slot, rows_ref):
            cols_ref[slot, 8 + tile * 128 : 136 + tile * 128, :] = turned
    lane = iota((8, 128), 1)
    row = lane - jnp.where(lane >= 80, 80, jnp.where(lane >= 40, 40, 0))
    live = jnp.where(row < 5, keep_above, jnp.where(row >= 21, keep_below, 1.0))
    live = jnp.where((row < 26) & (lane < 120), live, 0.0)[0:1, :]

    def similarity(step, carry):
        base = step * 32
        mean_x, power_x, cross = [
            tap_sum(lambda k: cols_ref[slot, pl.ds(base + 3 + k, 32), :]) for slot in range(3)
        ]
        mean_y = mean_y_ref[pl.ds(base, 32), :]
        power_y = power_y_ref[pl.ds(base, 32), :]
        both = mean_x * mean_y
        squares = mean_x * mean_x + mean_y * mean_y
        light_up = 2.0 * both + light_term
        light_down = squares + light_term
        sharp_up = 2.0 * (cross - both) + contrast_term
        sharp_down = power_x + power_y - squares + contrast_term
        over = 1.0 / (light_down * sharp_down)
        score = light_up * sharp_up * over
        scale = live * over
        cross_grad = -2.0 * light_up * scale
        power_grad = score * light_down * scale
        mean_grad = (
            -2.0 * mean_y * (sharp_up - light_up) + 2.0 * mean_x * score * (sharp_down - light_down)
        ) * scale
        at = pl.ds(base + 8, 32)
        parts_ref[0, at, :] = mean_grad
        parts_ref[1, at, :] = power_grad
        parts_ref[2, at, :] = cross_grad
        return carry

    lax.fori_loop(0, 20, similarity, 0)
    for tile in range(5):
        for slot in range(3):
            turned = tap_sum(
                lambda k: parts_ref[slot, tile * 128 + 3 + k : tile * 128 + 131 + k, :]
            ).T
            (square_ref, cross_ref, cols_ref)[slot][0, 0:128, :] = turned
        for channel in range(3):
            base = channel * 40
            down = [
                tap_sum(lambda k: (square_ref, cross_ref, cols_ref)[slot][0, base + k : base + k + 16, :])
                for slot in range(3)
            ]
            own = image_ref[channel, tile]
            truth = truth_ref[tile, base + 10 : base + 26, :]
            pull = down[0] + 2.0 * own * down[1] + truth * down[2]
            for half in range(2):
                value = swap_tiles(pull[half * 8 : half * 8 + 8])
                light_ref[tile * 6 + half * 3 + channel] = value
                for part in range(3):
                    piece = rounded(value)
                    split_ref[half, pl.ds(tile * 128 + channel * 3 + part, 8, stride=16), :] = piece
                    value = value - piece
    for copy in copies:
        copy.wait()
    moments = moment_ref[...]

    def scan(turn, pull_ref, behind):
        behind = list(behind)
        turned = [
            [
                pltpu.roll(
                    colour_ref[channel, group * 8 : group * 8 + 8, :], 128 - turn * 16 & 127, axis=1
                )
                for channel in range(3)
            ]
            for group in range(5)
        ]
        for entry in range(15, -1, -1):
            for group in range(5):
                at = (entry * 5 + group) * 8
                rows = pl.ds(turn * 640 + at, 8)
                colour = [
                    jnp.broadcast_to(turned[group][channel][:, entry : entry + 1], (8, 128))
                    for channel in range(3)
                ]
                for half in range(2):
                    slot = group * 2 + half
                    light = group * 6 + half * 3
                    value = (
                        colour[0] * light_ref[light]
                        + colour[1] * light_ref[light + 1]
                        + colour[2] * light_ref[light + 2]
                    )
                    delta = value - behind[slot]
                    behind[slot] = behind[slot] + alpha_ref[half, rows, :] * delta
                    pull_ref[at : at + 8, half * 128 : half * 128 + 128] = (
                        weight_ref[half, rows, :] * delta
                    )
        return tuple(behind)

    def reduce(turn, pull_ref):
        for part in range(5):
            coarse, fine = coarse_fine(pull_ref[part * 128 : part * 128 + 128, :])
            total = dot_nt(moments, coarse) + dot_nt(moments, fine)
            sums_ref[pl.ds(pl.multiple_of((turn * 5 + part) * 8, 8), 8), :] = total[0:8]

    def backward(count, behind):
        turn = 7 - 2 * count
        reduce(turn + 1, pull_b)
        behind = scan(turn, pull_a, behind)
        reduce(turn, pull_a)
        return scan(turn - 1, pull_b, behind)

    pull_b[...] = jnp.zeros((640, 256), F32)
    lax.fori_loop(0, 4, backward, (jnp.zeros((8, 128), F32),) * 10)
    reduce(0, pull_b)

    def tints(tile, carry):
        at = pl.ds(pl.multiple_of(tile * 16, 16), 16)
        total = jnp.zeros((16, 128), F32)
        for half in range(2):
            coarse, fine = coarse_fine(weight_ref[half, pl.ds(tile, 128, stride=ROWS), :])
            light = split_ref[half, at, :].astype(BF16)
            total = total + dot_nt(light, coarse) + dot_nt(light, fine)
        tint_ref[at, :] = total
        return carry

    lax.fori_loop(0, ROWS, tints, 0, unroll=4)

    def entry_grads(block, carry):
        rows = pl.ds(block * 8, 8)
        zeroth, by_x, by_y, by_xx, by_xy, by_yy = [
            sums_ref[pl.ds(block * 64 + slot, 8, stride=8), :] for slot in range(6)
        ]
        x, y, a, b, c = [entries_ref[slot, rows, :] for slot in range(5)]
        off_x = by_x - x * zeroth
        off_y = by_y - y * zeroth
        feats_ref[0, rows, :] = a * off_x + b * off_y
        feats_ref[1, rows, :] = c * off_y + b * off_x
        feats_ref[2, rows, :] = -0.5 * (by_xx - x * (by_x + off_x))
        feats_ref[3, rows, :] = x * by_y + y * off_x - by_xy
        feats_ref[4, rows, :] = -0.5 * (by_yy - y * (by_y + off_y))
        feats_ref[8, rows, :] = zeroth
        for channel in range(3):
            feats_ref[5 + channel, rows, :] = (
                tint_ref[pl.ds(block * 128 + channel * 3, 8, stride=16), :]
                + tint_ref[pl.ds(block * 128 + channel * 3 + 1, 8, stride=16), :]
                + tint_ref[pl.ds(block * 128 + channel * 3 + 2, 8, stride=16), :]
            )
        return carry

    lax.fori_loop(0, 5, entry_grads, 0)

    def gather_block(block, carry):
        place = place_ref[pl.ds(block * 8, 8), :]
        tile = place >> 7
        entry = place & 127
        other = entry * ROWS + tile
        high = other >> 7
        low = other & 127
        got = [jnp.zeros((8, 128), F32)] * FEATS
        for row in range(ROWS):
            same = high == row
            match = tile == row
            for feature in range(FEATS):
                line = feats_ref[feature, row : row + 1, :]
                if 5 <= feature < 8:
                    got[feature] = jnp.where(match, pick(line, entry), got[feature])
                else:
                    got[feature] = jnp.where(same, pick(line, low), got[feature])
        for feature in range(FEATS):
            put_feature(table_ref, block, feature, got[feature])
        return carry

    lax.fori_loop(0, 5, gather_block, 0)
    expand_feats(table_ref, count_ref, out_ref, out_ref.shape[0] // 6)


def pull_kernel(focal, centre_x, centre_y):
    def kernel(
        camera_ref, count_ref, params_ref, place_ref, chunks_ref, out_ref,
        table_ref, local_ref, grads_ref, sems, out_sems,
    ):
        copies = fetch_params(params_ref, local_ref, sems)
        strips = chunks_ref.shape[0] // 6
        compact_feats(chunks_ref, lambda number, chunk: count_ref[number], table_ref, strips)
        bounds = run_bounds(count_ref, strips)

        def block_grads(block, carry):
            rows = pl.ds(block * 8, 8)
            place = place_ref[rows, :]
            high = place >> 7
            low = place & 127
            got = [jnp.zeros((8, 128), F32)] * FEATS
            for row in range(ROWS):
                same = high == row
                for feature in range(FEATS):
                    value = pick(table_line(table_ref, row, feature), low)
                    got[feature] = jnp.where(same, value, got[feature])
            camera = select_camera(camera_ref, place, bounds)
            params = [
                local_ref[pl.ds(block * 512 + number, 8, stride=64), :] for number in range(59)
            ]
            ignored, pull = jax.vjp(
                lambda values: project(values, camera, focal, centre_x, centre_y), params
            )
            for number, grad in enumerate(pull(got[:8])[0]):
                if number == 10:
                    grad = got[8] / (1.0 + jnp.exp(params[10]))
                grads_ref[pl.ds(block * 512 + number, 8, stride=64), :] = grad
            for tile in range(8):
                result(block * 8 + tile).start()
            return carry

        def result(tile):
            return pltpu.make_async_copy(
                grads_ref.at[pl.ds(pl.multiple_of(tile * 64, 64), 59), :],
                out_ref.at[:, pl.ds(pl.multiple_of(tile * 128, 128), 128)],
                out_sems.at[tile],
            )

        for copy in copies:
            copy.wait()
        lax.fori_loop(0, 5, block_grads, 0)
        for tile in range(ROWS):
            result(tile).wait()

    return kernel


def shape(*dims, dtype=F32):
    return jax.ShapeDtypeStruct(dims, dtype)


def exchange(chunks, strips):
    sent = chunks.reshape(strips, 1, 768)
    got = lax.all_to_all(sent, "strip", split_axis=0, concat_axis=0, tiled=True)
    return got.reshape(strips * 6, 128)


def per_device(params, camera, send_index, send_count, tile_list, target):
    strips = lax.axis_size("strip")
    index = lax.axis_index("strip")
    per_view = strips // VIEWS
    offset = per_view // 2
    position = (index + offset) % strips
    rows_strip = target.shape[1]
    width = target.shape[2]
    focal = 0.5 * width
    centre_y = 0.5 * rows_strip * per_view
    top = ((position % per_view) * rows_strip + rows_strip // 2).astype(F32).reshape(1)
    keep = jnp.stack([position % per_view != 0, position % per_view != per_view - 1]).astype(F32)
    ahead = [(i, (i + 1) % strips) for i in range(strips)]
    behind = [((i + 1) % strips, i) for i in range(strips)]

    chunks, place = pl.pallas_call(
        owner_kernel(focal, 0.5 * width, centre_y),
        out_shape=(shape(strips * 6, 128), shape(ROWS, 128, dtype=jnp.int32)),
        in_specs=[SMEM, SMEM, ANY, VMEM],
        scratch_shapes=[
            pltpu.VMEM((strips, 128), jnp.int32),
            pltpu.VMEM((ROWS + 8, 128), jnp.int32),
            pltpu.VMEM((FEATS, ROWS, 128), F32),
            pltpu.VMEM(((ROWS + 2) * 16, 128), F32),
            pltpu.VMEM((ROWS * 64, 128), F32),
            pltpu.SemaphoreType.DMA((ROWS,)),
        ],
        name="owner",
    )(camera, send_count, params, send_index.T)
    arrived = exchange(chunks, strips)

    truth_above = lax.ppermute(target[:, 6:16, :], "strip", ahead)
    truth_below = lax.ppermute(target[:, 0:10, :], "strip", behind)
    truth, mean_y, power_y = pl.pallas_call(
        truth_kernel,
        out_shape=(shape(5, 128, 128), shape(640, 128), shape(640, 128)),
        in_specs=[SMEM, VMEM, VMEM, VMEM],
        scratch_shapes=[
            pltpu.VMEM((5, 128, 128), F32),
            pltpu.VMEM((128, 128), F32),
            pltpu.VMEM((2, 656, 128), F32),
        ],
        name="truth",
    )(keep, target, truth_above, truth_below)
    listed = pl.pallas_call(
        invert_kernel, out_shape=shape(ROWS, 128, dtype=jnp.int32), name="listed"
    )(tile_list)

    flat_list = tile_list.T.reshape(ROWS, 128)
    across = jnp.asarray(
        (np.arange(ROWS * 128) % ROWS * 16 + 8).astype(np.float32).reshape(ROWS, 128)
    )
    rows = entry_basis()
    basis = np.zeros((24, 256), np.float32)
    basis[0:18] = np.repeat(rows, 3, axis=0)
    moment = np.zeros((16, 256), np.float32)
    moment[0:6] = rows
    basis = jnp.asarray(basis, BF16)
    moment = jnp.asarray(moment, BF16)
    image, first, last, entries, colour, counts, alphas, weights = pl.pallas_call(
        render_kernel,
        out_shape=(
            shape(3, 5, 16, 128),
            shape(150, 128),
            shape(150, 128),
            shape(5, ROWS, 128),
            shape(3, ROWS, 128),
            shape(strips, dtype=jnp.int32),
            shape(2, 5120, 128),
            shape(2, 5120, 128),
        ),
        in_specs=[SMEM, VMEM, VMEM, VMEM, VMEM, VMEM],
        out_specs=(VMEM, VMEM, VMEM, VMEM, VMEM, SMEM, ANY, ANY),
        scratch_shapes=[
            pltpu.VMEM(((ROWS + 2) * 16, 128), F32),
            pltpu.VMEM((ROWS * 24, 128), F32),
            pltpu.VMEM((640, 256), F32),
            pltpu.VMEM((640, 256), F32),
            pltpu.VMEM((2, 5120, 128), F32),
            pltpu.VMEM((2, 5120, 128), F32),
            pltpu.VMEM((ROWS * 16, 128), F32),
            pltpu.VMEM((2, ROWS * 16, 128), F32),
            pltpu.SemaphoreType.DMA((32,)),
        ],
        name="render",
    )(top, arrived, flat_list, tile_list, across, basis)
    above = lax.ppermute(last, "strip", ahead)
    below = lax.ppermute(first, "strip", behind)
    grads = pl.pallas_call(
        gradient_kernel,
        out_shape=shape(strips * 6, 128),
        in_specs=[SMEM, SMEM] + [VMEM] * 10 + [ANY, ANY],
        scratch_shapes=[
            pltpu.VMEM((5, 128, 128), F32),
            pltpu.VMEM((5, 128, 128), F32),
            pltpu.VMEM((5, 128, 128), F32),
            pltpu.VMEM((128, 128), F32),
            pltpu.VMEM((3, 656, 128), F32),
            pltpu.VMEM((3, 656, 128), F32),
            pltpu.VMEM((2, 5120, 128), F32),
            pltpu.VMEM((2, 5120, 128), F32),
            pltpu.VMEM((640, 256), F32),
            pltpu.VMEM((640, 256), F32),
            pltpu.VMEM((30, 8, 128), F32),
            pltpu.VMEM((2, ROWS * 16, 128), F32),
            pltpu.VMEM((ROWS * 8 + 40, 128), F32),
            pltpu.VMEM((ROWS * 16, 128), F32),
            pltpu.VMEM((FEATS, ROWS, 128), F32),
            pltpu.VMEM(((ROWS + 2) * 16, 128), F32),
            pltpu.SemaphoreType.DMA((4,)),
        ],
        name="gradient",
    )(
        counts, keep, image, above, below, truth, mean_y, power_y,
        entries, colour, listed, moment, alphas, weights,
    )
    returned = exchange(grads, strips)
    return pl.pallas_call(
        pull_kernel(focal, 0.5 * width, centre_y),
        out_shape=shape(59, ROWS * 128),
        in_specs=[SMEM, SMEM, ANY, VMEM, VMEM],
        out_specs=ANY,
        scratch_shapes=[
            pltpu.VMEM(((ROWS + 2) * 16, 128), F32),
            pltpu.VMEM((ROWS * 64, 128), F32),
            pltpu.VMEM((ROWS * 64, 128), F32),
            pltpu.SemaphoreType.DMA((ROWS,)),
            pltpu.SemaphoreType.DMA((ROWS,)),
        ],
        name="pull",
    )(camera, send_count, params, place, returned)


def solution(mesh):
    return jax.shard_map(
        per_device,
        mesh=mesh,
        in_specs=(
            P(None, "strip"),
            P(),
            P("strip", None),
            P("strip"),
            P("strip", None),
            P(None, "strip", None),
        ),
        out_specs=P(None, "strip"),
        check_vma=False,
    )
```

```python
import numpy as np

import jax
import jax.numpy as jnp
from jax import lax
from jax.experimental import pallas as pl
from jax.experimental.pallas import tpu as pltpu
from jax.sharding import PartitionSpec as P

VIEWS = 4
ROWS = 40
FEATS = 9
LOG2E = 1.4426950408889634
harmonic_zero = 0.28209479177387814
harmonic_one = 0.4886025119029199
harmonic_two = (
    1.0925484305920792,
    -1.0925484305920792,
    0.31539156525252005,
    -1.0925484305920792,
    0.5462742152960396,
)
harmonic_three = (
    -0.5900435899266435,
    2.890611442640554,
    -0.4570457994644658,
    0.3731763325901154,
    -0.4570457994644658,
    1.445305721320277,
    -0.5900435899266435,
)
light_term = 0.0001
contrast_term = 0.0009
F32 = jnp.float32
BF16 = jnp.bfloat16
SMEM = pl.BlockSpec(memory_space=pltpu.SMEM)
VMEM = pl.BlockSpec(memory_space=pltpu.VMEM)
ANY = pl.BlockSpec(memory_space=pl.ANY)


def iota(shape, axis):
    return lax.broadcasted_iota(jnp.int32, shape, axis)


def dot_nt(a, b):
    return lax.dot_general(a, b, (((1,), (1,)), ((), ())), preferred_element_type=F32)


def rounded(x):
    return x.astype(BF16).astype(F32)


def pick(row, lanes):
    return jnp.take_along_axis(
        jnp.broadcast_to(row, lanes.shape), lanes, axis=1, mode="promise_in_bounds"
    )


def harmonics(along_x, along_y, along_z):
    square_x = along_x * along_x
    square_y = along_y * along_y
    square_z = along_z * along_z
    return [
        harmonic_zero + 0.0 * along_x,
        -harmonic_one * along_y,
        harmonic_one * along_z,
        -harmonic_one * along_x,
        harmonic_two[0] * along_x * along_y,
        harmonic_two[1] * along_y * along_z,
        harmonic_two[2] * (2.0 * square_z - square_x - square_y),
        harmonic_two[3] * along_x * along_z,
        harmonic_two[4] * (square_x - square_y),
        harmonic_three[0] * along_y * (3.0 * square_x - square_y),
        harmonic_three[1] * along_x * along_y * along_z,
        harmonic_three[2] * along_y * (4.0 * square_z - square_x - square_y),
        harmonic_three[3] * along_z * (2.0 * square_z - 3.0 * square_x - 3.0 * square_y),
        harmonic_three[4] * along_x * (4.0 * square_z - square_x - square_y),
        harmonic_three[5] * along_z * (square_x - square_y),
        harmonic_three[6] * along_x * (square_x - 3.0 * square_y),
    ]


def project(params, camera, focal, centre_x, centre_y):
    rotation = [[camera[3 * row + col] for col in range(3)] for row in range(3)]
    mean = [params[axis] for axis in range(3)]
    placed = [
        rotation[row][0] * mean[0]
        + rotation[row][1] * mean[1]
        + rotation[row][2] * mean[2]
        + camera[9 + row]
        for row in range(3)
    ]
    depth = placed[2]
    inverse = 1.0 / depth
    screen_x = focal * placed[0] * inverse + centre_x
    screen_y = focal * placed[1] * inverse + centre_y
    quaternion = params[6:10]
    scale = lax.rsqrt(
        quaternion[0] * quaternion[0]
        + quaternion[1] * quaternion[1]
        + quaternion[2] * quaternion[2]
        + quaternion[3] * quaternion[3]
    )
    real, imag_x, imag_y, imag_z = [part * scale for part in quaternion]
    turn = [
        [
            1.0 - 2.0 * (imag_y * imag_y + imag_z * imag_z),
            2.0 * (imag_x * imag_y - real * imag_z),
            2.0 * (imag_x * imag_z + real * imag_y),
        ],
        [
            2.0 * (imag_x * imag_y + real * imag_z),
            1.0 - 2.0 * (imag_x * imag_x + imag_z * imag_z),
            2.0 * (imag_y * imag_z - real * imag_x),
        ],
        [
            2.0 * (imag_x * imag_z - real * imag_y),
            2.0 * (imag_y * imag_z + real * imag_x),
            1.0 - 2.0 * (imag_x * imag_x + imag_y * imag_y),
        ],
    ]
    scales = [jnp.exp(part) for part in params[3:6]]
    near = focal * inverse
    slant = [-near * placed[0] * inverse, -near * placed[1] * inverse]
    facing = [
        [near * rotation[row][col] + slant[row] * rotation[2][col] for col in range(3)]
        for row in range(2)
    ]
    stretch = [
        [
            (
                facing[row][0] * turn[0][col]
                + facing[row][1] * turn[1][col]
                + facing[row][2] * turn[2][col]
            )
            * scales[col]
            for col in range(3)
        ]
        for row in range(2)
    ]
    cov_xx = (
        stretch[0][0] * stretch[0][0]
        + stretch[0][1] * stretch[0][1]
        + stretch[0][2] * stretch[0][2]
        + 0.3
    )
    cov_xy = (
        stretch[0][0] * stretch[1][0]
        + stretch[0][1] * stretch[1][1]
        + stretch[0][2] * stretch[1][2]
    )
    cov_yy = (
        stretch[1][0] * stretch[1][0]
        + stretch[1][1] * stretch[1][1]
        + stretch[1][2] * stretch[1][2]
        + 0.3
    )
    over = 1.0 / (cov_xx * cov_yy - cov_xy * cov_xy)
    shrink = 1.0 / jnp.sqrt(placed[0] * placed[0] + placed[1] * placed[1] + depth * depth)
    heading = [
        (
            rotation[0][col] * placed[0]
            + rotation[1][col] * placed[1]
            + rotation[2][col] * placed[2]
        )
        * shrink
        for col in range(3)
    ]
    basis = harmonics(heading[0], heading[1], heading[2])
    colour = []
    for channel in range(3):
        total = 0.5 + basis[0] * params[11 + channel]
        for k in range(1, 16):
            total = total + basis[k] * params[11 + 3 * k + channel]
        colour.append(total)
    return [
        screen_x,
        screen_y,
        cov_yy * over,
        -cov_xy * over,
        cov_xx * over,
        colour[0],
        colour[1],
        colour[2],
    ]


def log_sigmoid(logit):
    return jnp.minimum(logit, 0.0) - jnp.log(1.0 + jnp.exp(-jnp.abs(logit)))


def send_views(count_ref, strips):
    per_view = strips // VIEWS
    offset = per_view // 2
    runs = []
    for strip in range(strips):
        view = (strip + offset) % strips // per_view
        if not runs or runs[-1][1] != view:
            runs.append([strip, view])
    return runs


def compact_ints(chunk_ref, count_ref, out_ref, steps):
    lane = iota((1, 128), 1)

    def step(number, carry):
        start, held = carry
        live = count_ref[number]
        shift = start & 127
        row = start >> 7
        chunk = pltpu.roll(chunk_ref[pl.ds(number, 1), :], shift, axis=1)
        held = jnp.where(lane >= shift, chunk, held)
        out_ref[pl.ds(row, 1), :] = held
        held = jnp.where(shift + live >= 128, chunk, held)
        return start + live, held

    lax.fori_loop(0, steps, step, (jnp.int32(0), jnp.zeros((1, 128), jnp.int32)), unroll=16)


def compact_feats(chunk_ref, count_of, table_ref, steps, spot=None):
    lane = iota((8, 128), 1)

    def step(number, carry):
        start, held, last = carry
        if spot is not None:
            chunk = chunk_ref[pl.ds(spot(number), 8), :]
        elif isinstance(number, int) and number == steps - 1:
            chunk = pltpu.roll(chunk_ref[number * 6 - 2 : number * 6 + 6, :], 6, axis=0)
        else:
            chunk = chunk_ref[pl.ds(number * 6, 8), :]
        live = count_of(number, chunk)
        shift = start & 127
        row = start >> 7
        even = pltpu.roll(chunk, (shift + 48) & 127, axis=1)
        odd = pltpu.roll(chunk, (shift + 96) & 127, axis=1)
        chunk = pltpu.roll(chunk, shift, axis=1)
        rest = jnp.where(((lane - shift) & 127) < 48, even, pltpu.roll(odd, 7, axis=0))
        fresh = lane >= shift
        held = jnp.where(fresh, chunk, held)
        last = jnp.where(fresh, rest, last)
        base = pl.multiple_of(row * 16, 16)
        table_ref[pl.ds(base, 8), :] = held
        table_ref[pl.ds(base + 8, 8), :] = last
        crossed = shift + live >= 128
        held = jnp.where(crossed, chunk, held)
        last = jnp.where(crossed, rest, last)
        return start + live, held, last

    zero = jnp.zeros((8, 128), F32)
    carry = lax.fori_loop(0, steps - 16, step, (jnp.int32(0), zero, zero), unroll=16)
    for number in range(steps - 16, steps):
        carry = step(number, carry)


def expand_feats(table_ref, count_ref, out_ref, steps, spot):
    lane = iota((8, 128), 1)
    sub = iota((8, 128), 0)
    even = (sub & 1) == 0
    offset = lane - jnp.where(even, 80, 32)

    def step(number, start):
        live = count_ref[number]
        shift = start & 127
        base = pl.multiple_of((start >> 7) * 16, 16)
        back = 128 - shift
        this, rest = table_ref[pl.ds(base, 8), :], table_ref[pl.ds(base + 8, 8), :]
        next_, next_rest = table_ref[pl.ds(base + 16, 8), :], table_ref[pl.ds(base + 24, 8), :]

        def turned(value, by):
            return pltpu.roll(value, (back + by) & 127, axis=1)

        main = jnp.where(lane < back, turned(this, 0), turned(next_, 0))
        tail = jnp.where(
            offset < back,
            jnp.where(even, turned(rest, 80), turned(rest, 32)),
            jnp.where(even, turned(next_rest, 80), turned(next_rest, 32)),
        )
        tail = jnp.where((sub == 1) & (lane == 127), live.astype(F32), tail)
        out_ref[pl.ds(spot(number), 6), :] = jnp.where(lane < 80, main, tail)[0:6]
        return start + live

    lax.fori_loop(0, steps, step, jnp.int32(0), unroll=16)


def line_of(feature):
    return feature if feature < 6 else 8 + 2 * (feature - 6)


def put_feature(table_ref, block, feature, value):
    line = line_of(feature)
    table_ref[pl.ds(block * 128 + line, 8, stride=16), :] = value
    if feature >= 6:
        table_ref[pl.ds(block * 128 + line + 1, 8, stride=16), :] = value


def table_line(table_ref, row, feature):
    line = row * 16 + line_of(feature)
    return table_ref[line : line + 1, :]


def fetch_params(params_ref, local_ref, sems):
    copies = [
        pltpu.make_async_copy(
            params_ref.at[:, pl.ds(tile * 128, 128)],
            local_ref.at[pl.ds(tile * 64, 59), :],
            sems.at[tile],
        )
        for tile in range(ROWS)
    ]
    for copy in copies:
        copy.start()
    return copies


def invert(rows_ref, out_ref):
    high = iota((ROWS, 128), 0)
    low = iota((128, 128), 0)
    lane = iota((ROWS, 128), 1).astype(F32)
    total = jnp.zeros((2 * ROWS, 128), F32)
    for pair in range(ROWS // 2):
        lefts = []
        rights = []
        for row in (2 * pair, 2 * pair + 1):
            number = rows_ref[row : row + 1, :]
            same = high == (number >> 7)
            lefts.append(
                jnp.concatenate([jnp.where(same, float(row), 0.0), jnp.where(same, lane, 0.0)], 0)
            )
            rights.append(jnp.where(low == (number & 127), 1.0, 0.0))
        total = total + dot_nt(
            jnp.concatenate(lefts, 1).astype(BF16), jnp.concatenate(rights, 1).astype(BF16)
        )
    out_ref[...] = (total[:ROWS] * 128.0 + total[ROWS:]).astype(jnp.int32)


def select_camera(camera_ref, place, run_starts):
    values = []
    for entry in range(12):
        value = jnp.full(place.shape, camera_ref[run_starts[0][1], entry], F32)
        for start, view in run_starts[1:]:
            value = jnp.where(place >= start, camera_ref[view, entry], value)
        values.append(value)
    return values


def run_bounds(count_ref, strips):
    runs = send_views(count_ref, strips)
    bounds = [(jnp.int32(0), runs[0][1])]
    for (first, _), (last, view) in zip(runs[:-1], runs[1:]):
        begin = bounds[-1][0]
        total = lax.fori_loop(
            first, last, lambda number, sum_: sum_ + count_ref[number], begin, unroll=True
        )
        bounds.append((total, view))
    return bounds


def owner_kernel(focal, centre_x, centre_y):
    def kernel(
        camera_ref, count_ref, spot_ref, params_ref, index_ref, target_ref, list_ref,
        out_ref, place_ref, pack_ref,
        wide_ref, rows_ref, feats_ref, table_ref, local_ref, sems,
    ):
        copies = fetch_params(params_ref, local_ref, sems)
        for tile in range(5):
            for channel in range(3):
                at = tile * 56 + channel * 16
                pack_ref[at : at + 16, :] = target_ref[channel, :, tile * 128 : tile * 128 + 128]
            pack_ref[tile * 56 + 48 : tile * 56 + 56, :] = list_ref[
                tile * 8 : tile * 8 + 8, :
            ].astype(F32)
        strips = index_ref.shape[1]
        wide_ref[...] = jnp.concatenate(
            [index_ref[...], jnp.zeros((128 - index_ref.shape[0], strips), jnp.int32)], 0
        ).T
        compact_ints(wide_ref, count_ref, rows_ref, strips)
        invert(rows_ref, place_ref)
        bounds = run_bounds(count_ref, strips)
        for copy in copies:
            copy.wait()

        def project_block(block, carry):
            rows = pl.ds(block * 8, 8)
            camera = select_camera(camera_ref, place_ref[rows, :], bounds)
            params = [
                local_ref[pl.ds(block * 512 + number, 8, stride=64), :] for number in range(59)
            ]
            feats = project(params, camera, focal, centre_x, centre_y)
            feats.append(log_sigmoid(params[10]))
            for feature in range(FEATS):
                feats_ref[feature, rows, :] = feats[feature]
            return carry

        lax.fori_loop(0, 5, project_block, 0)

        def gather_block(block, carry):
            number = rows_ref[pl.ds(block * 8, 8), :]
            high = number >> 7
            low = number & 127
            got = [jnp.zeros((8, 128), F32)] * FEATS
            for row in range(ROWS):
                same = high == row
                for feature in range(FEATS):
                    value = pick(feats_ref[feature, row : row + 1, :], low)
                    got[feature] = jnp.where(same, value, got[feature])
            for feature in range(FEATS):
                put_feature(table_ref, block, feature, got[feature])
            return carry

        lax.fori_loop(0, 5, gather_block, 0)
        expand_feats(table_ref, count_ref, out_ref, strips, lambda number: spot_ref[number])

    return kernel


def entry_basis():
    pixel = np.arange(256)
    x = pixel % 16 - 7.5
    y = pixel // 16 - 7.5
    return np.stack([np.ones(256), x, y, x * x, x * y, y * y]).astype(np.float32)


def swap_tiles(x):
    sub = iota((8, 128), 0)
    group = iota((8, 128), 1) >> 4
    for k in (1, 2, 4):
        up = pltpu.roll(pltpu.roll(x, 8 - k, axis=0), 16 * k, axis=1)
        down = pltpu.roll(pltpu.roll(x, k, axis=0), 128 - 16 * k, axis=1)
        s = (sub & k) != 0
        g = (group & k) != 0
        x = jnp.where(s == g, x, jnp.where(g, up, down))
    return x


def coarse_fine(x):
    coarse = x.astype(BF16)
    return coarse, (x - coarse.astype(F32)).astype(BF16)


def by_entry(x):
    lane = iota((8, 128), 1)
    order = ((lane & 7) << 4) | (lane >> 3)
    return jnp.take_along_axis(swap_tiles(x), order, axis=1, mode="promise_in_bounds")


def by_tile(x):
    lane = iota((8, 128), 1)
    order = ((lane & 15) << 3) | (lane >> 4)
    return swap_tiles(jnp.take_along_axis(x, order, axis=1, mode="promise_in_bounds"))


def tile_rows(ref, half, tile):
    base = (tile >> 3) * 128 + (tile & 7)
    return jnp.concatenate(
        [ref[half, pl.ds(base + turn * 640, 16, stride=8), :] for turn in range(8)], 0
    )


def turned_colours(colour_ref, turn, group):
    return [
        pltpu.roll(
            colour_ref[channel, group * 8 : group * 8 + 8, :], 128 - turn * 16 & 127, axis=1
        )
        for channel in range(3)
    ]


def lit(turned, entry):
    return [jnp.broadcast_to(part[:, entry : entry + 1], (8, 128)) for part in turned]


def render_kernel(
    chunks_ref, basis_ref, moved_ref,
    image_ref, first_ref, last_ref, entries_ref, colour_ref, count_ref, alphas_ref, weights_ref,
    table_ref, order_ref, lines_ref, power_a, power_b, alpha_ref, weight_ref, tint_ref, shown_ref, sems,
):
    for tile in range(5):
        for channel in range(3):
            at = 150 + (channel * 5 + tile) * 10
            base = tile * 56 + channel * 16
            first_ref[at : at + 10, :] = moved_ref[base : base + 10, :]
            last_ref[at : at + 10, :] = moved_ref[base + 6 : base + 16, :]
    strips = chunks_ref.shape[0] // 6

    def count_of(number, chunk):
        live = chunk[1, 127].astype(jnp.int32)
        count_ref[number] = live
        return live

    compact_feats(chunks_ref, count_of, table_ref, strips)
    per_view = strips // VIEWS
    top = (lax.rem(position_of(strips), per_view) * 16 + 8).astype(F32)
    for group in range(5):
        rows = slice(group * 8, group * 8 + 8)
        order_ref[rows, :] = by_entry(moved_ref[group * 56 + 48 : group * 56 + 56, :]).astype(
            jnp.int32
        )

    def entry_block(block, carry):
        rows = pl.ds(block * 8, 8)
        number = order_ref[rows, :]
        high = number >> 7
        low = number & 127
        got = [jnp.zeros((8, 128), F32)] * FEATS
        for row in range(ROWS):
            same = high == row
            for feature in range(FEATS):
                value = pick(table_line(table_ref, row, feature), low)
                got[feature] = jnp.where(same, value, got[feature])
        across = (block * 8 + (iota((8, 128), 1) & 7)) * 16 + 8
        x = got[0] - across.astype(F32)
        y = got[1] - top
        a, b, c = got[2:5]
        for slot, value in enumerate((x, y, a, b, c)):
            entries_ref[slot, rows, :] = value
        terms = [
            got[8] - 0.5 * (a * x * x + c * y * y) - b * x * y,
            a * x + b * y,
            c * y + b * x,
            -0.5 * a,
            -b,
            -0.5 * c,
        ]
        for slot, term in enumerate(terms):
            term = term * LOG2E
            for part in range(3):
                piece = rounded(term)
                lines_ref[pl.ds(block * 24 + slot * 3 + part, 8, stride=120), :] = piece
                term = term - piece
        for slot in range(18, 24):
            lines_ref[pl.ds(block * 24 + slot, 8, stride=120), :] = jnp.zeros((8, 128), F32)
        for channel in range(3):
            colour_ref[channel, rows, :] = got[5 + channel]
        return carry

    lax.fori_loop(0, 5, entry_block, 0)
    values = [
        by_tile(colour_ref[channel, group * 8 : group * 8 + 8, :])
        for group in range(5)
        for channel in range(3)
    ]
    for number, value in enumerate(values):
        group, channel = divmod(number, 3)
        colour_ref[channel, group * 8 : group * 8 + 8, :] = value
        for part in range(3):
            piece = rounded(value)
            tint_ref[pl.ds(group * 128 + channel * 3 + part, 8, stride=16), :] = piece
            value = value - piece
    basis = basis_ref[...]

    def powers(turn, power_ref):
        for part in range(5):
            lines = lines_ref[pl.ds(pl.multiple_of((turn * 5 + part) * 24, 8), 24), :]
            power_ref[part * 128 : part * 128 + 128, :] = jnp.dot(
                lines.T.astype(BF16), basis, preferred_element_type=F32
            )

    def copies(turn):
        rows = pl.ds(turn * 640, 640)
        found = []
        for half in range(2):
            for slot, (near, far) in enumerate(((alpha_ref, alphas_ref), (weight_ref, weights_ref))):
                found.append(
                    pltpu.make_async_copy(
                        near.at[half, rows, :],
                        far.at[half, rows, :],
                        sems.at[turn * 4 + slot * 2 + half],
                    )
                )
        return found

    def scan(turn, power_ref, through):
        through = list(through)
        for entry in range(16):
            for group in range(5):
                at = group * 128 + entry * 8
                for half in range(2):
                    slot = group * 2 + half
                    alpha = jnp.exp2(power_ref[at : at + 8, half * 128 : half * 128 + 128])
                    weight = alpha * through[slot]
                    through[slot] = through[slot] - weight
                    alpha_ref[half, pl.ds(turn * 640 + at, 8), :] = alpha
                    weight_ref[half, pl.ds(turn * 640 + at, 8), :] = weight
        return tuple(through)

    def blend(pair, through):
        powers(2 * pair + 1, power_b)
        through = scan(2 * pair, power_a, through)
        powers(jnp.minimum(2 * pair + 2, 7), power_a)
        through = scan(2 * pair + 1, power_b, through)
        for turn in (2 * pair, 2 * pair + 1):
            for copy in copies(turn):
                copy.start()
        return through

    powers(0, power_a)
    lax.fori_loop(0, 4, blend, (jnp.ones((8, 128), F32),) * 10)

    def tints(tile, carry):
        at = pl.ds(pl.multiple_of(tile * 16, 16), 16)
        tint = tint_ref[at, :].astype(BF16)
        halves = [coarse_fine(tile_rows(weight_ref, half, tile)) for half in range(2)]
        weight = jnp.concatenate(
            [jnp.concatenate([halves[0][part], halves[1][part]], 1) for part in range(2)], 0
        )
        total = jnp.dot(jnp.concatenate([tint, tint], 1), weight, preferred_element_type=F32)
        for half in range(2):
            shown_ref[half, at, :] = total[:, half * 128 : half * 128 + 128]
        return carry

    lax.fori_loop(0, ROWS, tints, 0, unroll=4)
    for group in range(5):
        for channel in range(3):
            for half in range(2):
                parts = [
                    shown_ref[half, pl.ds(group * 128 + channel * 3 + part, 8, stride=16), :]
                    for part in range(3)
                ]
                image_ref[channel, group, half * 8 : half * 8 + 8, :] = swap_tiles(
                    parts[0] + parts[1] + parts[2]
                )
            at = (channel * 5 + group) * 10
            first_ref[at : at + 10, :] = image_ref[channel, group, 0:10, :]
            last_ref[at : at + 10, :] = image_ref[channel, group, 6:16, :]
    for turn in range(8):
        for copy in copies(turn):
            copy.wait()


def window_weights():
    offsets = np.arange(11, dtype=np.float64) - 5.0
    raw = np.exp(-offsets * offsets / 4.5)
    return [float(value) for value in raw / raw.sum()]


WINDOW = window_weights()


def tap_sum(load):
    total = WINDOW[5] * load(5)
    for k in range(5):
        total = total + WINDOW[k] * (load(k) + load(10 - k))
    return total


def down_rows(field_ref, slot, out_ref):
    for tile in range(5):
        for channel in range(3):
            base = channel * 40
            out_ref[base : base + 32, :] = tap_sum(
                lambda k: field_ref[tile, base + k : base + k + 32, :]
            )
        yield tile, out_ref[...].T


def extend(ext_ref, own, above, below, keep_above, keep_below):
    for tile in range(5):
        for channel in range(3):
            base = channel * 40
            ext_ref[tile, base : base + 10, :] = above(channel, tile) * keep_above
            ext_ref[tile, base + 10 : base + 26, :] = own(channel, tile)
            ext_ref[tile, base + 26 : base + 36, :] = below(channel, tile) * keep_below
            ext_ref[tile, base + 36 : base + 40, :] = jnp.zeros((4, 128), F32)
        ext_ref[tile, 120:128, :] = jnp.zeros((8, 128), F32)


def clear_ends(ref, slot):
    ref[slot, 0:8, :] = jnp.zeros((8, 128), F32)
    ref[slot, 648:656, :] = jnp.zeros((8, 128), F32)


def invert_kernel(moved_ref, out_ref, rows_ref):
    for group in range(5):
        rows_ref[group * 8 : group * 8 + 8, :] = moved_ref[
            group * 56 + 48 : group * 56 + 56, :
        ].astype(jnp.int32)
    invert(rows_ref, out_ref)


def gradient_kernel(
    count_ref, image_ref, above_ref, below_ref, moved_ref,
    entries_ref, colour_ref, place_ref, moment_ref, alphas_ref, weights_ref,
    out_ref,
    ext_ref, square_ref, cross_ref, truth_ref, ideal_ref, rows_ref, cols_ref, parts_ref,
    alpha_ref, weight_ref, pull_a, pull_b, light_ref, split_ref,
    sums_ref, tint_ref, feats_ref, table_ref, sems,
):
    copies = [
        pltpu.make_async_copy(far.at[half], near.at[half], sems.at[slot * 2 + half])
        for slot, (far, near) in enumerate(((alphas_ref, alpha_ref), (weights_ref, weight_ref)))
        for half in range(2)
    ]
    for copy in copies:
        copy.start()
    strips = out_ref.shape[0] // 6
    keep_above, keep_below = keeps(strips)
    def rim(base):
        return lambda ref: lambda channel, tile: ref[
            base + (channel * 5 + tile) * 10 : base + (channel * 5 + tile) * 10 + 10, :
        ]

    extend(
        ext_ref,
        lambda channel, tile: image_ref[channel, tile],
        rim(0)(above_ref),
        rim(0)(below_ref),
        keep_above,
        keep_below,
    )
    extend(
        truth_ref,
        lambda channel, tile: moved_ref[tile * 56 + channel * 16 : tile * 56 + channel * 16 + 16, :],
        rim(150)(above_ref),
        rim(150)(below_ref),
        keep_above,
        keep_below,
    )
    for tile in range(5):
        square_ref[tile] = ext_ref[tile] * ext_ref[tile]
        cross_ref[tile] = ext_ref[tile] * truth_ref[tile]
        ideal_ref[tile] = truth_ref[tile] * truth_ref[tile]
    rows_ref[...] = jnp.zeros((128, 128), F32)
    for slot in range(3):
        clear_ends(parts_ref, slot)
    for slot, source in enumerate((ext_ref, square_ref, cross_ref, truth_ref, ideal_ref)):
        clear_ends(cols_ref, slot)
        for tile, turned in down_rows(source, slot, rows_ref):
            cols_ref[slot, 8 + tile * 128 : 136 + tile * 128, :] = turned
    lane = iota((8, 128), 1)
    row = lane - jnp.where(lane >= 80, 80, jnp.where(lane >= 40, 40, 0))
    live = jnp.where(row < 5, keep_above, jnp.where(row >= 21, keep_below, 1.0))
    live = jnp.where((row < 26) & (lane < 120), live, 0.0)[0:1, :]

    def similarity(step, carry):
        base = step * 32
        mean_x, power_x, cross, mean_y, power_y = [
            tap_sum(lambda k: cols_ref[slot, pl.ds(base + 3 + k, 32), :]) for slot in range(5)
        ]
        both = mean_x * mean_y
        squares = mean_x * mean_x + mean_y * mean_y
        light_up = 2.0 * both + light_term
        light_down = squares + light_term
        sharp_up = 2.0 * (cross - both) + contrast_term
        sharp_down = power_x + power_y - squares + contrast_term
        over = 1.0 / (light_down * sharp_down)
        score = light_up * sharp_up * over
        scale = live * over
        cross_grad = -2.0 * light_up * scale
        power_grad = score * light_down * scale
        mean_grad = (
            -2.0 * mean_y * (sharp_up - light_up) + 2.0 * mean_x * score * (sharp_down - light_down)
        ) * scale
        at = pl.ds(base + 8, 32)
        parts_ref[0, at, :] = mean_grad
        parts_ref[1, at, :] = power_grad
        parts_ref[2, at, :] = cross_grad
        return carry

    lax.fori_loop(0, 20, similarity, 0)
    for tile in range(5):
        for slot in range(3):
            turned = tap_sum(
                lambda k: parts_ref[slot, tile * 128 + 3 + k : tile * 128 + 131 + k, :]
            ).T
            (square_ref, cross_ref, cols_ref)[slot][0, 0:128, :] = turned
        for channel in range(3):
            base = channel * 40
            down = [
                tap_sum(lambda k: (square_ref, cross_ref, cols_ref)[slot][0, base + k : base + k + 16, :])
                for slot in range(3)
            ]
            own = image_ref[channel, tile]
            truth = truth_ref[tile, base + 10 : base + 26, :]
            pull = down[0] + 2.0 * own * down[1] + truth * down[2]
            for half in range(2):
                value = swap_tiles(pull[half * 8 : half * 8 + 8])
                light_ref[tile * 6 + half * 3 + channel] = value
                for part in range(3):
                    piece = rounded(value)
                    split_ref[half, pl.ds(tile * 128 + channel * 3 + part, 8, stride=16), :] = piece
                    value = value - piece
    for copy in copies:
        copy.wait()
    moments = moment_ref[...]

    def scan(turn, pull_ref, behind):
        behind = list(behind)
        turned = [
            [
                pltpu.roll(
                    colour_ref[channel, group * 8 : group * 8 + 8, :], 128 - turn * 16 & 127, axis=1
                )
                for channel in range(3)
            ]
            for group in range(5)
        ]
        for entry in range(15, -1, -1):
            for group in range(5):
                at = group * 128 + entry * 8
                rows = pl.ds(turn * 640 + at, 8)
                colour = [
                    jnp.broadcast_to(turned[group][channel][:, entry : entry + 1], (8, 128))
                    for channel in range(3)
                ]
                for half in range(2):
                    slot = group * 2 + half
                    light = group * 6 + half * 3
                    value = (
                        colour[0] * light_ref[light]
                        + colour[1] * light_ref[light + 1]
                        + colour[2] * light_ref[light + 2]
                    )
                    delta = value - behind[slot]
                    behind[slot] = behind[slot] + alpha_ref[half, rows, :] * delta
                    pull_ref[at : at + 8, half * 128 : half * 128 + 128] = (
                        weight_ref[half, rows, :] * delta
                    )
        return tuple(behind)

    def reduce(turn, pull_ref):
        for part in range(5):
            coarse, fine = coarse_fine(pull_ref[part * 128 : part * 128 + 128, :])
            total = dot_nt(moments, coarse) + dot_nt(moments, fine)
            sums_ref[pl.ds(pl.multiple_of((turn * 5 + part) * 8, 8), 8), :] = total[0:8]

    def backward(count, behind):
        turn = 7 - 2 * count
        reduce(turn + 1, pull_b)
        behind = scan(turn, pull_a, behind)
        reduce(turn, pull_a)
        return scan(turn - 1, pull_b, behind)

    pull_b[...] = jnp.zeros((640, 256), F32)
    lax.fori_loop(0, 4, backward, (jnp.zeros((8, 128), F32),) * 10)
    reduce(0, pull_b)

    def tints(tile, carry):
        at = pl.ds(pl.multiple_of(tile * 16, 16), 16)
        halves = [coarse_fine(tile_rows(weight_ref, half, tile)) for half in range(2)]
        weight = jnp.concatenate(
            [jnp.concatenate([halves[0][part], halves[1][part]], 1) for part in range(2)], 0
        )
        light = jnp.concatenate([split_ref[half, at, :].astype(BF16) for half in range(2)], 1)
        total = dot_nt(light, weight)
        total = total[:, 0:128] + total[:, 128:256]
        tint_ref[at, :] = total
        return carry

    lax.fori_loop(0, ROWS, tints, 0, unroll=4)

    def entry_grads(block, carry):
        rows = pl.ds(block * 8, 8)
        zeroth, by_x, by_y, by_xx, by_xy, by_yy = [
            sums_ref[pl.ds(block * 8 + slot, 8, stride=40), :] for slot in range(6)
        ]
        x, y, a, b, c = [entries_ref[slot, rows, :] for slot in range(5)]
        off_x = by_x - x * zeroth
        off_y = by_y - y * zeroth
        feats_ref[0, rows, :] = a * off_x + b * off_y
        feats_ref[1, rows, :] = c * off_y + b * off_x
        feats_ref[2, rows, :] = -0.5 * (by_xx - x * (by_x + off_x))
        feats_ref[3, rows, :] = x * by_y + y * off_x - by_xy
        feats_ref[4, rows, :] = -0.5 * (by_yy - y * (by_y + off_y))
        feats_ref[8, rows, :] = zeroth
        for channel in range(3):
            feats_ref[5 + channel, rows, :] = (
                tint_ref[pl.ds(block * 128 + channel * 3, 8, stride=16), :]
                + tint_ref[pl.ds(block * 128 + channel * 3 + 1, 8, stride=16), :]
                + tint_ref[pl.ds(block * 128 + channel * 3 + 2, 8, stride=16), :]
            )
        return carry

    lax.fori_loop(0, 5, entry_grads, 0)
    values = [
        by_entry(feats_ref[5 + channel, group * 8 : group * 8 + 8, :])
        for group in range(5)
        for channel in range(3)
    ]
    for number, value in enumerate(values):
        group, channel = divmod(number, 3)
        feats_ref[5 + channel, group * 8 : group * 8 + 8, :] = value

    def gather_block(block, carry):
        place = place_ref[pl.ds(block * 8, 8), :]
        tile = place >> 7
        entry = place & 127
        high = (tile & 56) | (entry >> 4)
        low = ((entry & 15) << 3) | (tile & 7)
        got = [jnp.zeros((8, 128), F32)] * FEATS
        for row in range(ROWS):
            same = high == row
            for feature in range(FEATS):
                value = pick(feats_ref[feature, row : row + 1, :], low)
                got[feature] = jnp.where(same, value, got[feature])
        for feature in range(FEATS):
            put_feature(table_ref, block, feature, got[feature])
        return carry

    lax.fori_loop(0, 5, gather_block, 0)
    expand_feats(table_ref, count_ref, out_ref, strips, lambda number: number * 6)


def pull_kernel(focal, centre_x, centre_y):
    def kernel(
        camera_ref, count_ref, spot_ref, params_ref, place_ref, chunks_ref, out_ref,
        table_ref, wide_ref, local_ref, grads_ref, sems, out_sems,
    ):
        copies = fetch_params(params_ref, local_ref, sems)
        strips = chunks_ref.shape[0] // 6
        wide_ref[0 : strips * 6, :] = chunks_ref[...]
        compact_feats(
            wide_ref,
            lambda number, chunk: count_ref[number],
            table_ref,
            strips,
            lambda number: spot_ref[number],
        )
        bounds = run_bounds(count_ref, strips)

        def block_grads(block, carry):
            rows = pl.ds(block * 8, 8)
            place = place_ref[rows, :]
            high = place >> 7
            low = place & 127
            got = [jnp.zeros((8, 128), F32)] * FEATS
            for row in range(ROWS):
                same = high == row
                for feature in range(FEATS):
                    value = pick(table_line(table_ref, row, feature), low)
                    got[feature] = jnp.where(same, value, got[feature])
            camera = select_camera(camera_ref, place, bounds)
            params = [
                local_ref[pl.ds(block * 512 + number, 8, stride=64), :] for number in range(59)
            ]
            ignored, pull = jax.vjp(
                lambda values: project(values, camera, focal, centre_x, centre_y), params
            )
            for number, grad in enumerate(pull(got[:8])[0]):
                if number == 10:
                    grad = got[8] / (1.0 + jnp.exp(params[10]))
                grads_ref[pl.ds(block * 512 + number, 8, stride=64), :] = grad
            for tile in range(8):
                result(block * 8 + tile).start()
            return carry

        def result(tile):
            return pltpu.make_async_copy(
                grads_ref.at[pl.ds(pl.multiple_of(tile * 64, 64), 59), :],
                out_ref.at[:, pl.ds(pl.multiple_of(tile * 128, 128), 128)],
                out_sems.at[tile],
            )

        for copy in copies:
            copy.wait()
        lax.fori_loop(0, 5, block_grads, 0)
        for tile in range(ROWS):
            result(tile).wait()

    return kernel


def shape(*dims, dtype=F32):
    return jax.ShapeDtypeStruct(dims, dtype)


def device_of(strip):
    core = strip & 1
    z, y, x = (strip >> 1) & 3, (strip >> 3) & 3, strip >> 5
    z = z + (y & 1) * (3 - 2 * z)
    y = y + (x & 1) * (3 - 2 * y)
    return ((x * 4 + y) * 4 + z) * 2 + core


def strip_of(device):
    core = device & 1
    z, y, x = (device >> 1) & 3, (device >> 3) & 3, device >> 5
    y = y + (x & 1) * (3 - 2 * y)
    z = z + (y & 1) * (3 - 2 * z)
    return ((x * 4 + y) * 4 + z) * 2 + core


def position_of(strips):
    return lax.rem(strip_of(lax.axis_index("strip")) + strips // VIEWS // 2, strips)


def keeps(strips):
    per_view = strips // VIEWS
    place = lax.rem(position_of(strips), per_view)
    return (place != 0).astype(F32), (place != per_view - 1).astype(F32)


def exchange(chunks, strips):
    sent = chunks.reshape(strips, 1, 768)
    got = lax.all_to_all(sent, "strip", split_axis=0, concat_axis=0, tiled=True)
    return got.reshape(strips * 6, 128)


def per_device(params, camera, send_index, send_count, tile_list, target):
    strips = lax.axis_size("strip")
    per_view = strips // VIEWS
    rows_strip = target.shape[1]
    width = target.shape[2]
    focal = 0.5 * width
    centre_y = 0.5 * rows_strip * per_view
    spots = [device_of(strip) for strip in range(strips)]
    spot_rows = jnp.asarray(np.array(spots, np.int32) * 6)
    ahead = [(spots[i], spots[(i + 1) % strips]) for i in range(strips)]
    behind = [(spots[(i + 1) % strips], spots[i]) for i in range(strips)]

    chunks, place, pack = pl.pallas_call(
        owner_kernel(focal, 0.5 * width, centre_y),
        out_shape=(
            shape(strips * 6, 128), shape(ROWS, 128, dtype=jnp.int32), shape(280, 128)
        ),
        in_specs=[SMEM, SMEM, SMEM, ANY, VMEM, VMEM, VMEM],
        scratch_shapes=[
            pltpu.VMEM((strips, 128), jnp.int32),
            pltpu.VMEM((ROWS + 8, 128), jnp.int32),
            pltpu.VMEM((FEATS, ROWS, 128), F32),
            pltpu.VMEM(((ROWS + 2) * 16, 128), F32),
            pltpu.VMEM((ROWS * 64, 128), F32),
            pltpu.SemaphoreType.DMA((ROWS,)),
        ],
        name="owner",
    )(camera, send_count, spot_rows, params, send_index.T, target, tile_list)
    arrived = exchange(chunks, strips)
    moved = lax.ppermute(pack, "strip", list(enumerate(spots)))

    listed = pl.pallas_call(
        invert_kernel,
        out_shape=shape(ROWS, 128, dtype=jnp.int32),
        scratch_shapes=[pltpu.VMEM((ROWS, 128), jnp.int32)],
        name="listed",
    )(moved)
    rows = entry_basis()
    basis = np.zeros((24, 256), np.float32)
    basis[0:18] = np.repeat(rows, 3, axis=0)
    moment = np.zeros((16, 256), np.float32)
    moment[0:6] = rows
    basis = jnp.asarray(basis, BF16)
    moment = jnp.asarray(moment, BF16)
    image, first, last, entries, colour, counts, alphas, weights = pl.pallas_call(
        render_kernel,
        out_shape=(
            shape(3, 5, 16, 128),
            shape(300, 128),
            shape(300, 128),
            shape(5, ROWS, 128),
            shape(3, ROWS, 128),
            shape(strips, dtype=jnp.int32),
            shape(2, 5120, 128),
            shape(2, 5120, 128),
        ),
        in_specs=[VMEM, VMEM, VMEM],
        out_specs=(VMEM, VMEM, VMEM, VMEM, VMEM, SMEM, ANY, ANY),
        scratch_shapes=[
            pltpu.VMEM(((ROWS + 2) * 16, 128), F32),
            pltpu.VMEM((ROWS, 128), jnp.int32),
            pltpu.VMEM((ROWS * 24, 128), F32),
            pltpu.VMEM((640, 256), F32),
            pltpu.VMEM((640, 256), F32),
            pltpu.VMEM((2, 5120, 128), F32),
            pltpu.VMEM((2, 5120, 128), F32),
            pltpu.VMEM((ROWS * 16, 128), F32),
            pltpu.VMEM((2, ROWS * 16, 128), F32),
            pltpu.SemaphoreType.DMA((32,)),
        ],
        name="render",
    )(arrived, basis, moved)
    above = lax.ppermute(last, "strip", ahead)
    below = lax.ppermute(first, "strip", behind)
    grads = pl.pallas_call(
        gradient_kernel,
        out_shape=shape(strips * 6, 128),
        in_specs=[SMEM] + [VMEM] * 8 + [ANY, ANY],
        scratch_shapes=[
            pltpu.VMEM((5, 128, 128), F32),
            pltpu.VMEM((5, 128, 128), F32),
            pltpu.VMEM((5, 128, 128), F32),
            pltpu.VMEM((5, 128, 128), F32),
            pltpu.VMEM((5, 128, 128), F32),
            pltpu.VMEM((128, 128), F32),
            pltpu.VMEM((5, 656, 128), F32),
            pltpu.VMEM((3, 656, 128), F32),
            pltpu.VMEM((2, 5120, 128), F32),
            pltpu.VMEM((2, 5120, 128), F32),
            pltpu.VMEM((640, 256), F32),
            pltpu.VMEM((640, 256), F32),
            pltpu.VMEM((30, 8, 128), F32),
            pltpu.VMEM((2, ROWS * 16, 128), F32),
            pltpu.VMEM((ROWS * 8 + 40, 128), F32),
            pltpu.VMEM((ROWS * 16, 128), F32),
            pltpu.VMEM((FEATS, ROWS, 128), F32),
            pltpu.VMEM(((ROWS + 2) * 16, 128), F32),
            pltpu.SemaphoreType.DMA((4,)),
        ],
        name="gradient",
    )(
        counts, image, above, below, moved,
        entries, colour, listed, moment, alphas, weights,
    )
    returned = exchange(grads, strips)
    return pl.pallas_call(
        pull_kernel(focal, 0.5 * width, centre_y),
        out_shape=shape(59, ROWS * 128),
        in_specs=[SMEM, SMEM, SMEM, ANY, VMEM, VMEM],
        out_specs=ANY,
        scratch_shapes=[
            pltpu.VMEM(((ROWS + 2) * 16, 128), F32),
            pltpu.VMEM((strips * 6 + 8, 128), F32),
            pltpu.VMEM((ROWS * 64, 128), F32),
            pltpu.VMEM((ROWS * 64, 128), F32),
            pltpu.SemaphoreType.DMA((ROWS,)),
            pltpu.SemaphoreType.DMA((ROWS,)),
        ],
        name="pull",
    )(camera, send_count, spot_rows, params, place, returned)


def solution(mesh):
    return jax.shard_map(
        per_device,
        mesh=mesh,
        in_specs=(
            P(None, "strip"),
            P(),
            P("strip", None),
            P("strip"),
            P("strip", None),
            P(None, "strip", None),
        ),
        out_specs=P(None, "strip"),
        check_vma=False,
    )
```

```python
import numpy as np

import jax
import jax.numpy as jnp
from jax import lax
from jax.experimental import pallas as pl
from jax.experimental.pallas import tpu as pltpu
from jax.sharding import PartitionSpec as P

VIEWS = 4
ROWS = 40
FEATS = 9
STEP = 9
LOG2E = 1.4426950408889634
harmonic_zero = 0.28209479177387814
harmonic_one = 0.4886025119029199
harmonic_two = (
    1.0925484305920792,
    -1.0925484305920792,
    0.31539156525252005,
    -1.0925484305920792,
    0.5462742152960396,
)
harmonic_three = (
    -0.5900435899266435,
    2.890611442640554,
    -0.4570457994644658,
    0.3731763325901154,
    -0.4570457994644658,
    1.445305721320277,
    -0.5900435899266435,
)
light_term = 0.0001
contrast_term = 0.0009
F32 = jnp.float32
BF16 = jnp.bfloat16
SMEM = pl.BlockSpec(memory_space=pltpu.SMEM)
VMEM = pl.BlockSpec(memory_space=pltpu.VMEM)
ANY = pl.BlockSpec(memory_space=pl.ANY)


def iota(shape, axis):
    return lax.broadcasted_iota(jnp.int32, shape, axis)


def dot_nt(a, b):
    return lax.dot_general(a, b, (((1,), (1,)), ((), ())), preferred_element_type=F32)


def rounded(x):
    return x.astype(BF16).astype(F32)


def pick(row, lanes):
    return jnp.take_along_axis(
        jnp.broadcast_to(row, lanes.shape), lanes, axis=1, mode="promise_in_bounds"
    )


def harmonics(along_x, along_y, along_z):
    square_x = along_x * along_x
    square_y = along_y * along_y
    square_z = along_z * along_z
    return [
        harmonic_zero + 0.0 * along_x,
        -harmonic_one * along_y,
        harmonic_one * along_z,
        -harmonic_one * along_x,
        harmonic_two[0] * along_x * along_y,
        harmonic_two[1] * along_y * along_z,
        harmonic_two[2] * (2.0 * square_z - square_x - square_y),
        harmonic_two[3] * along_x * along_z,
        harmonic_two[4] * (square_x - square_y),
        harmonic_three[0] * along_y * (3.0 * square_x - square_y),
        harmonic_three[1] * along_x * along_y * along_z,
        harmonic_three[2] * along_y * (4.0 * square_z - square_x - square_y),
        harmonic_three[3] * along_z * (2.0 * square_z - 3.0 * square_x - 3.0 * square_y),
        harmonic_three[4] * along_x * (4.0 * square_z - square_x - square_y),
        harmonic_three[5] * along_z * (square_x - square_y),
        harmonic_three[6] * along_x * (square_x - 3.0 * square_y),
    ]


def project(params, camera, focal, centre_x, centre_y):
    rotation = [[camera[3 * row + col] for col in range(3)] for row in range(3)]
    mean = [params[axis] for axis in range(3)]
    placed = [
        rotation[row][0] * mean[0]
        + rotation[row][1] * mean[1]
        + rotation[row][2] * mean[2]
        + camera[9 + row]
        for row in range(3)
    ]
    depth = placed[2]
    inverse = 1.0 / depth
    screen_x = focal * placed[0] * inverse + centre_x
    screen_y = focal * placed[1] * inverse + centre_y
    quaternion = params[6:10]
    scale = lax.rsqrt(
        quaternion[0] * quaternion[0]
        + quaternion[1] * quaternion[1]
        + quaternion[2] * quaternion[2]
        + quaternion[3] * quaternion[3]
    )
    real, imag_x, imag_y, imag_z = [part * scale for part in quaternion]
    turn = [
        [
            1.0 - 2.0 * (imag_y * imag_y + imag_z * imag_z),
            2.0 * (imag_x * imag_y - real * imag_z),
            2.0 * (imag_x * imag_z + real * imag_y),
        ],
        [
            2.0 * (imag_x * imag_y + real * imag_z),
            1.0 - 2.0 * (imag_x * imag_x + imag_z * imag_z),
            2.0 * (imag_y * imag_z - real * imag_x),
        ],
        [
            2.0 * (imag_x * imag_z - real * imag_y),
            2.0 * (imag_y * imag_z + real * imag_x),
            1.0 - 2.0 * (imag_x * imag_x + imag_y * imag_y),
        ],
    ]
    scales = [jnp.exp(part) for part in params[3:6]]
    near = focal * inverse
    slant = [-near * placed[0] * inverse, -near * placed[1] * inverse]
    facing = [
        [near * rotation[row][col] + slant[row] * rotation[2][col] for col in range(3)]
        for row in range(2)
    ]
    stretch = [
        [
            (
                facing[row][0] * turn[0][col]
                + facing[row][1] * turn[1][col]
                + facing[row][2] * turn[2][col]
            )
            * scales[col]
            for col in range(3)
        ]
        for row in range(2)
    ]
    cov_xx = (
        stretch[0][0] * stretch[0][0]
        + stretch[0][1] * stretch[0][1]
        + stretch[0][2] * stretch[0][2]
        + 0.3
    )
    cov_xy = (
        stretch[0][0] * stretch[1][0]
        + stretch[0][1] * stretch[1][1]
        + stretch[0][2] * stretch[1][2]
    )
    cov_yy = (
        stretch[1][0] * stretch[1][0]
        + stretch[1][1] * stretch[1][1]
        + stretch[1][2] * stretch[1][2]
        + 0.3
    )
    over = 1.0 / (cov_xx * cov_yy - cov_xy * cov_xy)
    shrink = 1.0 / jnp.sqrt(placed[0] * placed[0] + placed[1] * placed[1] + depth * depth)
    heading = [
        (
            rotation[0][col] * placed[0]
            + rotation[1][col] * placed[1]
            + rotation[2][col] * placed[2]
        )
        * shrink
        for col in range(3)
    ]
    basis = harmonics(heading[0], heading[1], heading[2])
    colour = []
    for channel in range(3):
        total = 0.5 + basis[0] * params[11 + channel]
        for k in range(1, 16):
            total = total + basis[k] * params[11 + 3 * k + channel]
        colour.append(total)
    return [
        screen_x,
        screen_y,
        cov_yy * over,
        -cov_xy * over,
        cov_xx * over,
        colour[0],
        colour[1],
        colour[2],
    ]


def log_sigmoid(logit):
    return jnp.minimum(logit, 0.0) - jnp.log(1.0 + jnp.exp(-jnp.abs(logit)))


def send_views(count_ref, strips):
    per_view = strips // VIEWS
    offset = per_view // 2
    runs = []
    for strip in range(strips):
        view = (strip + offset) % strips // per_view
        if not runs or runs[-1][1] != view:
            runs.append([strip, view])
    return runs


def compact_ints(chunk_ref, count_ref, out_ref, steps, shift_ref, line_ref):
    lane = iota((1, 128), 1)

    def step(number, carry):
        start, held = carry
        live = count_ref[number]
        shift = start & 127
        row = start >> 7
        shift_ref[number] = shift
        line_ref[number] = row * 16
        chunk = pltpu.roll(chunk_ref[pl.ds(number, 1), :], shift, axis=1)
        held = jnp.where(lane >= shift, chunk, held)
        out_ref[pl.ds(row, 1), :] = held
        held = jnp.where(shift + live >= 128, chunk, held)
        return start + live, held

    lax.fori_loop(0, steps, step, (jnp.int32(0), jnp.zeros((1, 128), jnp.int32)), unroll=16)


def compact_feats(chunk_ref, place_of, table_ref, steps, spot=None):
    lane = iota((8, 128), 1)

    def step(number, carry):
        start, held, last = carry
        if spot is not None:
            chunk = chunk_ref[pl.ds(spot(number), 8), :]
        elif isinstance(number, int) and number == steps - 1:
            chunk = pltpu.roll(chunk_ref[number * 6 - 2 : number * 6 + 6, :], 6, axis=0)
        else:
            chunk = chunk_ref[pl.ds(number * 6, 8), :]
        shift, line, crossed, start = place_of(number, chunk, start)
        even = pltpu.roll(chunk, (shift + 48) & 127, axis=1)
        odd = pltpu.roll(chunk, (shift + 96) & 127, axis=1)
        chunk = pltpu.roll(chunk, shift, axis=1)
        rest = jnp.where(((lane - shift) & 127) < 48, even, pltpu.roll(odd, 7, axis=0))
        fresh = lane >= shift
        held = jnp.where(fresh, chunk, held)
        last = jnp.where(fresh, rest, last)
        base = pl.multiple_of(line, 16)
        table_ref[pl.ds(base, 8), :] = held
        table_ref[pl.ds(base + 8, 8), :] = last
        held = jnp.where(crossed, chunk, held)
        last = jnp.where(crossed, rest, last)
        return start, held, last

    zero = jnp.zeros((8, 128), F32)
    carry = lax.fori_loop(0, steps - 16, step, (jnp.int32(0), zero, zero), unroll=16)
    for number in range(steps - 16, steps):
        carry = step(number, carry)


def expand_feats(table_ref, shift_ref, line_ref, out_ref, steps, spot, count_ref=None):
    lane = iota((8, 128), 1)
    sub = iota((8, 128), 0)
    even = (sub & 1) == 0
    mark = (sub == 1) & (lane == 127)

    def step(number, carry):
        back = 128 - shift_ref[number]
        base = pl.multiple_of(line_ref[number], 16)
        here = lane < back
        main = jnp.where(
            here,
            pltpu.roll(table_ref[pl.ds(base, 8), :], back, axis=1),
            pltpu.roll(table_ref[pl.ds(base + 16, 8), :], back, axis=1),
        )
        rest = jnp.where(
            here,
            pltpu.roll(table_ref[pl.ds(base + 8, 8), :], back, axis=1),
            pltpu.roll(table_ref[pl.ds(base + 24, 8), :], back, axis=1),
        )
        tail = jnp.where(even, pltpu.roll(rest, 80, axis=1), pltpu.roll(rest, 32, axis=1))
        if count_ref is not None:
            tail = jnp.where(mark, count_ref[number].astype(F32), tail)
        out_ref[pl.ds(spot(number), 6), :] = jnp.where(lane < 80, main, tail)[0:6]
        return carry

    lax.fori_loop(0, steps, step, 0, unroll=16)


def line_of(feature):
    return feature if feature < 6 else 8 + 2 * (feature - 6)


def put_feature(table_ref, block, feature, value):
    line = line_of(feature)
    table_ref[pl.ds(block * 128 + line, 8, stride=16), :] = value
    if feature >= 6:
        table_ref[pl.ds(block * 128 + line + 1, 8, stride=16), :] = value


def table_line(table_ref, row, feature):
    line = row * 16 + line_of(feature)
    return table_ref[line : line + 1, :]


def fetch_params(params_ref, local_ref, sems):
    copies = [
        pltpu.make_async_copy(
            params_ref.at[:, pl.ds(tile * 128, 128)],
            local_ref.at[pl.ds(tile * 64, 59), :],
            sems.at[tile],
        )
        for tile in range(ROWS)
    ]
    for copy in copies:
        copy.start()
    return copies


def invert(rows_ref, out_ref):
    high = iota((ROWS, 128), 0)
    low = iota((128, 128), 0)
    lane = iota((ROWS, 128), 1).astype(F32)
    total = jnp.zeros((2 * ROWS, 128), F32)
    for pair in range(ROWS // 2):
        lefts = []
        rights = []
        for row in (2 * pair, 2 * pair + 1):
            number = rows_ref[row : row + 1, :]
            same = high == (number >> 7)
            lefts.append(
                jnp.concatenate([jnp.where(same, float(row), 0.0), jnp.where(same, lane, 0.0)], 0)
            )
            rights.append(jnp.where(low == (number & 127), 1.0, 0.0))
        total = total + dot_nt(
            jnp.concatenate(lefts, 1).astype(BF16), jnp.concatenate(rights, 1).astype(BF16)
        )
    out_ref[...] = (total[:ROWS] * 128.0 + total[ROWS:]).astype(jnp.int32)


def select_camera(camera_ref, place, run_starts):
    values = []
    for entry in range(12):
        value = jnp.full(place.shape, camera_ref[run_starts[0][1], entry], F32)
        for start, view in run_starts[1:]:
            value = jnp.where(place >= start, camera_ref[view, entry], value)
        values.append(value)
    return values


def run_bounds(count_ref, strips):
    runs = send_views(count_ref, strips)
    bounds = [(jnp.int32(0), runs[0][1])]
    for (first, _), (last, view) in zip(runs[:-1], runs[1:]):
        begin = bounds[-1][0]
        total = lax.fori_loop(
            first, last, lambda number, sum_: sum_ + count_ref[number], begin, unroll=True
        )
        bounds.append((total, view))
    return bounds


def owner_kernel(focal, centre_x, centre_y):
    def kernel(
        camera_ref, count_ref, spot_ref, params_ref, index_ref, target_ref, list_ref,
        out_ref, place_ref, pack_ref, shift_ref, line_ref,
        wide_ref, rows_ref, feats_ref, table_ref, local_ref, sems,
    ):
        copies = fetch_params(params_ref, local_ref, sems)
        for tile in range(5):
            for channel in range(3):
                at = tile * 56 + channel * 16
                pack_ref[at : at + 16, :] = target_ref[channel, :, tile * 128 : tile * 128 + 128]
            pack_ref[tile * 56 + 48 : tile * 56 + 56, :] = list_ref[
                tile * 8 : tile * 8 + 8, :
            ].astype(F32)
        strips = index_ref.shape[1]
        wide_ref[...] = jnp.concatenate(
            [index_ref[...], jnp.zeros((128 - index_ref.shape[0], strips), jnp.int32)], 0
        ).T
        compact_ints(wide_ref, count_ref, rows_ref, strips, shift_ref, line_ref)
        invert(rows_ref, place_ref)
        bounds = run_bounds(count_ref, strips)
        for copy in copies:
            copy.wait()

        def project_block(block, carry):
            rows = pl.ds(block * 8, 8)
            camera = select_camera(camera_ref, place_ref[rows, :], bounds)
            params = [
                local_ref[pl.ds(block * 512 + number, 8, stride=64), :] for number in range(59)
            ]
            feats = project(params, camera, focal, centre_x, centre_y)
            feats.append(log_sigmoid(params[10]))
            for feature in range(FEATS):
                feats_ref[feature, rows, :] = feats[feature]
            return carry

        lax.fori_loop(0, 5, project_block, 0)

        def gather_block(block, carry):
            number = rows_ref[pl.ds(block * 8, 8), :]
            high = number >> 7
            low = number & 127
            got = [jnp.zeros((8, 128), F32)] * FEATS
            for row in range(ROWS):
                same = high == row
                for feature in range(FEATS):
                    value = pick(feats_ref[feature, row : row + 1, :], low)
                    got[feature] = jnp.where(same, value, got[feature])
            for feature in range(FEATS):
                put_feature(table_ref, block, feature, got[feature])
            return carry

        lax.fori_loop(0, 5, gather_block, 0)
        expand_feats(
            table_ref, shift_ref, line_ref, out_ref, strips,
            lambda number: spot_ref[number], count_ref,
        )

    return kernel


def pixel_basis(rows, times):
    row = iota((rows, 256), 0)
    pixel = iota((rows, 256), 1)
    x = (pixel & 15).astype(F32) - 7.5
    y = (pixel >> 4).astype(F32) - 7.5
    value = jnp.where(row < 6 * times, y * y, 0.0)
    for number, term in ((5, x * y), (4, x * x), (3, y), (2, x), (1, 1.0)):
        value = jnp.where(row < number * times, term, value)
    return value.astype(BF16)


def swap_tiles(x):
    sub = iota((8, 128), 0)
    group = iota((8, 128), 1) >> 4
    for k in (1, 2, 4):
        up = pltpu.roll(pltpu.roll(x, 8 - k, axis=0), 16 * k, axis=1)
        down = pltpu.roll(pltpu.roll(x, k, axis=0), 128 - 16 * k, axis=1)
        s = (sub & k) != 0
        g = (group & k) != 0
        x = jnp.where(s == g, x, jnp.where(g, up, down))
    return x


def coarse_fine(x):
    coarse = x.astype(BF16)
    return coarse, (x - coarse.astype(F32)).astype(BF16)


def by_entry(x):
    lane = iota((8, 128), 1)
    order = ((lane & 7) << 4) | (lane >> 3)
    return jnp.take_along_axis(swap_tiles(x), order, axis=1, mode="promise_in_bounds")


def by_tile(x):
    lane = iota((8, 128), 1)
    order = ((lane & 15) << 3) | (lane >> 4)
    return swap_tiles(jnp.take_along_axis(x, order, axis=1, mode="promise_in_bounds"))


def tile_rows(ref, half, tile):
    base = (tile >> 3) * (16 * STEP) + (tile & 7)
    return jnp.concatenate(
        [ref[half, pl.ds(base + turn * (80 * STEP), 16, stride=STEP), :] for turn in range(8)], 0
    )


def turned_colours(colour_ref, turn, group):
    return [
        pltpu.roll(
            colour_ref[channel, group * 8 : group * 8 + 8, :], 128 - turn * 16 & 127, axis=1
        )
        for channel in range(3)
    ]


def lit(turned, entry):
    return [jnp.broadcast_to(part[:, entry : entry + 1], (8, 128)) for part in turned]


def render_kernel(
    chunks_ref, moved_ref,
    image_ref, first_ref, last_ref, entries_ref, colour_ref, shift_ref, line_ref,
    alpha_ref, weight_ref,
    table_ref, order_ref, lines_ref, power_a, power_b, tint_ref, shown_ref,
):
    for tile in range(5):
        for channel in range(3):
            at = 150 + (channel * 5 + tile) * 10
            base = tile * 56 + channel * 16
            first_ref[at : at + 10, :] = moved_ref[base : base + 10, :]
            last_ref[at : at + 10, :] = moved_ref[base + 6 : base + 16, :]
    strips = chunks_ref.shape[0] // 6

    def place_of(number, chunk, start):
        live = chunk[1, 127].astype(jnp.int32)
        shift = start & 127
        line = (start >> 7) * 16
        shift_ref[number] = shift
        line_ref[number] = line
        return shift, line, shift + live >= 128, start + live

    compact_feats(chunks_ref, place_of, table_ref, strips)
    per_view = strips // VIEWS
    top = (lax.rem(position_of(strips), per_view) * 16 + 8).astype(F32)
    for group in range(5):
        rows = slice(group * 8, group * 8 + 8)
        order_ref[rows, :] = by_entry(moved_ref[group * 56 + 48 : group * 56 + 56, :]).astype(
            jnp.int32
        )

    def entry_block(block, carry):
        rows = pl.ds(block * 8, 8)
        number = order_ref[rows, :]
        high = number >> 7
        low = number & 127
        got = [jnp.zeros((8, 128), F32)] * FEATS
        for row in range(ROWS):
            same = high == row
            for feature in range(FEATS):
                value = pick(table_line(table_ref, row, feature), low)
                got[feature] = jnp.where(same, value, got[feature])
        across = (block * 8 + (iota((8, 128), 1) & 7)) * 16 + 8
        x = got[0] - across.astype(F32)
        y = got[1] - top
        a, b, c = got[2:5]
        for slot, value in enumerate((x, y, a, b, c)):
            entries_ref[slot, rows, :] = value
        terms = [
            got[8] - 0.5 * (a * x * x + c * y * y) - b * x * y,
            a * x + b * y,
            c * y + b * x,
            -0.5 * a,
            -b,
            -0.5 * c,
        ]
        for slot, term in enumerate(terms):
            term = term * LOG2E
            for part in range(3):
                piece = rounded(term)
                lines_ref[pl.ds(block * 24 + slot * 3 + part, 8, stride=120), :] = piece
                term = term - piece
        for slot in range(18, 24):
            lines_ref[pl.ds(block * 24 + slot, 8, stride=120), :] = jnp.zeros((8, 128), F32)
        for channel in range(3):
            colour_ref[channel, rows, :] = got[5 + channel]
        return carry

    lax.fori_loop(0, 5, entry_block, 0)
    values = [
        by_tile(colour_ref[channel, group * 8 : group * 8 + 8, :])
        for group in range(5)
        for channel in range(3)
    ]
    for number, value in enumerate(values):
        group, channel = divmod(number, 3)
        colour_ref[channel, group * 8 : group * 8 + 8, :] = value
        for part in range(3):
            piece = rounded(value)
            tint_ref[pl.ds(group * 128 + channel * 3 + part, 8, stride=16), :] = piece
            value = value - piece
    basis = pixel_basis(24, 3)

    def powers(turn, power_ref):
        for part in range(5):
            lines = lines_ref[pl.ds(pl.multiple_of((turn * 5 + part) * 24, 8), 24), :]
            power_ref[part * 128 : part * 128 + 128, :] = jnp.dot(
                lines.T.astype(BF16), basis, preferred_element_type=F32
            )

    def scan(turn, power_ref, through):
        through = list(through)
        for entry in range(16):
            for group in range(5):
                at = group * 128 + entry * 8
                for half in range(2):
                    slot = group * 2 + half
                    alpha = jnp.exp2(power_ref[at : at + 8, half * 128 : half * 128 + 128])
                    weight = alpha * through[slot]
                    through[slot] = through[slot] - weight
                    alpha_ref[half, pl.ds(turn * 640 + at, 8), :] = alpha
                    spot = pl.ds(turn * (80 * STEP) + (group * 16 + entry) * STEP, 8)
                    weight_ref[half, spot, :] = weight
        return tuple(through)

    def blend(pair, through):
        powers(2 * pair + 1, power_b)
        through = scan(2 * pair, power_a, through)
        powers(jnp.minimum(2 * pair + 2, 7), power_a)
        through = scan(2 * pair + 1, power_b, through)
        return through

    powers(0, power_a)
    lax.fori_loop(0, 4, blend, (jnp.ones((8, 128), F32),) * 10)

    def tints(tile, carry):
        at = pl.ds(pl.multiple_of(tile * 16, 16), 16)
        tint = tint_ref[at, :].astype(BF16)
        halves = [coarse_fine(tile_rows(weight_ref, half, tile)) for half in range(2)]
        weight = jnp.concatenate(
            [jnp.concatenate([halves[0][part], halves[1][part]], 1) for part in range(2)], 0
        )
        total = jnp.dot(jnp.concatenate([tint, tint], 1), weight, preferred_element_type=F32)
        for half in range(2):
            shown_ref[half, at, :] = total[:, half * 128 : half * 128 + 128]
        return carry

    lax.fori_loop(0, ROWS, tints, 0, unroll=8)
    for group in range(5):
        for channel in range(3):
            for half in range(2):
                parts = [
                    shown_ref[half, pl.ds(group * 128 + channel * 3 + part, 8, stride=16), :]
                    for part in range(3)
                ]
                image_ref[channel, group, half * 8 : half * 8 + 8, :] = swap_tiles(
                    parts[0] + parts[1] + parts[2]
                )
            at = (channel * 5 + group) * 10
            first_ref[at : at + 10, :] = image_ref[channel, group, 0:10, :]
            last_ref[at : at + 10, :] = image_ref[channel, group, 6:16, :]


def window_weights():
    offsets = np.arange(11, dtype=np.float64) - 5.0
    raw = np.exp(-offsets * offsets / 4.5)
    return [float(value) for value in raw / raw.sum()]


WINDOW = window_weights()


def tap_sum(load):
    total = WINDOW[5] * load(5)
    for k in range(5):
        total = total + WINDOW[k] * (load(k) + load(10 - k))
    return total


def down_rows(field_ref, slot, out_ref):
    for tile in range(5):
        for channel in range(3):
            base = channel * 40
            out_ref[base : base + 32, :] = tap_sum(
                lambda k: field_ref[tile, base + k : base + k + 32, :]
            )
        yield tile, out_ref[...].T


def extend(ext_ref, own, above, below, keep_above, keep_below):
    for tile in range(5):
        for channel in range(3):
            base = channel * 40
            ext_ref[tile, base : base + 10, :] = above(channel, tile) * keep_above
            ext_ref[tile, base + 10 : base + 26, :] = own(channel, tile)
            ext_ref[tile, base + 26 : base + 36, :] = below(channel, tile) * keep_below
            ext_ref[tile, base + 36 : base + 40, :] = jnp.zeros((4, 128), F32)
        ext_ref[tile, 120:128, :] = jnp.zeros((8, 128), F32)


def clear_ends(ref, slot):
    ref[slot, 0:8, :] = jnp.zeros((8, 128), F32)
    ref[slot, 648:656, :] = jnp.zeros((8, 128), F32)


def invert_kernel(moved_ref, out_ref, rows_ref):
    for group in range(5):
        rows_ref[group * 8 : group * 8 + 8, :] = moved_ref[
            group * 56 + 48 : group * 56 + 56, :
        ].astype(jnp.int32)
    invert(rows_ref, out_ref)


def gradient_kernel(
    shift_ref, line_ref, image_ref, above_ref, below_ref, moved_ref,
    entries_ref, colour_ref, place_ref, alpha_ref, weight_ref,
    out_ref,
    ext_ref, square_ref, cross_ref, truth_ref, ideal_ref, rows_ref, cols_ref, parts_ref,
    pull_a, pull_b, light_ref, split_ref, sums_ref, tint_ref, feats_ref, table_ref,
):
    strips = out_ref.shape[0] // 6
    keep_above, keep_below = keeps(strips)
    def rim(base):
        return lambda ref: lambda channel, tile: ref[
            base + (channel * 5 + tile) * 10 : base + (channel * 5 + tile) * 10 + 10, :
        ]

    extend(
        ext_ref,
        lambda channel, tile: image_ref[channel, tile],
        rim(0)(above_ref),
        rim(0)(below_ref),
        keep_above,
        keep_below,
    )
    extend(
        truth_ref,
        lambda channel, tile: moved_ref[tile * 56 + channel * 16 : tile * 56 + channel * 16 + 16, :],
        rim(150)(above_ref),
        rim(150)(below_ref),
        keep_above,
        keep_below,
    )
    for tile in range(5):
        square_ref[tile] = ext_ref[tile] * ext_ref[tile]
        cross_ref[tile] = ext_ref[tile] * truth_ref[tile]
        ideal_ref[tile] = truth_ref[tile] * truth_ref[tile]
    rows_ref[...] = jnp.zeros((128, 128), F32)
    for slot in range(3):
        clear_ends(parts_ref, slot)
    for slot, source in enumerate((ext_ref, square_ref, cross_ref, truth_ref, ideal_ref)):
        clear_ends(cols_ref, slot)
        for tile, turned in down_rows(source, slot, rows_ref):
            cols_ref[slot, 8 + tile * 128 : 136 + tile * 128, :] = turned
    lane = iota((8, 128), 1)
    row = lane - jnp.where(lane >= 80, 80, jnp.where(lane >= 40, 40, 0))
    live = jnp.where(row < 5, keep_above, jnp.where(row >= 21, keep_below, 1.0))
    live = jnp.where((row < 26) & (lane < 120), live, 0.0)[0:1, :]

    def similarity(step, carry):
        base = step * 32
        mean_x, power_x, cross, mean_y, power_y = [
            tap_sum(lambda k: cols_ref[slot, pl.ds(base + 3 + k, 32), :]) for slot in range(5)
        ]
        both = mean_x * mean_y
        squares = mean_x * mean_x + mean_y * mean_y
        light_up = 2.0 * both + light_term
        light_down = squares + light_term
        sharp_up = 2.0 * (cross - both) + contrast_term
        sharp_down = power_x + power_y - squares + contrast_term
        over = 1.0 / (light_down * sharp_down)
        score = light_up * sharp_up * over
        scale = live * over
        cross_grad = -2.0 * light_up * scale
        power_grad = score * light_down * scale
        mean_grad = (
            -2.0 * mean_y * (sharp_up - light_up) + 2.0 * mean_x * score * (sharp_down - light_down)
        ) * scale
        at = pl.ds(base + 8, 32)
        parts_ref[0, at, :] = mean_grad
        parts_ref[1, at, :] = power_grad
        parts_ref[2, at, :] = cross_grad
        return carry

    lax.fori_loop(0, 20, similarity, 0)
    for tile in range(5):
        for slot in range(3):
            turned = tap_sum(
                lambda k: parts_ref[slot, tile * 128 + 3 + k : tile * 128 + 131 + k, :]
            ).T
            (square_ref, cross_ref, cols_ref)[slot][0, 0:128, :] = turned
        for channel in range(3):
            base = channel * 40
            down = [
                tap_sum(lambda k: (square_ref, cross_ref, cols_ref)[slot][0, base + k : base + k + 16, :])
                for slot in range(3)
            ]
            own = image_ref[channel, tile]
            truth = truth_ref[tile, base + 10 : base + 26, :]
            pull = down[0] + 2.0 * own * down[1] + truth * down[2]
            for half in range(2):
                value = swap_tiles(pull[half * 8 : half * 8 + 8])
                light_ref[tile * 6 + half * 3 + channel] = value
                for part in range(3):
                    piece = rounded(value)
                    split_ref[half, pl.ds(tile * 128 + channel * 3 + part, 8, stride=16), :] = piece
                    value = value - piece
    moments = pixel_basis(16, 1)

    def scan(turn, pull_ref, behind):
        behind = list(behind)
        turned = [
            [
                pltpu.roll(
                    colour_ref[channel, group * 8 : group * 8 + 8, :], 128 - turn * 16 & 127, axis=1
                )
                for channel in range(3)
            ]
            for group in range(5)
        ]
        for entry in range(15, -1, -1):
            for group in range(5):
                at = group * 128 + entry * 8
                rows = pl.ds(turn * 640 + at, 8)
                spot = pl.ds(turn * (80 * STEP) + (group * 16 + entry) * STEP, 8)
                colour = [
                    jnp.broadcast_to(turned[group][channel][:, entry : entry + 1], (8, 128))
                    for channel in range(3)
                ]
                for half in range(2):
                    slot = group * 2 + half
                    light = group * 6 + half * 3
                    value = (
                        colour[0] * light_ref[light]
                        + colour[1] * light_ref[light + 1]
                        + colour[2] * light_ref[light + 2]
                    )
                    delta = value - behind[slot]
                    behind[slot] = behind[slot] + alpha_ref[half, rows, :] * delta
                    pull_ref[at : at + 8, half * 128 : half * 128 + 128] = (
                        weight_ref[half, spot, :] * delta
                    )
        return tuple(behind)

    def reduce(turn, pull_ref):
        for part in range(5):
            coarse, fine = coarse_fine(pull_ref[part * 128 : part * 128 + 128, :])
            total = dot_nt(moments, coarse) + dot_nt(moments, fine)
            sums_ref[pl.ds(pl.multiple_of((turn * 5 + part) * 8, 8), 8), :] = total[0:8]

    def backward(count, behind):
        turn = 7 - 2 * count
        reduce(turn + 1, pull_b)
        behind = scan(turn, pull_a, behind)
        reduce(turn, pull_a)
        return scan(turn - 1, pull_b, behind)

    pull_b[...] = jnp.zeros((640, 256), F32)
    lax.fori_loop(0, 4, backward, (jnp.zeros((8, 128), F32),) * 10)
    reduce(0, pull_b)

    def tints(tile, carry):
        at = pl.ds(pl.multiple_of(tile * 16, 16), 16)
        halves = [coarse_fine(tile_rows(weight_ref, half, tile)) for half in range(2)]
        weight = jnp.concatenate(
            [jnp.concatenate([halves[0][part], halves[1][part]], 1) for part in range(2)], 0
        )
        light = jnp.concatenate([split_ref[half, at, :].astype(BF16) for half in range(2)], 1)
        total = dot_nt(light, weight)
        total = total[:, 0:128] + total[:, 128:256]
        tint_ref[at, :] = total
        return carry

    lax.fori_loop(0, ROWS, tints, 0, unroll=8)

    def entry_grads(block, carry):
        rows = pl.ds(block * 8, 8)
        zeroth, by_x, by_y, by_xx, by_xy, by_yy = [
            sums_ref[pl.ds(block * 8 + slot, 8, stride=40), :] for slot in range(6)
        ]
        x, y, a, b, c = [entries_ref[slot, rows, :] for slot in range(5)]
        off_x = by_x - x * zeroth
        off_y = by_y - y * zeroth
        feats_ref[0, rows, :] = a * off_x + b * off_y
        feats_ref[1, rows, :] = c * off_y + b * off_x
        feats_ref[2, rows, :] = -0.5 * (by_xx - x * (by_x + off_x))
        feats_ref[3, rows, :] = x * by_y + y * off_x - by_xy
        feats_ref[4, rows, :] = -0.5 * (by_yy - y * (by_y + off_y))
        feats_ref[8, rows, :] = zeroth
        for channel in range(3):
            feats_ref[5 + channel, rows, :] = (
                tint_ref[pl.ds(block * 128 + channel * 3, 8, stride=16), :]
                + tint_ref[pl.ds(block * 128 + channel * 3 + 1, 8, stride=16), :]
                + tint_ref[pl.ds(block * 128 + channel * 3 + 2, 8, stride=16), :]
            )
        return carry

    lax.fori_loop(0, 5, entry_grads, 0)
    values = [
        by_entry(feats_ref[5 + channel, group * 8 : group * 8 + 8, :])
        for group in range(5)
        for channel in range(3)
    ]
    for number, value in enumerate(values):
        group, channel = divmod(number, 3)
        feats_ref[5 + channel, group * 8 : group * 8 + 8, :] = value

    def gather_block(block, carry):
        place = place_ref[pl.ds(block * 8, 8), :]
        tile = place >> 7
        entry = place & 127
        high = (tile & 56) | (entry >> 4)
        low = ((entry & 15) << 3) | (tile & 7)
        got = [jnp.zeros((8, 128), F32)] * FEATS
        for row in range(ROWS):
            same = high == row
            for feature in range(FEATS):
                value = pick(feats_ref[feature, row : row + 1, :], low)
                got[feature] = jnp.where(same, value, got[feature])
        for feature in range(FEATS):
            put_feature(table_ref, block, feature, got[feature])
        return carry

    lax.fori_loop(0, 5, gather_block, 0)
    expand_feats(table_ref, shift_ref, line_ref, out_ref, strips, lambda number: number * 6)


def pull_kernel(focal, centre_x, centre_y):
    def kernel(
        camera_ref, count_ref, spot_ref, shift_ref, line_ref, params_ref, place_ref, chunks_ref,
        out_ref,
        table_ref, wide_ref, local_ref, grads_ref, sems, out_sems,
    ):
        copies = fetch_params(params_ref, local_ref, sems)
        strips = chunks_ref.shape[0] // 6
        wide_ref[0 : strips * 6, :] = chunks_ref[...]
        compact_feats(
            wide_ref,
            lambda number, chunk, start: (
                shift_ref[number],
                line_ref[number],
                shift_ref[number] + count_ref[number] >= 128,
                start,
            ),
            table_ref,
            strips,
            lambda number: spot_ref[number],
        )
        bounds = run_bounds(count_ref, strips)

        def block_grads(block, carry):
            rows = pl.ds(block * 8, 8)
            place = place_ref[rows, :]
            high = place >> 7
            low = place & 127
            got = [jnp.zeros((8, 128), F32)] * FEATS
            for row in range(ROWS):
                same = high == row
                for feature in range(FEATS):
                    value = pick(table_line(table_ref, row, feature), low)
                    got[feature] = jnp.where(same, value, got[feature])
            camera = select_camera(camera_ref, place, bounds)
            params = [
                local_ref[pl.ds(block * 512 + number, 8, stride=64), :] for number in range(59)
            ]
            ignored, pull = jax.vjp(
                lambda values: project(values, camera, focal, centre_x, centre_y), params
            )
            for number, grad in enumerate(pull(got[:8])[0]):
                if number == 10:
                    grad = got[8] / (1.0 + jnp.exp(params[10]))
                grads_ref[pl.ds(block * 512 + number, 8, stride=64), :] = grad
            for tile in range(8):
                result(block * 8 + tile).start()
            return carry

        def result(tile):
            return pltpu.make_async_copy(
                grads_ref.at[pl.ds(pl.multiple_of(tile * 64, 64), 59), :],
                out_ref.at[:, pl.ds(pl.multiple_of(tile * 128, 128), 128)],
                out_sems.at[tile],
            )

        for copy in copies:
            copy.wait()
        lax.fori_loop(0, 5, block_grads, 0)
        for tile in range(ROWS):
            result(tile).wait()

    return kernel


def shape(*dims, dtype=F32):
    return jax.ShapeDtypeStruct(dims, dtype)


def device_of(strip):
    core = strip & 1
    z, y, x = (strip >> 1) & 3, (strip >> 3) & 3, strip >> 5
    z = z + (y & 1) * (3 - 2 * z)
    y = y + (x & 1) * (3 - 2 * y)
    return ((x * 4 + y) * 4 + z) * 2 + core


def strip_of(device):
    core = device & 1
    z, y, x = (device >> 1) & 3, (device >> 3) & 3, device >> 5
    y = y + (x & 1) * (3 - 2 * y)
    z = z + (y & 1) * (3 - 2 * z)
    return ((x * 4 + y) * 4 + z) * 2 + core


def position_of(strips):
    return lax.rem(strip_of(lax.axis_index("strip")) + strips // VIEWS // 2, strips)


def keeps(strips):
    per_view = strips // VIEWS
    place = lax.rem(position_of(strips), per_view)
    return (place != 0).astype(F32), (place != per_view - 1).astype(F32)


def exchange(chunks, strips):
    sent = chunks.reshape(strips, 1, 768)
    got = lax.all_to_all(sent, "strip", split_axis=0, concat_axis=0, tiled=True)
    return got.reshape(strips * 6, 128)


def per_device(params, camera, send_index, send_count, tile_list, target):
    strips = lax.axis_size("strip")
    per_view = strips // VIEWS
    rows_strip = target.shape[1]
    width = target.shape[2]
    focal = 0.5 * width
    centre_y = 0.5 * rows_strip * per_view
    spots = [device_of(strip) for strip in range(strips)]
    spot_rows = jnp.asarray(np.array(spots, np.int32) * 6)
    ahead = [(spots[i], spots[(i + 1) % strips]) for i in range(strips)]
    behind = [(spots[(i + 1) % strips], spots[i]) for i in range(strips)]

    chunks, place, pack, sent_shift, sent_line = pl.pallas_call(
        owner_kernel(focal, 0.5 * width, centre_y),
        out_shape=(
            shape(strips * 6, 128),
            shape(ROWS, 128, dtype=jnp.int32),
            shape(280, 128),
            shape(strips, dtype=jnp.int32),
            shape(strips, dtype=jnp.int32),
        ),
        out_specs=(VMEM, VMEM, VMEM, SMEM, SMEM),
        in_specs=[SMEM, SMEM, SMEM, ANY, VMEM, VMEM, VMEM],
        scratch_shapes=[
            pltpu.VMEM((strips, 128), jnp.int32),
            pltpu.VMEM((ROWS + 8, 128), jnp.int32),
            pltpu.VMEM((FEATS, ROWS, 128), F32),
            pltpu.VMEM(((ROWS + 2) * 16, 128), F32),
            pltpu.VMEM((ROWS * 64, 128), F32),
            pltpu.SemaphoreType.DMA((ROWS,)),
        ],
        name="owner",
    )(camera, send_count, spot_rows, params, send_index.T, target, tile_list)
    arrived = exchange(chunks, strips)
    moved = lax.ppermute(pack, "strip", list(enumerate(spots)))

    listed = pl.pallas_call(
        invert_kernel,
        out_shape=shape(ROWS, 128, dtype=jnp.int32),
        scratch_shapes=[pltpu.VMEM((ROWS, 128), jnp.int32)],
        compiler_params=pltpu.CompilerParams(vmem_limit_bytes=8 << 20),
        name="listed",
    )(moved)
    image, first, last, entries, colour, shifts, places, alphas, weights = pl.pallas_call(
        render_kernel,
        out_shape=(
            shape(3, 5, 16, 128),
            shape(300, 128),
            shape(300, 128),
            shape(5, ROWS, 128),
            shape(3, ROWS, 128),
            shape(strips, dtype=jnp.int32),
            shape(strips, dtype=jnp.int32),
            shape(2, 5120, 128),
            shape(2, 640 * STEP, 128),
        ),
        in_specs=[VMEM, VMEM],
        out_specs=(VMEM, VMEM, VMEM, VMEM, VMEM, SMEM, SMEM, VMEM, VMEM),
        scratch_shapes=[
            pltpu.VMEM(((ROWS + 2) * 16, 128), F32),
            pltpu.VMEM((ROWS, 128), jnp.int32),
            pltpu.VMEM((ROWS * 24, 128), F32),
            pltpu.VMEM((640, 256), F32),
            pltpu.VMEM((640, 256), F32),
            pltpu.VMEM((ROWS * 16, 128), F32),
            pltpu.VMEM((2, ROWS * 16, 128), F32),
        ],
        compiler_params=pltpu.CompilerParams(vmem_limit_bytes=24 << 20),
        name="render",
    )(arrived, moved)
    above = lax.ppermute(last, "strip", ahead)
    below = lax.ppermute(first, "strip", behind)
    grads = pl.pallas_call(
        gradient_kernel,
        out_shape=shape(strips * 6, 128),
        in_specs=[SMEM, SMEM] + [VMEM] * 9,
        scratch_shapes=[
            pltpu.VMEM((5, 128, 128), F32),
            pltpu.VMEM((5, 128, 128), F32),
            pltpu.VMEM((5, 128, 128), F32),
            pltpu.VMEM((5, 128, 128), F32),
            pltpu.VMEM((5, 128, 128), F32),
            pltpu.VMEM((128, 128), F32),
            pltpu.VMEM((5, 656, 128), F32),
            pltpu.VMEM((3, 656, 128), F32),
            pltpu.VMEM((640, 256), F32),
            pltpu.VMEM((640, 256), F32),
            pltpu.VMEM((30, 8, 128), F32),
            pltpu.VMEM((2, ROWS * 16, 128), F32),
            pltpu.VMEM((ROWS * 8 + 40, 128), F32),
            pltpu.VMEM((ROWS * 16, 128), F32),
            pltpu.VMEM((FEATS, ROWS, 128), F32),
            pltpu.VMEM(((ROWS + 2) * 16, 128), F32),
        ],
        compiler_params=pltpu.CompilerParams(vmem_limit_bytes=24 << 20),
        name="gradient",
    )(
        shifts, places, image, above, below, moved,
        entries, colour, listed, alphas, weights,
    )
    returned = exchange(grads, strips)
    return pl.pallas_call(
        pull_kernel(focal, 0.5 * width, centre_y),
        out_shape=shape(59, ROWS * 128),
        in_specs=[SMEM] * 5 + [ANY, VMEM, VMEM],
        out_specs=ANY,
        scratch_shapes=[
            pltpu.VMEM(((ROWS + 2) * 16, 128), F32),
            pltpu.VMEM((strips * 6 + 8, 128), F32),
            pltpu.VMEM((ROWS * 64, 128), F32),
            pltpu.VMEM((ROWS * 64, 128), F32),
            pltpu.SemaphoreType.DMA((ROWS,)),
            pltpu.SemaphoreType.DMA((ROWS,)),
        ],
        compiler_params=pltpu.CompilerParams(vmem_limit_bytes=16 << 20),
        name="pull",
    )(camera, send_count, spot_rows, sent_shift, sent_line, params, place, returned)


def solution(mesh):
    return jax.shard_map(
        per_device,
        mesh=mesh,
        in_specs=(
            P(None, "strip"),
            P(),
            P("strip", None),
            P("strip"),
            P("strip", None),
            P(None, "strip", None),
        ),
        out_specs=P(None, "strip"),
        check_vma=False,
    )
```

```python
import numpy as np

import jax
import jax.numpy as jnp
from jax import lax
from jax.experimental import pallas as pl
from jax.experimental.pallas import tpu as pltpu
from jax.sharding import PartitionSpec as P

VIEWS = 4
ROWS = 40
FEATS = 9
GAP = 24
PLACE = 72
STEP = 9
LOG2E = 1.4426950408889634
harmonic_zero = 0.28209479177387814
harmonic_one = 0.4886025119029199
harmonic_two = (
    1.0925484305920792,
    -1.0925484305920792,
    0.31539156525252005,
    -1.0925484305920792,
    0.5462742152960396,
)
harmonic_three = (
    -0.5900435899266435,
    2.890611442640554,
    -0.4570457994644658,
    0.3731763325901154,
    -0.4570457994644658,
    1.445305721320277,
    -0.5900435899266435,
)
light_term = 0.0001
contrast_term = 0.0009
F32 = jnp.float32
BF16 = jnp.bfloat16
SMEM = pl.BlockSpec(memory_space=pltpu.SMEM)
VMEM = pl.BlockSpec(memory_space=pltpu.VMEM)
ANY = pl.BlockSpec(memory_space=pl.ANY)


def iota(shape, axis):
    return lax.broadcasted_iota(jnp.int32, shape, axis)


def dot_nt(a, b):
    return lax.dot_general(a, b, (((1,), (1,)), ((), ())), preferred_element_type=F32)


def rounded(x):
    return x.astype(BF16).astype(F32)


def pick(row, lanes):
    return jnp.take_along_axis(
        jnp.broadcast_to(row, lanes.shape), lanes, axis=1, mode="promise_in_bounds"
    )


def harmonics(along_x, along_y, along_z):
    square_x = along_x * along_x
    square_y = along_y * along_y
    square_z = along_z * along_z
    return [
        harmonic_zero + 0.0 * along_x,
        -harmonic_one * along_y,
        harmonic_one * along_z,
        -harmonic_one * along_x,
        harmonic_two[0] * along_x * along_y,
        harmonic_two[1] * along_y * along_z,
        harmonic_two[2] * (2.0 * square_z - square_x - square_y),
        harmonic_two[3] * along_x * along_z,
        harmonic_two[4] * (square_x - square_y),
        harmonic_three[0] * along_y * (3.0 * square_x - square_y),
        harmonic_three[1] * along_x * along_y * along_z,
        harmonic_three[2] * along_y * (4.0 * square_z - square_x - square_y),
        harmonic_three[3] * along_z * (2.0 * square_z - 3.0 * square_x - 3.0 * square_y),
        harmonic_three[4] * along_x * (4.0 * square_z - square_x - square_y),
        harmonic_three[5] * along_z * (square_x - square_y),
        harmonic_three[6] * along_x * (square_x - 3.0 * square_y),
    ]


def project(params, camera, focal, centre_x, centre_y):
    rotation = [[camera[3 * row + col] for col in range(3)] for row in range(3)]
    mean = [params[axis] for axis in range(3)]
    placed = [
        rotation[row][0] * mean[0]
        + rotation[row][1] * mean[1]
        + rotation[row][2] * mean[2]
        + camera[9 + row]
        for row in range(3)
    ]
    depth = placed[2]
    inverse = 1.0 / depth
    screen_x = focal * placed[0] * inverse + centre_x
    screen_y = focal * placed[1] * inverse + centre_y
    quaternion = params[6:10]
    scale = lax.rsqrt(
        quaternion[0] * quaternion[0]
        + quaternion[1] * quaternion[1]
        + quaternion[2] * quaternion[2]
        + quaternion[3] * quaternion[3]
    )
    real, imag_x, imag_y, imag_z = [part * scale for part in quaternion]
    turn = [
        [
            1.0 - 2.0 * (imag_y * imag_y + imag_z * imag_z),
            2.0 * (imag_x * imag_y - real * imag_z),
            2.0 * (imag_x * imag_z + real * imag_y),
        ],
        [
            2.0 * (imag_x * imag_y + real * imag_z),
            1.0 - 2.0 * (imag_x * imag_x + imag_z * imag_z),
            2.0 * (imag_y * imag_z - real * imag_x),
        ],
        [
            2.0 * (imag_x * imag_z - real * imag_y),
            2.0 * (imag_y * imag_z + real * imag_x),
            1.0 - 2.0 * (imag_x * imag_x + imag_y * imag_y),
        ],
    ]
    scales = [jnp.exp(part) for part in params[3:6]]
    near = focal * inverse
    slant = [-near * placed[0] * inverse, -near * placed[1] * inverse]
    facing = [
        [near * rotation[row][col] + slant[row] * rotation[2][col] for col in range(3)]
        for row in range(2)
    ]
    stretch = [
        [
            (
                facing[row][0] * turn[0][col]
                + facing[row][1] * turn[1][col]
                + facing[row][2] * turn[2][col]
            )
            * scales[col]
            for col in range(3)
        ]
        for row in range(2)
    ]
    cov_xx = (
        stretch[0][0] * stretch[0][0]
        + stretch[0][1] * stretch[0][1]
        + stretch[0][2] * stretch[0][2]
        + 0.3
    )
    cov_xy = (
        stretch[0][0] * stretch[1][0]
        + stretch[0][1] * stretch[1][1]
        + stretch[0][2] * stretch[1][2]
    )
    cov_yy = (
        stretch[1][0] * stretch[1][0]
        + stretch[1][1] * stretch[1][1]
        + stretch[1][2] * stretch[1][2]
        + 0.3
    )
    over = 1.0 / (cov_xx * cov_yy - cov_xy * cov_xy)
    shrink = 1.0 / jnp.sqrt(placed[0] * placed[0] + placed[1] * placed[1] + depth * depth)
    heading = [
        (
            rotation[0][col] * placed[0]
            + rotation[1][col] * placed[1]
            + rotation[2][col] * placed[2]
        )
        * shrink
        for col in range(3)
    ]
    basis = harmonics(heading[0], heading[1], heading[2])
    colour = []
    for channel in range(3):
        total = 0.5 + basis[0] * params[11 + channel]
        for k in range(1, 16):
            total = total + basis[k] * params[11 + 3 * k + channel]
        colour.append(total)
    return [
        screen_x,
        screen_y,
        cov_yy * over,
        -cov_xy * over,
        cov_xx * over,
        colour[0],
        colour[1],
        colour[2],
    ]


def log_sigmoid(logit):
    return jnp.minimum(logit, 0.0) - jnp.log(1.0 + jnp.exp(-jnp.abs(logit)))


def send_views(count_ref, strips):
    per_view = strips // VIEWS
    offset = per_view // 2
    runs = []
    for strip in range(strips):
        view = (strip + offset) % strips // per_view
        if not runs or runs[-1][1] != view:
            runs.append([strip, view])
    return runs


def compact_ints(chunk_ref, count_ref, out_ref, steps):
    lane = iota((1, 128), 1)

    def step(number, carry):
        start, held = carry
        live = count_ref[number]
        shift = start & 127
        row = start >> 7
        chunk = pltpu.roll(chunk_ref[pl.ds(number, 1), :], shift, axis=1)
        held = jnp.where(lane >= shift, chunk, held)
        out_ref[pl.ds(row, 1), :] = held
        held = jnp.where(shift + live >= 128, chunk, held)
        return start + live, held

    lax.fori_loop(0, steps, step, (jnp.int32(0), jnp.zeros((1, 128), jnp.int32)), unroll=16)


def compact_feats(chunk_ref, place_of, table_ref, steps, spot=None):
    lane = iota((8, 128), 1)

    def step(number, carry):
        start, held, last = carry
        if spot is not None:
            chunk = chunk_ref[pl.ds(spot(number), 8), :]
        elif isinstance(number, int) and number == steps - 1:
            chunk = pltpu.roll(chunk_ref[number * 6 - 2 : number * 6 + 6, :], 6, axis=0)
        else:
            chunk = chunk_ref[pl.ds(number * 6, 8), :]
        shift, line, crossed, start = place_of(number, chunk, start)
        even = pltpu.roll(chunk, (shift + 48) & 127, axis=1)
        odd = pltpu.roll(chunk, (shift + 96) & 127, axis=1)
        chunk = pltpu.roll(chunk, shift, axis=1)
        rest = jnp.where(((lane - shift) & 127) < 48, even, pltpu.roll(odd, 7, axis=0))
        fresh = lane >= shift
        held = jnp.where(fresh, chunk, held)
        last = jnp.where(fresh, rest, last)
        base = pl.multiple_of(line, 8)
        table_ref[pl.ds(base, 8), :] = held
        table_ref[pl.ds(base + 8, 8), :] = last
        held = jnp.where(crossed, chunk, held)
        last = jnp.where(crossed, rest, last)
        return start, held, last

    zero = jnp.zeros((8, 128), F32)
    carry = lax.fori_loop(0, steps - 16, step, (jnp.int32(0), zero, zero), unroll=16)
    for number in range(steps - 16, steps):
        carry = step(number, carry)


def expand_feats(table_ref, place_of, out_ref, steps, spot, count_ref=None):
    lane = iota((8, 128), 1)
    sub = iota((8, 128), 0)
    even = (sub & 1) == 0
    mark = (sub == 1) & (lane == 127)

    def step(number, start):
        shift, line, start = place_of(number, start)
        back = 128 - shift
        base = pl.multiple_of(line, 8)
        here = lane < back
        main = jnp.where(
            here,
            pltpu.roll(table_ref[pl.ds(base, 8), :], back, axis=1),
            pltpu.roll(table_ref[pl.ds(base + GAP, 8), :], back, axis=1),
        )
        rest = jnp.where(
            here,
            pltpu.roll(table_ref[pl.ds(base + 8, 8), :], back, axis=1),
            pltpu.roll(table_ref[pl.ds(base + GAP + 8, 8), :], back, axis=1),
        )
        tail = jnp.where(even, pltpu.roll(rest, 80, axis=1), pltpu.roll(rest, 32, axis=1))
        if count_ref is not None:
            tail = jnp.where(mark, count_ref[number].astype(F32), tail)
        out_ref[pl.ds(spot(number), 6), :] = jnp.where(lane < 80, main, tail)[0:6]
        return start

    lax.fori_loop(0, steps, step, jnp.int32(0), unroll=16)


def line_of(feature):
    return feature if feature < 6 else 8 + 2 * (feature - 6)


def put_feature(table_ref, block, feature, value):
    line = line_of(feature)
    table_ref[pl.ds(block * (8 * GAP) + line, 8, stride=GAP), :] = value
    if feature >= 6:
        table_ref[pl.ds(block * (8 * GAP) + line + 1, 8, stride=GAP), :] = value


def table_line(table_ref, row, feature):
    line = row * GAP + line_of(feature)
    return table_ref[line : line + 1, :]


def fetch_params(params_ref, local_ref, sems):
    copies = [
        pltpu.make_async_copy(
            params_ref.at[:, pl.ds(tile * 128, 128)],
            local_ref.at[pl.ds(tile * PLACE, 59), :],
            sems.at[tile],
        )
        for tile in range(ROWS)
    ]
    for copy in copies:
        copy.start()
    return copies


def invert(rows_ref, out_ref):
    high = iota((ROWS, 128), 0)
    low = iota((128, 128), 0)
    lane = iota((ROWS, 128), 1).astype(F32)
    total = jnp.zeros((2 * ROWS, 128), F32)
    for pair in range(ROWS // 2):
        lefts = []
        rights = []
        for row in (2 * pair, 2 * pair + 1):
            number = rows_ref[row : row + 1, :]
            same = high == (number >> 7)
            lefts.append(
                jnp.concatenate([jnp.where(same, float(row), 0.0), jnp.where(same, lane, 0.0)], 0)
            )
            rights.append(jnp.where(low == (number & 127), 1.0, 0.0))
        total = total + dot_nt(
            jnp.concatenate(lefts, 1).astype(BF16), jnp.concatenate(rights, 1).astype(BF16)
        )
    out_ref[...] = (total[:ROWS] * 128.0 + total[ROWS:]).astype(jnp.int32)


def select_camera(camera_ref, place, run_starts):
    values = []
    for entry in range(12):
        value = jnp.full(place.shape, camera_ref[run_starts[0][1], entry], F32)
        for start, view in run_starts[1:]:
            value = jnp.where(place >= start, camera_ref[view, entry], value)
        values.append(value)
    return values


def run_bounds(count_ref, strips):
    runs = send_views(count_ref, strips)
    bounds = [(jnp.int32(0), runs[0][1])]
    for (first, _), (last, view) in zip(runs[:-1], runs[1:]):
        begin = bounds[-1][0]
        total = lax.fori_loop(
            first, last, lambda number, sum_: sum_ + count_ref[number], begin, unroll=True
        )
        bounds.append((total, view))
    return bounds


def owner_kernel(focal, centre_x, centre_y):
    def kernel(
        camera_ref, count_ref, spot_ref, params_ref, index_ref, target_ref, list_ref,
        out_ref, place_ref, pack_ref,
        wide_ref, rows_ref, feats_ref, table_ref, local_ref, sems,
    ):
        copies = fetch_params(params_ref, local_ref, sems)
        for tile in range(5):
            for channel in range(3):
                at = tile * 56 + channel * 16
                pack_ref[at : at + 16, :] = target_ref[channel, :, tile * 128 : tile * 128 + 128]
            pack_ref[tile * 56 + 48 : tile * 56 + 56, :] = list_ref[
                tile * 8 : tile * 8 + 8, :
            ].astype(F32)
        strips = index_ref.shape[1]
        wide_ref[...] = jnp.concatenate(
            [index_ref[...], jnp.zeros((128 - index_ref.shape[0], strips), jnp.int32)], 0
        ).T
        compact_ints(wide_ref, count_ref, rows_ref, strips)
        invert(rows_ref, place_ref)
        bounds = run_bounds(count_ref, strips)
        for copy in copies:
            copy.wait()

        def project_block(block, carry):
            rows = pl.ds(block * 8, 8)
            camera = select_camera(camera_ref, place_ref[rows, :], bounds)
            params = [
                local_ref[pl.ds(block * (8 * PLACE) + number, 8, stride=PLACE), :]
                for number in range(59)
            ]
            feats = project(params, camera, focal, centre_x, centre_y)
            feats.append(log_sigmoid(params[10]))
            for feature in range(FEATS):
                feats_ref[feature, rows, :] = feats[feature]
            return carry

        lax.fori_loop(0, 5, project_block, 0)

        def gather_block(block, carry):
            number = rows_ref[pl.ds(block * 8, 8), :]
            high = number >> 7
            low = number & 127
            got = [jnp.zeros((8, 128), F32)] * FEATS
            for row in range(ROWS):
                same = high == row
                for feature in range(FEATS):
                    value = pick(feats_ref[feature, row : row + 1, :], low)
                    got[feature] = jnp.where(same, value, got[feature])
            for feature in range(FEATS):
                put_feature(table_ref, block, feature, got[feature])
            return carry

        lax.fori_loop(0, 5, gather_block, 0)
        expand_feats(
            table_ref,
            lambda number, start: (start & 127, (start >> 7) * GAP, start + count_ref[number]),
            out_ref,
            strips,
            lambda number: spot_ref[number],
            count_ref,
        )

    return kernel


def pixel_basis(rows, times):
    row = iota((rows, 256), 0)
    pixel = iota((rows, 256), 1)
    x = (pixel & 15).astype(F32) - 7.5
    y = (pixel >> 4).astype(F32) - 7.5
    value = jnp.where(row < 6 * times, y * y, 0.0)
    for number, term in ((5, x * y), (4, x * x), (3, y), (2, x), (1, 1.0)):
        value = jnp.where(row < number * times, term, value)
    return value.astype(BF16)


def swap_tiles(x):
    sub = iota((8, 128), 0)
    group = iota((8, 128), 1) >> 4
    for k in (1, 2, 4):
        up = pltpu.roll(pltpu.roll(x, 8 - k, axis=0), 16 * k, axis=1)
        down = pltpu.roll(pltpu.roll(x, k, axis=0), 128 - 16 * k, axis=1)
        s = (sub & k) != 0
        g = (group & k) != 0
        x = jnp.where(s == g, x, jnp.where(g, up, down))
    return x


def coarse_fine(x):
    coarse = x.astype(BF16)
    return coarse, (x - coarse.astype(F32)).astype(BF16)


def by_entry(x):
    lane = iota((8, 128), 1)
    order = ((lane & 7) << 4) | (lane >> 3)
    return jnp.take_along_axis(swap_tiles(x), order, axis=1, mode="promise_in_bounds")


def by_tile(x):
    lane = iota((8, 128), 1)
    order = ((lane & 15) << 3) | (lane >> 4)
    return swap_tiles(jnp.take_along_axis(x, order, axis=1, mode="promise_in_bounds"))


def tile_rows(ref, half, tile):
    base = (tile >> 3) * (16 * STEP) + (tile & 7)
    return jnp.concatenate(
        [ref[half, pl.ds(base + turn * (80 * STEP), 16, stride=STEP), :] for turn in range(8)], 0
    )


def turned_colours(colour_ref, turn, group):
    return [
        pltpu.roll(
            colour_ref[channel, group * 8 : group * 8 + 8, :], 128 - turn * 16 & 127, axis=1
        )
        for channel in range(3)
    ]


def lit(turned, entry):
    return [jnp.broadcast_to(part[:, entry : entry + 1], (8, 128)) for part in turned]


def render_kernel(
    chunks_ref, moved_ref,
    image_ref, first_ref, last_ref, entries_ref, colour_ref, shift_ref, line_ref,
    alpha_ref, weight_ref,
    table_ref, order_ref, lines_ref, power_a, power_b, tint_ref, shown_ref,
):
    for tile in range(5):
        for channel in range(3):
            at = 150 + (channel * 5 + tile) * 10
            base = tile * 56 + channel * 16
            first_ref[at : at + 10, :] = moved_ref[base : base + 10, :]
            last_ref[at : at + 10, :] = moved_ref[base + 6 : base + 16, :]
    strips = chunks_ref.shape[0] // 6

    def place_of(number, chunk, start):
        live = chunk[1, 127].astype(jnp.int32)
        shift = start & 127
        line = (start >> 7) * GAP
        shift_ref[number] = shift
        line_ref[number] = line
        return shift, line, shift + live >= 128, start + live

    compact_feats(chunks_ref, place_of, table_ref, strips)
    per_view = strips // VIEWS
    top = (lax.rem(position_of(strips), per_view) * 16 + 8).astype(F32)
    for group in range(5):
        rows = slice(group * 8, group * 8 + 8)
        order_ref[rows, :] = by_entry(moved_ref[group * 56 + 48 : group * 56 + 56, :]).astype(
            jnp.int32
        )

    def entry_block(block, carry):
        rows = pl.ds(block * 8, 8)
        number = order_ref[rows, :]
        high = number >> 7
        low = number & 127
        got = [jnp.zeros((8, 128), F32)] * FEATS
        for row in range(ROWS):
            same = high == row
            for feature in range(FEATS):
                value = pick(table_line(table_ref, row, feature), low)
                got[feature] = jnp.where(same, value, got[feature])
        across = (block * 8 + (iota((8, 128), 1) & 7)) * 16 + 8
        x = got[0] - across.astype(F32)
        y = got[1] - top
        a, b, c = got[2:5]
        for slot, value in enumerate((x, y, a, b, c)):
            entries_ref[slot, rows, :] = value
        terms = [
            got[8] - 0.5 * (a * x * x + c * y * y) - b * x * y,
            a * x + b * y,
            c * y + b * x,
            -0.5 * a,
            -b,
            -0.5 * c,
        ]
        for slot, term in enumerate(terms):
            term = term * LOG2E
            for part in range(3):
                piece = rounded(term)
                lines_ref[pl.ds(block * 24 + slot * 3 + part, 8, stride=120), :] = piece
                term = term - piece
        for slot in range(18, 24):
            lines_ref[pl.ds(block * 24 + slot, 8, stride=120), :] = jnp.zeros((8, 128), F32)
        for channel in range(3):
            colour_ref[channel, rows, :] = got[5 + channel]
        return carry

    lax.fori_loop(0, 5, entry_block, 0)
    values = [
        by_tile(colour_ref[channel, group * 8 : group * 8 + 8, :])
        for group in range(5)
        for channel in range(3)
    ]
    for number, value in enumerate(values):
        group, channel = divmod(number, 3)
        colour_ref[channel, group * 8 : group * 8 + 8, :] = value
        for part in range(3):
            piece = rounded(value)
            tint_ref[pl.ds(group * (8 * GAP) + channel * 3 + part, 8, stride=GAP), :] = piece
            value = value - piece
    basis = pixel_basis(24, 3)

    def powers(turn, power_ref):
        for part in range(5):
            lines = lines_ref[pl.ds(pl.multiple_of((turn * 5 + part) * 24, 8), 24), :]
            power_ref[part * 128 : part * 128 + 128, :] = jnp.dot(
                lines.T.astype(BF16), basis, preferred_element_type=F32
            )

    def scan(turn, power_ref, through):
        through = list(through)
        for entry in range(16):
            for group in range(5):
                at = group * 128 + entry * 8
                for half in range(2):
                    slot = group * 2 + half
                    alpha = jnp.exp2(power_ref[at : at + 8, half * 128 : half * 128 + 128])
                    weight = alpha * through[slot]
                    through[slot] = through[slot] - weight
                    alpha_ref[half, pl.ds(turn * 640 + at, 8), :] = alpha
                    spot = pl.ds(turn * (80 * STEP) + (group * 16 + entry) * STEP, 8)
                    weight_ref[half, spot, :] = weight
        return tuple(through)

    def blend(pair, through):
        powers(2 * pair + 1, power_b)
        through = scan(2 * pair, power_a, through)
        powers(jnp.minimum(2 * pair + 2, 7), power_a)
        through = scan(2 * pair + 1, power_b, through)
        return through

    powers(0, power_a)
    lax.fori_loop(0, 4, blend, (jnp.ones((8, 128), F32),) * 10)

    def tints(tile, carry):
        at = pl.ds(pl.multiple_of(tile * GAP, 8), 16)
        tint = tint_ref[at, :].astype(BF16)
        halves = [coarse_fine(tile_rows(weight_ref, half, tile)) for half in range(2)]
        weight = jnp.concatenate(
            [jnp.concatenate([halves[0][part], halves[1][part]], 1) for part in range(2)], 0
        )
        total = jnp.dot(jnp.concatenate([tint, tint], 1), weight, preferred_element_type=F32)
        for half in range(2):
            shown_ref[half, at, :] = total[:, half * 128 : half * 128 + 128]
        return carry

    lax.fori_loop(0, ROWS, tints, 0, unroll=8)
    for group in range(5):
        for channel in range(3):
            for half in range(2):
                parts = [
                    shown_ref[half, pl.ds(group * (8 * GAP) + channel * 3 + part, 8, stride=GAP), :]
                    for part in range(3)
                ]
                image_ref[channel, group, half * 8 : half * 8 + 8, :] = swap_tiles(
                    parts[0] + parts[1] + parts[2]
                )
            at = (channel * 5 + group) * 10
            first_ref[at : at + 10, :] = image_ref[channel, group, 0:10, :]
            last_ref[at : at + 10, :] = image_ref[channel, group, 6:16, :]


def window_weights():
    offsets = np.arange(11, dtype=np.float64) - 5.0
    raw = np.exp(-offsets * offsets / 4.5)
    return [float(value) for value in raw / raw.sum()]


WINDOW = window_weights()


def tap_sum(load):
    total = WINDOW[5] * load(5)
    for k in range(5):
        total = total + WINDOW[k] * (load(k) + load(10 - k))
    return total


def down_rows(field_ref, slot, out_ref):
    for tile in range(5):
        for channel in range(3):
            base = channel * 40
            out_ref[base : base + 32, :] = tap_sum(
                lambda k: field_ref[tile, base + k : base + k + 32, :]
            )
        yield tile, out_ref[...].T


def extend(ext_ref, own, above, below, keep_above, keep_below):
    for tile in range(5):
        for channel in range(3):
            base = channel * 40
            ext_ref[tile, base : base + 10, :] = above(channel, tile) * keep_above
            ext_ref[tile, base + 10 : base + 26, :] = own(channel, tile)
            ext_ref[tile, base + 26 : base + 36, :] = below(channel, tile) * keep_below
            ext_ref[tile, base + 36 : base + 40, :] = jnp.zeros((4, 128), F32)
        ext_ref[tile, 120:128, :] = jnp.zeros((8, 128), F32)


def clear_ends(ref, slot):
    ref[slot, 0:8, :] = jnp.zeros((8, 128), F32)
    ref[slot, 648:656, :] = jnp.zeros((8, 128), F32)


def invert_kernel(moved_ref, out_ref, rows_ref):
    for group in range(5):
        rows_ref[group * 8 : group * 8 + 8, :] = moved_ref[
            group * 56 + 48 : group * 56 + 56, :
        ].astype(jnp.int32)
    invert(rows_ref, out_ref)


def gradient_kernel(
    shift_ref, line_ref, image_ref, above_ref, below_ref, moved_ref,
    entries_ref, colour_ref, place_ref, alpha_ref, weight_ref,
    out_ref,
    ext_ref, square_ref, cross_ref, truth_ref, ideal_ref, rows_ref, cols_ref, parts_ref,
    pull_a, pull_b, light_ref, split_ref, sums_ref, tint_ref, feats_ref, table_ref,
):
    strips = out_ref.shape[0] // 6
    keep_above, keep_below = keeps(strips)
    def rim(base):
        return lambda ref: lambda channel, tile: ref[
            base + (channel * 5 + tile) * 10 : base + (channel * 5 + tile) * 10 + 10, :
        ]

    extend(
        ext_ref,
        lambda channel, tile: image_ref[channel, tile],
        rim(0)(above_ref),
        rim(0)(below_ref),
        keep_above,
        keep_below,
    )
    extend(
        truth_ref,
        lambda channel, tile: moved_ref[tile * 56 + channel * 16 : tile * 56 + channel * 16 + 16, :],
        rim(150)(above_ref),
        rim(150)(below_ref),
        keep_above,
        keep_below,
    )
    for tile in range(5):
        square_ref[tile] = ext_ref[tile] * ext_ref[tile]
        cross_ref[tile] = ext_ref[tile] * truth_ref[tile]
        ideal_ref[tile] = truth_ref[tile] * truth_ref[tile]
    rows_ref[...] = jnp.zeros((128, 128), F32)
    for slot in range(3):
        clear_ends(parts_ref, slot)
    for slot, source in enumerate((ext_ref, square_ref, cross_ref, truth_ref, ideal_ref)):
        clear_ends(cols_ref, slot)
        for tile, turned in down_rows(source, slot, rows_ref):
            cols_ref[slot, 8 + tile * 128 : 136 + tile * 128, :] = turned
    lane = iota((8, 128), 1)
    row = lane - jnp.where(lane >= 80, 80, jnp.where(lane >= 40, 40, 0))
    live = jnp.where(row < 5, keep_above, jnp.where(row >= 21, keep_below, 1.0))
    live = jnp.where((row < 26) & (lane < 120), live, 0.0)[0:1, :]

    def similarity(step, carry):
        base = step * 32
        mean_x, power_x, cross, mean_y, power_y = [
            tap_sum(lambda k: cols_ref[slot, pl.ds(base + 3 + k, 32), :]) for slot in range(5)
        ]
        both = mean_x * mean_y
        squares = mean_x * mean_x + mean_y * mean_y
        light_up = 2.0 * both + light_term
        light_down = squares + light_term
        sharp_up = 2.0 * (cross - both) + contrast_term
        sharp_down = power_x + power_y - squares + contrast_term
        over = 1.0 / (light_down * sharp_down)
        score = light_up * sharp_up * over
        scale = live * over
        cross_grad = -2.0 * light_up * scale
        power_grad = score * light_down * scale
        mean_grad = (
            -2.0 * mean_y * (sharp_up - light_up) + 2.0 * mean_x * score * (sharp_down - light_down)
        ) * scale
        at = pl.ds(base + 8, 32)
        parts_ref[0, at, :] = mean_grad
        parts_ref[1, at, :] = power_grad
        parts_ref[2, at, :] = cross_grad
        return carry

    lax.fori_loop(0, 20, similarity, 0)
    for tile in range(5):
        for slot in range(3):
            turned = tap_sum(
                lambda k: parts_ref[slot, tile * 128 + 3 + k : tile * 128 + 131 + k, :]
            ).T
            (square_ref, cross_ref, cols_ref)[slot][0, 0:128, :] = turned
        for channel in range(3):
            base = channel * 40
            down = [
                tap_sum(lambda k: (square_ref, cross_ref, cols_ref)[slot][0, base + k : base + k + 16, :])
                for slot in range(3)
            ]
            own = image_ref[channel, tile]
            truth = truth_ref[tile, base + 10 : base + 26, :]
            pull = down[0] + 2.0 * own * down[1] + truth * down[2]
            for half in range(2):
                value = swap_tiles(pull[half * 8 : half * 8 + 8])
                light_ref[tile * 6 + half * 3 + channel] = value
                for part in range(3):
                    piece = rounded(value)
                    split_ref[half, pl.ds(tile * (8 * GAP) + channel * 3 + part, 8, stride=GAP), :] = piece
                    value = value - piece
    moments = pixel_basis(16, 1)

    def scan(turn, pull_ref, behind):
        behind = list(behind)
        turned = [
            [
                pltpu.roll(
                    colour_ref[channel, group * 8 : group * 8 + 8, :], 128 - turn * 16 & 127, axis=1
                )
                for channel in range(3)
            ]
            for group in range(5)
        ]
        for entry in range(15, -1, -1):
            for group in range(5):
                at = group * 128 + entry * 8
                rows = pl.ds(turn * 640 + at, 8)
                spot = pl.ds(turn * (80 * STEP) + (group * 16 + entry) * STEP, 8)
                colour = [
                    jnp.broadcast_to(turned[group][channel][:, entry : entry + 1], (8, 128))
                    for channel in range(3)
                ]
                for half in range(2):
                    slot = group * 2 + half
                    light = group * 6 + half * 3
                    value = (
                        colour[0] * light_ref[light]
                        + colour[1] * light_ref[light + 1]
                        + colour[2] * light_ref[light + 2]
                    )
                    delta = value - behind[slot]
                    behind[slot] = behind[slot] + alpha_ref[half, rows, :] * delta
                    pull_ref[at : at + 8, half * 128 : half * 128 + 128] = (
                        weight_ref[half, spot, :] * delta
                    )
        return tuple(behind)

    def reduce(turn, pull_ref):
        for part in range(5):
            coarse, fine = coarse_fine(pull_ref[part * 128 : part * 128 + 128, :])
            total = dot_nt(moments, coarse) + dot_nt(moments, fine)
            sums_ref[pl.ds(pl.multiple_of((turn * 5 + part) * 8, 8), 8), :] = total[0:8]

    def backward(count, behind):
        turn = 7 - 2 * count
        reduce(turn + 1, pull_b)
        behind = scan(turn, pull_a, behind)
        reduce(turn, pull_a)
        return scan(turn - 1, pull_b, behind)

    pull_b[...] = jnp.zeros((640, 256), F32)
    lax.fori_loop(0, 4, backward, (jnp.zeros((8, 128), F32),) * 10)
    reduce(0, pull_b)

    def tints(tile, carry):
        at = pl.ds(pl.multiple_of(tile * GAP, 8), 16)
        halves = [coarse_fine(tile_rows(weight_ref, half, tile)) for half in range(2)]
        weight = jnp.concatenate(
            [jnp.concatenate([halves[0][part], halves[1][part]], 1) for part in range(2)], 0
        )
        light = jnp.concatenate([split_ref[half, at, :].astype(BF16) for half in range(2)], 1)
        total = dot_nt(light, weight)
        total = total[:, 0:128] + total[:, 128:256]
        tint_ref[at, :] = total
        return carry

    lax.fori_loop(0, ROWS, tints, 0, unroll=8)

    def entry_grads(block, carry):
        rows = pl.ds(block * 8, 8)
        zeroth, by_x, by_y, by_xx, by_xy, by_yy = [
            sums_ref[pl.ds(block * 8 + slot, 8, stride=40), :] for slot in range(6)
        ]
        x, y, a, b, c = [entries_ref[slot, rows, :] for slot in range(5)]
        off_x = by_x - x * zeroth
        off_y = by_y - y * zeroth
        feats_ref[0, rows, :] = a * off_x + b * off_y
        feats_ref[1, rows, :] = c * off_y + b * off_x
        feats_ref[2, rows, :] = -0.5 * (by_xx - x * (by_x + off_x))
        feats_ref[3, rows, :] = x * by_y + y * off_x - by_xy
        feats_ref[4, rows, :] = -0.5 * (by_yy - y * (by_y + off_y))
        feats_ref[8, rows, :] = zeroth
        for channel in range(3):
            feats_ref[5 + channel, rows, :] = (
                tint_ref[pl.ds(block * (8 * GAP) + channel * 3, 8, stride=GAP), :]
                + tint_ref[pl.ds(block * (8 * GAP) + channel * 3 + 1, 8, stride=GAP), :]
                + tint_ref[pl.ds(block * (8 * GAP) + channel * 3 + 2, 8, stride=GAP), :]
            )
        return carry

    lax.fori_loop(0, 5, entry_grads, 0)
    values = [
        by_entry(feats_ref[5 + channel, group * 8 : group * 8 + 8, :])
        for group in range(5)
        for channel in range(3)
    ]
    for number, value in enumerate(values):
        group, channel = divmod(number, 3)
        feats_ref[5 + channel, group * 8 : group * 8 + 8, :] = value

    def gather_block(block, carry):
        place = place_ref[pl.ds(block * 8, 8), :]
        tile = place >> 7
        entry = place & 127
        high = (tile & 56) | (entry >> 4)
        low = ((entry & 15) << 3) | (tile & 7)
        got = [jnp.zeros((8, 128), F32)] * FEATS
        for row in range(ROWS):
            same = high == row
            for feature in range(FEATS):
                value = pick(feats_ref[feature, row : row + 1, :], low)
                got[feature] = jnp.where(same, value, got[feature])
        for feature in range(FEATS):
            put_feature(table_ref, block, feature, got[feature])
        return carry

    lax.fori_loop(0, 5, gather_block, 0)
    expand_feats(
        table_ref,
        lambda number, start: (shift_ref[number], line_ref[number], start),
        out_ref,
        strips,
        lambda number: number * 6,
    )


def pull_kernel(focal, centre_x, centre_y):
    def kernel(
        camera_ref, count_ref, spot_ref, params_ref, place_ref, chunks_ref, out_ref,
        table_ref, wide_ref, local_ref, grads_ref, sems, out_sems,
    ):
        copies = fetch_params(params_ref, local_ref, sems)
        strips = chunks_ref.shape[0] // 6
        wide_ref[0 : strips * 6, :] = chunks_ref[...]
        compact_feats(
            wide_ref,
            lambda number, chunk, start: (
                start & 127,
                (start >> 7) * GAP,
                (start & 127) + count_ref[number] >= 128,
                start + count_ref[number],
            ),
            table_ref,
            strips,
            lambda number: spot_ref[number],
        )
        bounds = run_bounds(count_ref, strips)

        def block_grads(block, carry):
            rows = pl.ds(block * 8, 8)
            place = place_ref[rows, :]
            high = place >> 7
            low = place & 127
            got = [jnp.zeros((8, 128), F32)] * FEATS
            for row in range(ROWS):
                same = high == row
                for feature in range(FEATS):
                    value = pick(table_line(table_ref, row, feature), low)
                    got[feature] = jnp.where(same, value, got[feature])
            camera = select_camera(camera_ref, place, bounds)
            params = [
                local_ref[pl.ds(block * (8 * PLACE) + number, 8, stride=PLACE), :]
                for number in range(59)
            ]
            ignored, pull = jax.vjp(
                lambda values: project(values, camera, focal, centre_x, centre_y), params
            )
            for number, grad in enumerate(pull(got[:8])[0]):
                if number == 10:
                    grad = got[8] / (1.0 + jnp.exp(params[10]))
                grads_ref[pl.ds(block * (8 * PLACE) + number, 8, stride=PLACE), :] = grad
            for tile in range(8):
                result(block * 8 + tile).start()
            return carry

        def result(tile):
            return pltpu.make_async_copy(
                grads_ref.at[pl.ds(pl.multiple_of(tile * PLACE, 8), 59), :],
                out_ref.at[:, pl.ds(pl.multiple_of(tile * 128, 128), 128)],
                out_sems.at[tile],
            )

        for copy in copies:
            copy.wait()
        lax.fori_loop(0, 5, block_grads, 0)
        for tile in range(ROWS):
            result(tile).wait()

    return kernel


def shape(*dims, dtype=F32):
    return jax.ShapeDtypeStruct(dims, dtype)


def device_of(strip):
    core = strip & 1
    z, y, x = (strip >> 1) & 3, (strip >> 3) & 3, strip >> 5
    z = z + (y & 1) * (3 - 2 * z)
    y = y + (x & 1) * (3 - 2 * y)
    return ((x * 4 + y) * 4 + z) * 2 + core


def strip_of(device):
    core = device & 1
    z, y, x = (device >> 1) & 3, (device >> 3) & 3, device >> 5
    y = y + (x & 1) * (3 - 2 * y)
    z = z + (y & 1) * (3 - 2 * z)
    return ((x * 4 + y) * 4 + z) * 2 + core


def position_of(strips):
    return lax.rem(strip_of(lax.axis_index("strip")) + strips // VIEWS // 2, strips)


def keeps(strips):
    per_view = strips // VIEWS
    place = lax.rem(position_of(strips), per_view)
    return (place != 0).astype(F32), (place != per_view - 1).astype(F32)


def exchange(chunks, strips):
    sent = chunks.reshape(strips, 1, 768)
    got = lax.all_to_all(sent, "strip", split_axis=0, concat_axis=0, tiled=True)
    return got.reshape(strips * 6, 128)


def per_device(params, camera, send_index, send_count, tile_list, target):
    strips = lax.axis_size("strip")
    per_view = strips // VIEWS
    rows_strip = target.shape[1]
    width = target.shape[2]
    focal = 0.5 * width
    centre_y = 0.5 * rows_strip * per_view
    spots = [device_of(strip) for strip in range(strips)]
    spot_rows = jnp.asarray(np.array(spots, np.int32) * 6)
    ahead = [(spots[i], spots[(i + 1) % strips]) for i in range(strips)]
    behind = [(spots[(i + 1) % strips], spots[i]) for i in range(strips)]

    chunks, place, pack = pl.pallas_call(
        owner_kernel(focal, 0.5 * width, centre_y),
        out_shape=(
            shape(strips * 6, 128),
            shape(ROWS, 128, dtype=jnp.int32),
            shape(280, 128),
        ),
        in_specs=[SMEM, SMEM, SMEM, ANY, VMEM, VMEM, VMEM],
        scratch_shapes=[
            pltpu.VMEM((strips, 128), jnp.int32),
            pltpu.VMEM((ROWS + 8, 128), jnp.int32),
            pltpu.VMEM((FEATS, ROWS, 128), F32),
            pltpu.VMEM(((ROWS + 2) * GAP, 128), F32),
            pltpu.VMEM((ROWS * PLACE, 128), F32),
            pltpu.SemaphoreType.DMA((ROWS,)),
        ],
        name="owner",
    )(camera, send_count, spot_rows, params, send_index.T, target, tile_list)
    arrived = exchange(chunks, strips)
    moved = lax.ppermute(pack, "strip", list(enumerate(spots)))

    listed = pl.pallas_call(
        invert_kernel,
        out_shape=shape(ROWS, 128, dtype=jnp.int32),
        scratch_shapes=[pltpu.VMEM((ROWS, 128), jnp.int32)],
        compiler_params=pltpu.CompilerParams(vmem_limit_bytes=8 << 20),
        name="listed",
    )(moved)
    image, first, last, entries, colour, shifts, places, alphas, weights = pl.pallas_call(
        render_kernel,
        out_shape=(
            shape(3, 5, 16, 128),
            shape(300, 128),
            shape(300, 128),
            shape(5, ROWS, 128),
            shape(3, ROWS, 128),
            shape(strips, dtype=jnp.int32),
            shape(strips, dtype=jnp.int32),
            shape(2, 5120, 128),
            shape(2, 640 * STEP, 128),
        ),
        in_specs=[VMEM, VMEM],
        out_specs=(VMEM, VMEM, VMEM, VMEM, VMEM, SMEM, SMEM, VMEM, VMEM),
        scratch_shapes=[
            pltpu.VMEM(((ROWS + 2) * GAP, 128), F32),
            pltpu.VMEM((ROWS, 128), jnp.int32),
            pltpu.VMEM((ROWS * 24, 128), F32),
            pltpu.VMEM((640, 256), F32),
            pltpu.VMEM((640, 256), F32),
            pltpu.VMEM((ROWS * GAP, 128), F32),
            pltpu.VMEM((2, ROWS * GAP, 128), F32),
        ],
        compiler_params=pltpu.CompilerParams(vmem_limit_bytes=24 << 20),
        name="render",
    )(arrived, moved)
    above = lax.ppermute(last, "strip", ahead)
    below = lax.ppermute(first, "strip", behind)
    grads = pl.pallas_call(
        gradient_kernel,
        out_shape=shape(strips * 6, 128),
        in_specs=[SMEM, SMEM] + [VMEM] * 9,
        scratch_shapes=[
            pltpu.VMEM((5, 128, 128), F32),
            pltpu.VMEM((5, 128, 128), F32),
            pltpu.VMEM((5, 128, 128), F32),
            pltpu.VMEM((5, 128, 128), F32),
            pltpu.VMEM((5, 128, 128), F32),
            pltpu.VMEM((128, 128), F32),
            pltpu.VMEM((5, 656, 128), F32),
            pltpu.VMEM((3, 656, 128), F32),
            pltpu.VMEM((640, 256), F32),
            pltpu.VMEM((640, 256), F32),
            pltpu.VMEM((30, 8, 128), F32),
            pltpu.VMEM((2, ROWS * GAP, 128), F32),
            pltpu.VMEM((ROWS * 8 + 40, 128), F32),
            pltpu.VMEM((ROWS * GAP, 128), F32),
            pltpu.VMEM((FEATS, ROWS, 128), F32),
            pltpu.VMEM(((ROWS + 2) * GAP, 128), F32),
        ],
        compiler_params=pltpu.CompilerParams(vmem_limit_bytes=24 << 20),
        name="gradient",
    )(
        shifts, places, image, above, below, moved,
        entries, colour, listed, alphas, weights,
    )
    returned = exchange(grads, strips)
    return pl.pallas_call(
        pull_kernel(focal, 0.5 * width, centre_y),
        out_shape=shape(59, ROWS * 128),
        in_specs=[SMEM] * 3 + [ANY, VMEM, VMEM],
        out_specs=ANY,
        scratch_shapes=[
            pltpu.VMEM(((ROWS + 2) * GAP, 128), F32),
            pltpu.VMEM((strips * 6 + 8, 128), F32),
            pltpu.VMEM((ROWS * PLACE, 128), F32),
            pltpu.VMEM((ROWS * PLACE, 128), F32),
            pltpu.SemaphoreType.DMA((ROWS,)),
            pltpu.SemaphoreType.DMA((ROWS,)),
        ],
        compiler_params=pltpu.CompilerParams(vmem_limit_bytes=16 << 20),
        name="pull",
    )(camera, send_count, spot_rows, params, place, returned)


def solution(mesh):
    return jax.shard_map(
        per_device,
        mesh=mesh,
        in_specs=(
            P(None, "strip"),
            P(),
            P("strip", None),
            P("strip"),
            P("strip", None),
            P(None, "strip", None),
        ),
        out_specs=P(None, "strip"),
        check_vma=False,
    )
```

```python
import numpy as np

import jax
import jax.numpy as jnp
from jax import lax
from jax.experimental import pallas as pl
from jax.experimental.pallas import tpu as pltpu
from jax.sharding import PartitionSpec as P

VIEWS = 4
ROWS = 40
FEATS = 9
GAP = 24
PLACE = 72
STEP = 9
LOG2E = 1.4426950408889634
harmonic_zero = 0.28209479177387814
harmonic_one = 0.4886025119029199
harmonic_two = (
    1.0925484305920792,
    -1.0925484305920792,
    0.31539156525252005,
    -1.0925484305920792,
    0.5462742152960396,
)
harmonic_three = (
    -0.5900435899266435,
    2.890611442640554,
    -0.4570457994644658,
    0.3731763325901154,
    -0.4570457994644658,
    1.445305721320277,
    -0.5900435899266435,
)
light_term = 0.0001
contrast_term = 0.0009
F32 = jnp.float32
BF16 = jnp.bfloat16
SMEM = pl.BlockSpec(memory_space=pltpu.SMEM)
VMEM = pl.BlockSpec(memory_space=pltpu.VMEM)
ANY = pl.BlockSpec(memory_space=pl.ANY)


def iota(shape, axis):
    return lax.broadcasted_iota(jnp.int32, shape, axis)


def dot_nt(a, b):
    return lax.dot_general(a, b, (((1,), (1,)), ((), ())), preferred_element_type=F32)


def rounded(x):
    return x.astype(BF16).astype(F32)


def pick(row, lanes):
    return jnp.take_along_axis(
        jnp.broadcast_to(row, lanes.shape), lanes, axis=1, mode="promise_in_bounds"
    )


def harmonics(along_x, along_y, along_z):
    square_x = along_x * along_x
    square_y = along_y * along_y
    square_z = along_z * along_z
    return [
        harmonic_zero + 0.0 * along_x,
        -harmonic_one * along_y,
        harmonic_one * along_z,
        -harmonic_one * along_x,
        harmonic_two[0] * along_x * along_y,
        harmonic_two[1] * along_y * along_z,
        harmonic_two[2] * (2.0 * square_z - square_x - square_y),
        harmonic_two[3] * along_x * along_z,
        harmonic_two[4] * (square_x - square_y),
        harmonic_three[0] * along_y * (3.0 * square_x - square_y),
        harmonic_three[1] * along_x * along_y * along_z,
        harmonic_three[2] * along_y * (4.0 * square_z - square_x - square_y),
        harmonic_three[3] * along_z * (2.0 * square_z - 3.0 * square_x - 3.0 * square_y),
        harmonic_three[4] * along_x * (4.0 * square_z - square_x - square_y),
        harmonic_three[5] * along_z * (square_x - square_y),
        harmonic_three[6] * along_x * (square_x - 3.0 * square_y),
    ]


def project(params, camera, focal, centre_x, centre_y):
    rotation = [[camera[3 * row + col] for col in range(3)] for row in range(3)]
    mean = [params[axis] for axis in range(3)]
    placed = [
        rotation[row][0] * mean[0]
        + rotation[row][1] * mean[1]
        + rotation[row][2] * mean[2]
        + camera[9 + row]
        for row in range(3)
    ]
    depth = placed[2]
    inverse = 1.0 / depth
    screen_x = focal * placed[0] * inverse + centre_x
    screen_y = focal * placed[1] * inverse + centre_y
    quaternion = params[6:10]
    scale = lax.rsqrt(
        quaternion[0] * quaternion[0]
        + quaternion[1] * quaternion[1]
        + quaternion[2] * quaternion[2]
        + quaternion[3] * quaternion[3]
    )
    real, imag_x, imag_y, imag_z = [part * scale for part in quaternion]
    turn = [
        [
            1.0 - 2.0 * (imag_y * imag_y + imag_z * imag_z),
            2.0 * (imag_x * imag_y - real * imag_z),
            2.0 * (imag_x * imag_z + real * imag_y),
        ],
        [
            2.0 * (imag_x * imag_y + real * imag_z),
            1.0 - 2.0 * (imag_x * imag_x + imag_z * imag_z),
            2.0 * (imag_y * imag_z - real * imag_x),
        ],
        [
            2.0 * (imag_x * imag_z - real * imag_y),
            2.0 * (imag_y * imag_z + real * imag_x),
            1.0 - 2.0 * (imag_x * imag_x + imag_y * imag_y),
        ],
    ]
    scales = [jnp.exp(part) for part in params[3:6]]
    near = focal * inverse
    slant = [-near * placed[0] * inverse, -near * placed[1] * inverse]
    facing = [
        [near * rotation[row][col] + slant[row] * rotation[2][col] for col in range(3)]
        for row in range(2)
    ]
    stretch = [
        [
            (
                facing[row][0] * turn[0][col]
                + facing[row][1] * turn[1][col]
                + facing[row][2] * turn[2][col]
            )
            * scales[col]
            for col in range(3)
        ]
        for row in range(2)
    ]
    cov_xx = (
        stretch[0][0] * stretch[0][0]
        + stretch[0][1] * stretch[0][1]
        + stretch[0][2] * stretch[0][2]
        + 0.3
    )
    cov_xy = (
        stretch[0][0] * stretch[1][0]
        + stretch[0][1] * stretch[1][1]
        + stretch[0][2] * stretch[1][2]
    )
    cov_yy = (
        stretch[1][0] * stretch[1][0]
        + stretch[1][1] * stretch[1][1]
        + stretch[1][2] * stretch[1][2]
        + 0.3
    )
    over = 1.0 / (cov_xx * cov_yy - cov_xy * cov_xy)
    shrink = 1.0 / jnp.sqrt(placed[0] * placed[0] + placed[1] * placed[1] + depth * depth)
    heading = [
        (
            rotation[0][col] * placed[0]
            + rotation[1][col] * placed[1]
            + rotation[2][col] * placed[2]
        )
        * shrink
        for col in range(3)
    ]
    basis = harmonics(heading[0], heading[1], heading[2])
    colour = []
    for channel in range(3):
        total = 0.5 + basis[0] * params[11 + channel]
        for k in range(1, 16):
            total = total + basis[k] * params[11 + 3 * k + channel]
        colour.append(total)
    return [
        screen_x,
        screen_y,
        cov_yy * over,
        -cov_xy * over,
        cov_xx * over,
        colour[0],
        colour[1],
        colour[2],
    ]


def log_sigmoid(logit):
    return jnp.minimum(logit, 0.0) - jnp.log(1.0 + jnp.exp(-jnp.abs(logit)))


def send_views(count_ref, strips):
    per_view = strips // VIEWS
    offset = per_view // 2
    runs = []
    for strip in range(strips):
        view = (strip + offset) % strips // per_view
        if not runs or runs[-1][1] != view:
            runs.append([strip, view])
    return runs


def compact_ints(chunk_ref, count_ref, out_ref, steps):
    lane = iota((1, 128), 1)

    def step(number, carry):
        start, held = carry
        live = count_ref[number]
        shift = start & 127
        row = start >> 7
        chunk = pltpu.roll(chunk_ref[pl.ds(number, 1), :], shift, axis=1)
        held = jnp.where(lane >= shift, chunk, held)
        out_ref[pl.ds(row, 1), :] = held
        held = jnp.where(shift + live >= 128, chunk, held)
        return start + live, held

    lax.fori_loop(0, steps, step, (jnp.int32(0), jnp.zeros((1, 128), jnp.int32)), unroll=16)


def compact_feats(chunk_ref, place_of, table_ref, steps, spot=None):
    lane = iota((8, 128), 1)

    def step(number, carry):
        start, held, last = carry
        if spot is not None:
            chunk = chunk_ref[pl.ds(spot(number), 8), :]
        elif isinstance(number, int) and number == steps - 1:
            chunk = pltpu.roll(chunk_ref[number * 6 - 2 : number * 6 + 6, :], 6, axis=0)
        else:
            chunk = chunk_ref[pl.ds(number * 6, 8), :]
        shift, line, crossed, start = place_of(number, chunk, start)
        even = pltpu.roll(chunk, (shift + 48) & 127, axis=1)
        odd = pltpu.roll(chunk, (shift + 96) & 127, axis=1)
        chunk = pltpu.roll(chunk, shift, axis=1)
        rest = jnp.where(((lane - shift) & 127) < 48, even, pltpu.roll(odd, 7, axis=0))
        fresh = lane >= shift
        held = jnp.where(fresh, chunk, held)
        last = jnp.where(fresh, rest, last)
        base = pl.multiple_of(line, 8)
        table_ref[pl.ds(base, 8), :] = held
        table_ref[pl.ds(base + 8, 8), :] = last
        held = jnp.where(crossed, chunk, held)
        last = jnp.where(crossed, rest, last)
        return start, held, last

    zero = jnp.zeros((8, 128), F32)
    carry = lax.fori_loop(0, steps - 16, step, (jnp.int32(0), zero, zero), unroll=56)
    for number in range(steps - 16, steps):
        carry = step(number, carry)


def expand_feats(table_ref, place_of, out_ref, steps, spot, count_ref=None):
    lane = iota((8, 128), 1)
    sub = iota((8, 128), 0)
    even = (sub & 1) == 0
    mark = (sub == 1) & (lane == 127)

    def step(number, start):
        shift, line, start = place_of(number, start)
        back = 128 - shift
        base = pl.multiple_of(line, 8)
        here = lane < back
        main = jnp.where(
            here,
            pltpu.roll(table_ref[pl.ds(base, 8), :], back, axis=1),
            pltpu.roll(table_ref[pl.ds(base + GAP, 8), :], back, axis=1),
        )
        rest = jnp.where(
            here,
            pltpu.roll(table_ref[pl.ds(base + 8, 8), :], back, axis=1),
            pltpu.roll(table_ref[pl.ds(base + GAP + 8, 8), :], back, axis=1),
        )
        tail = jnp.where(even, pltpu.roll(rest, 80, axis=1), pltpu.roll(rest, 32, axis=1))
        if count_ref is not None:
            tail = jnp.where(mark, count_ref[number].astype(F32), tail)
        out_ref[pl.ds(spot(number), 6), :] = jnp.where(lane < 80, main, tail)[0:6]
        return start

    lax.fori_loop(0, steps, step, jnp.int32(0), unroll=16)


def line_of(feature):
    return feature if feature < 6 else 8 + 2 * (feature - 6)


def put_feature(table_ref, block, feature, value):
    line = line_of(feature)
    table_ref[pl.ds(block * (8 * GAP) + line, 8, stride=GAP), :] = value
    if feature >= 6:
        table_ref[pl.ds(block * (8 * GAP) + line + 1, 8, stride=GAP), :] = value


def table_line(table_ref, row, feature):
    line = row * GAP + line_of(feature)
    return table_ref[line : line + 1, :]


def fetch_params(params_ref, local_ref, sems):
    copies = [
        pltpu.make_async_copy(
            params_ref.at[:, pl.ds(tile * 128, 128)],
            local_ref.at[pl.ds(tile * PLACE, 59), :],
            sems.at[tile],
        )
        for tile in range(ROWS)
    ]
    for copy in copies:
        copy.start()
    return copies


def invert(rows_ref, out_ref):
    high = iota((ROWS, 128), 0)
    low = iota((128, 128), 0)
    lane = iota((ROWS, 128), 1).astype(F32)
    total = jnp.zeros((2 * ROWS, 128), F32)
    for pair in range(ROWS // 2):
        lefts = []
        rights = []
        for row in (2 * pair, 2 * pair + 1):
            number = rows_ref[row : row + 1, :]
            same = high == (number >> 7)
            lefts.append(
                jnp.concatenate([jnp.where(same, float(row), 0.0), jnp.where(same, lane, 0.0)], 0)
            )
            rights.append(jnp.where(low == (number & 127), 1.0, 0.0))
        total = total + dot_nt(
            jnp.concatenate(lefts, 1).astype(BF16), jnp.concatenate(rights, 1).astype(BF16)
        )
    out_ref[...] = (total[:ROWS] * 128.0 + total[ROWS:]).astype(jnp.int32)


def select_camera(camera_ref, place, run_starts):
    values = []
    for entry in range(12):
        value = jnp.full(place.shape, camera_ref[run_starts[0][1], entry], F32)
        for start, view in run_starts[1:]:
            value = jnp.where(place >= start, camera_ref[view, entry], value)
        values.append(value)
    return values


def run_bounds(count_ref, strips):
    runs = send_views(count_ref, strips)
    bounds = [(jnp.int32(0), runs[0][1])]
    for (first, _), (last, view) in zip(runs[:-1], runs[1:]):
        begin = bounds[-1][0]
        total = lax.fori_loop(
            first, last, lambda number, sum_: sum_ + count_ref[number], begin, unroll=True
        )
        bounds.append((total, view))
    return bounds


def owner_kernel(focal, centre_x, centre_y):
    def kernel(
        camera_ref, count_ref, spot_ref, params_ref, index_ref, target_ref, list_ref,
        out_ref, place_ref, pack_ref,
        wide_ref, rows_ref, feats_ref, table_ref, local_ref, sems,
    ):
        copies = fetch_params(params_ref, local_ref, sems)
        for tile in range(5):
            for channel in range(3):
                at = tile * 56 + channel * 16
                pack_ref[at : at + 16, :] = target_ref[channel, :, tile * 128 : tile * 128 + 128]
            pack_ref[tile * 56 + 48 : tile * 56 + 56, :] = list_ref[
                tile * 8 : tile * 8 + 8, :
            ].astype(F32)
        strips = index_ref.shape[1]
        wide_ref[...] = jnp.concatenate(
            [index_ref[...], jnp.zeros((128 - index_ref.shape[0], strips), jnp.int32)], 0
        ).T
        compact_ints(wide_ref, count_ref, rows_ref, strips)
        invert(rows_ref, place_ref)
        bounds = run_bounds(count_ref, strips)
        for copy in copies:
            copy.wait()

        def project_block(block, carry):
            rows = pl.ds(block * 8, 8)
            camera = select_camera(camera_ref, place_ref[rows, :], bounds)
            params = [
                local_ref[pl.ds(block * (8 * PLACE) + number, 8, stride=PLACE), :]
                for number in range(59)
            ]
            feats = project(params, camera, focal, centre_x, centre_y)
            feats.append(log_sigmoid(params[10]))
            for feature in range(FEATS):
                feats_ref[feature, rows, :] = feats[feature]
            return carry

        lax.fori_loop(0, 5, project_block, 0)

        def gather_block(block, carry):
            number = rows_ref[pl.ds(block * 8, 8), :]
            high = number >> 7
            low = number & 127
            got = [jnp.zeros((8, 128), F32)] * FEATS
            for row in range(ROWS):
                same = high == row
                for feature in range(FEATS):
                    value = pick(feats_ref[feature, row : row + 1, :], low)
                    got[feature] = jnp.where(same, value, got[feature])
            for feature in range(FEATS):
                put_feature(table_ref, block, feature, got[feature])
            return carry

        lax.fori_loop(0, 5, gather_block, 0)
        expand_feats(
            table_ref,
            lambda number, start: (start & 127, (start >> 7) * GAP, start + count_ref[number]),
            out_ref,
            strips,
            lambda number: spot_ref[number],
            count_ref,
        )

    return kernel


def pixel_basis(rows, times):
    row = iota((rows, 256), 0)
    pixel = iota((rows, 256), 1)
    x = (pixel & 15).astype(F32) - 7.5
    y = (pixel >> 4).astype(F32) - 7.5
    value = jnp.where(row < 6 * times, y * y, 0.0)
    for number, term in ((5, x * y), (4, x * x), (3, y), (2, x), (1, 1.0)):
        value = jnp.where(row < number * times, term, value)
    return value.astype(BF16)


def swap_tiles(x):
    sub = iota((8, 128), 0)
    group = iota((8, 128), 1) >> 4
    for k in (1, 2, 4):
        up = pltpu.roll(pltpu.roll(x, 8 - k, axis=0), 16 * k, axis=1)
        down = pltpu.roll(pltpu.roll(x, k, axis=0), 128 - 16 * k, axis=1)
        s = (sub & k) != 0
        g = (group & k) != 0
        x = jnp.where(s == g, x, jnp.where(g, up, down))
    return x


def coarse_fine(x):
    coarse = x.astype(BF16)
    return coarse, (x - coarse.astype(F32)).astype(BF16)


def by_entry(x):
    lane = iota((8, 128), 1)
    order = ((lane & 7) << 4) | (lane >> 3)
    return jnp.take_along_axis(swap_tiles(x), order, axis=1, mode="promise_in_bounds")


def by_tile(x):
    lane = iota((8, 128), 1)
    order = ((lane & 15) << 3) | (lane >> 4)
    return swap_tiles(jnp.take_along_axis(x, order, axis=1, mode="promise_in_bounds"))


def tile_rows(ref, half, tile):
    base = (tile >> 3) * (16 * STEP) + (tile & 7)
    return jnp.concatenate(
        [ref[half, pl.ds(base + turn * (80 * STEP), 16, stride=STEP), :] for turn in range(8)], 0
    )


def turned_colours(colour_ref, turn, group):
    return [
        pltpu.roll(
            colour_ref[channel, group * 8 : group * 8 + 8, :], 128 - turn * 16 & 127, axis=1
        )
        for channel in range(3)
    ]


def lit(turned, entry):
    return [jnp.broadcast_to(part[:, entry : entry + 1], (8, 128)) for part in turned]


def render_kernel(
    chunks_ref, moved_ref,
    image_ref, first_ref, last_ref, entries_ref, colour_ref, shift_ref, line_ref,
    alpha_ref, weight_ref,
    table_ref, order_ref, lines_ref, power_a, power_b, tint_ref, shown_ref,
):
    for tile in range(5):
        for channel in range(3):
            at = 150 + (channel * 5 + tile) * 10
            base = tile * 56 + channel * 16
            first_ref[at : at + 10, :] = moved_ref[base : base + 10, :]
            last_ref[at : at + 10, :] = moved_ref[base + 6 : base + 16, :]
    strips = chunks_ref.shape[0] // 6

    def place_of(number, chunk, start):
        live = chunk[1, 127].astype(jnp.int32)
        shift = start & 127
        line = (start >> 7) * GAP
        shift_ref[number] = shift
        line_ref[number] = line
        return shift, line, shift + live >= 128, start + live

    compact_feats(chunks_ref, place_of, table_ref, strips)
    per_view = strips // VIEWS
    top = (lax.rem(position_of(strips), per_view) * 16 + 8).astype(F32)
    for group in range(5):
        rows = slice(group * 8, group * 8 + 8)
        order_ref[rows, :] = by_entry(moved_ref[group * 56 + 48 : group * 56 + 56, :]).astype(
            jnp.int32
        )

    def entry_block(block, carry):
        rows = pl.ds(block * 8, 8)
        number = order_ref[rows, :]
        high = number >> 7
        low = number & 127
        got = [jnp.zeros((8, 128), F32)] * FEATS
        for row in range(ROWS):
            same = high == row
            for feature in range(FEATS):
                value = pick(table_line(table_ref, row, feature), low)
                got[feature] = jnp.where(same, value, got[feature])
        across = (block * 8 + (iota((8, 128), 1) & 7)) * 16 + 8
        x = got[0] - across.astype(F32)
        y = got[1] - top
        a, b, c = got[2:5]
        for slot, value in enumerate((x, y, a, b, c)):
            entries_ref[slot, rows, :] = value
        terms = [
            got[8] - 0.5 * (a * x * x + c * y * y) - b * x * y,
            a * x + b * y,
            c * y + b * x,
            -0.5 * a,
            -b,
            -0.5 * c,
        ]
        for slot, term in enumerate(terms):
            term = term * LOG2E
            for part in range(3):
                piece = rounded(term)
                lines_ref[pl.ds(block * 24 + slot * 3 + part, 8, stride=120), :] = piece
                term = term - piece
        for slot in range(18, 24):
            lines_ref[pl.ds(block * 24 + slot, 8, stride=120), :] = jnp.zeros((8, 128), F32)
        for channel in range(3):
            colour_ref[channel, rows, :] = got[5 + channel]
        return carry

    lax.fori_loop(0, 5, entry_block, 0)
    values = [
        by_tile(colour_ref[channel, group * 8 : group * 8 + 8, :])
        for group in range(5)
        for channel in range(3)
    ]
    for number, value in enumerate(values):
        group, channel = divmod(number, 3)
        colour_ref[channel, group * 8 : group * 8 + 8, :] = value
        for part in range(3):
            piece = rounded(value)
            tint_ref[pl.ds(group * (8 * GAP) + channel * 3 + part, 8, stride=GAP), :] = piece
            value = value - piece
    basis = pixel_basis(24, 3)

    def powers(turn, power_ref):
        for part in range(5):
            lines = lines_ref[pl.ds(pl.multiple_of((turn * 5 + part) * 24, 8), 24), :]
            power_ref[part * 128 : part * 128 + 128, :] = jnp.dot(
                lines.T.astype(BF16), basis, preferred_element_type=F32
            )

    def scan(turn, power_ref, through):
        through = list(through)
        for entry in range(16):
            for group in range(5):
                at = group * 128 + entry * 8
                for half in range(2):
                    slot = group * 2 + half
                    alpha = jnp.exp2(power_ref[at : at + 8, half * 128 : half * 128 + 128])
                    weight = alpha * through[slot]
                    through[slot] = through[slot] - weight
                    alpha_ref[half, pl.ds(turn * 640 + at, 8), :] = alpha
                    spot = pl.ds(turn * (80 * STEP) + (group * 16 + entry) * STEP, 8)
                    weight_ref[half, spot, :] = weight
        return tuple(through)

    def blend(pair, through):
        powers(2 * pair + 1, power_b)
        through = scan(2 * pair, power_a, through)
        powers(jnp.minimum(2 * pair + 2, 7), power_a)
        through = scan(2 * pair + 1, power_b, through)
        return through

    powers(0, power_a)
    lax.fori_loop(0, 4, blend, (jnp.ones((8, 128), F32),) * 10)

    def tints(tile, carry):
        at = pl.ds(pl.multiple_of(tile * GAP, 8), 16)
        tint = tint_ref[at, :].astype(BF16)
        halves = [coarse_fine(tile_rows(weight_ref, half, tile)) for half in range(2)]
        weight = jnp.concatenate(
            [jnp.concatenate([halves[0][part], halves[1][part]], 1) for part in range(2)], 0
        )
        total = jnp.dot(jnp.concatenate([tint, tint], 1), weight, preferred_element_type=F32)
        for half in range(2):
            shown_ref[half, at, :] = total[:, half * 128 : half * 128 + 128]
        return carry

    lax.fori_loop(0, ROWS, tints, 0, unroll=8)
    for group in range(5):
        for channel in range(3):
            for half in range(2):
                parts = [
                    shown_ref[half, pl.ds(group * (8 * GAP) + channel * 3 + part, 8, stride=GAP), :]
                    for part in range(3)
                ]
                image_ref[channel, group, half * 8 : half * 8 + 8, :] = swap_tiles(
                    parts[0] + parts[1] + parts[2]
                )
            at = (channel * 5 + group) * 10
            first_ref[at : at + 10, :] = image_ref[channel, group, 0:10, :]
            last_ref[at : at + 10, :] = image_ref[channel, group, 6:16, :]


def window_weights():
    offsets = np.arange(11, dtype=np.float64) - 5.0
    raw = np.exp(-offsets * offsets / 4.5)
    return [float(value) for value in raw / raw.sum()]


WINDOW = window_weights()


def tap_sum(load):
    total = WINDOW[5] * load(5)
    for k in range(5):
        total = total + WINDOW[k] * (load(k) + load(10 - k))
    return total


def down_rows(field_ref, slot, out_ref):
    for tile in range(5):
        for channel in range(3):
            base = channel * 40
            out_ref[base : base + 32, :] = tap_sum(
                lambda k: field_ref[tile, base + k : base + k + 32, :]
            )
        yield tile, out_ref[...].T


def extend(ext_ref, own, above, below, keep_above, keep_below):
    for tile in range(5):
        for channel in range(3):
            base = channel * 40
            ext_ref[tile, base : base + 10, :] = above(channel, tile) * keep_above
            ext_ref[tile, base + 10 : base + 26, :] = own(channel, tile)
            ext_ref[tile, base + 26 : base + 36, :] = below(channel, tile) * keep_below
            ext_ref[tile, base + 36 : base + 40, :] = jnp.zeros((4, 128), F32)
        ext_ref[tile, 120:128, :] = jnp.zeros((8, 128), F32)


def clear_ends(ref, slot):
    ref[slot, 0:8, :] = jnp.zeros((8, 128), F32)
    ref[slot, 648:656, :] = jnp.zeros((8, 128), F32)


def invert_kernel(moved_ref, out_ref, rows_ref):
    for group in range(5):
        rows_ref[group * 8 : group * 8 + 8, :] = moved_ref[
            group * 56 + 48 : group * 56 + 56, :
        ].astype(jnp.int32)
    invert(rows_ref, out_ref)


def gradient_kernel(
    shift_ref, line_ref, image_ref, above_ref, below_ref, moved_ref,
    entries_ref, colour_ref, place_ref, alpha_ref, weight_ref,
    out_ref,
    ext_ref, square_ref, cross_ref, truth_ref, ideal_ref, rows_ref, cols_ref, parts_ref,
    pull_a, pull_b, light_ref, split_ref, sums_ref, tint_ref, feats_ref, table_ref,
):
    strips = out_ref.shape[0] // 6
    keep_above, keep_below = keeps(strips)
    def rim(base):
        return lambda ref: lambda channel, tile: ref[
            base + (channel * 5 + tile) * 10 : base + (channel * 5 + tile) * 10 + 10, :
        ]

    extend(
        ext_ref,
        lambda channel, tile: image_ref[channel, tile],
        rim(0)(above_ref),
        rim(0)(below_ref),
        keep_above,
        keep_below,
    )
    extend(
        truth_ref,
        lambda channel, tile: moved_ref[tile * 56 + channel * 16 : tile * 56 + channel * 16 + 16, :],
        rim(150)(above_ref),
        rim(150)(below_ref),
        keep_above,
        keep_below,
    )
    for tile in range(5):
        square_ref[tile] = ext_ref[tile] * ext_ref[tile]
        cross_ref[tile] = ext_ref[tile] * truth_ref[tile]
        ideal_ref[tile] = truth_ref[tile] * truth_ref[tile]
    rows_ref[...] = jnp.zeros((128, 128), F32)
    for slot in range(3):
        clear_ends(parts_ref, slot)
    for slot, source in enumerate((ext_ref, square_ref, cross_ref, truth_ref, ideal_ref)):
        clear_ends(cols_ref, slot)
        for tile, turned in down_rows(source, slot, rows_ref):
            cols_ref[slot, 8 + tile * 128 : 136 + tile * 128, :] = turned
    lane = iota((8, 128), 1)
    row = lane - jnp.where(lane >= 80, 80, jnp.where(lane >= 40, 40, 0))
    live = jnp.where(row < 5, keep_above, jnp.where(row >= 21, keep_below, 1.0))
    live = jnp.where((row < 26) & (lane < 120), live, 0.0)[0:1, :]

    def similarity(step, carry):
        base = step * 32
        mean_x, power_x, cross, mean_y, power_y = [
            tap_sum(lambda k: cols_ref[slot, pl.ds(base + 3 + k, 32), :]) for slot in range(5)
        ]
        both = mean_x * mean_y
        squares = mean_x * mean_x + mean_y * mean_y
        light_up = 2.0 * both + light_term
        light_down = squares + light_term
        sharp_up = 2.0 * (cross - both) + contrast_term
        sharp_down = power_x + power_y - squares + contrast_term
        over = 1.0 / (light_down * sharp_down)
        score = light_up * sharp_up * over
        scale = live * over
        cross_grad = -2.0 * light_up * scale
        power_grad = score * light_down * scale
        mean_grad = (
            -2.0 * mean_y * (sharp_up - light_up) + 2.0 * mean_x * score * (sharp_down - light_down)
        ) * scale
        at = pl.ds(base + 8, 32)
        parts_ref[0, at, :] = mean_grad
        parts_ref[1, at, :] = power_grad
        parts_ref[2, at, :] = cross_grad
        return carry

    lax.fori_loop(0, 20, similarity, 0)
    for tile in range(5):
        for slot in range(3):
            turned = tap_sum(
                lambda k: parts_ref[slot, tile * 128 + 3 + k : tile * 128 + 131 + k, :]
            ).T
            (square_ref, cross_ref, cols_ref)[slot][0, 0:128, :] = turned
        for channel in range(3):
            base = channel * 40
            down = [
                tap_sum(lambda k: (square_ref, cross_ref, cols_ref)[slot][0, base + k : base + k + 16, :])
                for slot in range(3)
            ]
            own = image_ref[channel, tile]
            truth = truth_ref[tile, base + 10 : base + 26, :]
            pull = down[0] + 2.0 * own * down[1] + truth * down[2]
            for half in range(2):
                value = swap_tiles(pull[half * 8 : half * 8 + 8])
                light_ref[tile * 6 + half * 3 + channel] = value
                for part in range(3):
                    piece = rounded(value)
                    split_ref[half, pl.ds(tile * (8 * GAP) + channel * 3 + part, 8, stride=GAP), :] = piece
                    value = value - piece
    moments = pixel_basis(16, 1)

    def scan(turn, pull_ref, behind):
        behind = list(behind)
        turned = [
            [
                pltpu.roll(
                    colour_ref[channel, group * 8 : group * 8 + 8, :], 128 - turn * 16 & 127, axis=1
                )
                for channel in range(3)
            ]
            for group in range(5)
        ]
        for entry in range(15, -1, -1):
            for group in range(5):
                at = group * 128 + entry * 8
                rows = pl.ds(turn * 640 + at, 8)
                spot = pl.ds(turn * (80 * STEP) + (group * 16 + entry) * STEP, 8)
                colour = [
                    jnp.broadcast_to(turned[group][channel][:, entry : entry + 1], (8, 128))
                    for channel in range(3)
                ]
                for half in range(2):
                    slot = group * 2 + half
                    light = group * 6 + half * 3
                    value = (
                        colour[0] * light_ref[light]
                        + colour[1] * light_ref[light + 1]
                        + colour[2] * light_ref[light + 2]
                    )
                    delta = value - behind[slot]
                    behind[slot] = behind[slot] + alpha_ref[half, rows, :] * delta
                    pull_ref[at : at + 8, half * 128 : half * 128 + 128] = (
                        weight_ref[half, spot, :] * delta
                    )
        return tuple(behind)

    def reduce(turn, pull_ref):
        for part in range(5):
            coarse, fine = coarse_fine(pull_ref[part * 128 : part * 128 + 128, :])
            total = dot_nt(moments, coarse) + dot_nt(moments, fine)
            sums_ref[pl.ds(pl.multiple_of((turn * 5 + part) * 8, 8), 8), :] = total[0:8]

    def backward(count, behind):
        turn = 7 - 2 * count
        reduce(turn + 1, pull_b)
        behind = scan(turn, pull_a, behind)
        reduce(turn, pull_a)
        return scan(turn - 1, pull_b, behind)

    pull_b[...] = jnp.zeros((640, 256), F32)
    lax.fori_loop(0, 4, backward, (jnp.zeros((8, 128), F32),) * 10)
    reduce(0, pull_b)

    def tints(tile, carry):
        at = pl.ds(pl.multiple_of(tile * GAP, 8), 16)
        halves = [coarse_fine(tile_rows(weight_ref, half, tile)) for half in range(2)]
        weight = jnp.concatenate(
            [jnp.concatenate([halves[0][part], halves[1][part]], 1) for part in range(2)], 0
        )
        light = jnp.concatenate([split_ref[half, at, :].astype(BF16) for half in range(2)], 1)
        total = dot_nt(light, weight)
        total = total[:, 0:128] + total[:, 128:256]
        tint_ref[at, :] = total
        return carry

    lax.fori_loop(0, ROWS, tints, 0, unroll=8)

    def entry_grads(block, carry):
        rows = pl.ds(block * 8, 8)
        zeroth, by_x, by_y, by_xx, by_xy, by_yy = [
            sums_ref[pl.ds(block * 8 + slot, 8, stride=40), :] for slot in range(6)
        ]
        x, y, a, b, c = [entries_ref[slot, rows, :] for slot in range(5)]
        off_x = by_x - x * zeroth
        off_y = by_y - y * zeroth
        feats_ref[0, rows, :] = a * off_x + b * off_y
        feats_ref[1, rows, :] = c * off_y + b * off_x
        feats_ref[2, rows, :] = -0.5 * (by_xx - x * (by_x + off_x))
        feats_ref[3, rows, :] = x * by_y + y * off_x - by_xy
        feats_ref[4, rows, :] = -0.5 * (by_yy - y * (by_y + off_y))
        feats_ref[8, rows, :] = zeroth
        for channel in range(3):
            feats_ref[5 + channel, rows, :] = (
                tint_ref[pl.ds(block * (8 * GAP) + channel * 3, 8, stride=GAP), :]
                + tint_ref[pl.ds(block * (8 * GAP) + channel * 3 + 1, 8, stride=GAP), :]
                + tint_ref[pl.ds(block * (8 * GAP) + channel * 3 + 2, 8, stride=GAP), :]
            )
        return carry

    lax.fori_loop(0, 5, entry_grads, 0)
    values = [
        by_entry(feats_ref[5 + channel, group * 8 : group * 8 + 8, :])
        for group in range(5)
        for channel in range(3)
    ]
    for number, value in enumerate(values):
        group, channel = divmod(number, 3)
        feats_ref[5 + channel, group * 8 : group * 8 + 8, :] = value

    def gather_block(block, carry):
        place = place_ref[pl.ds(block * 8, 8), :]
        tile = place >> 7
        entry = place & 127
        high = (tile & 56) | (entry >> 4)
        low = ((entry & 15) << 3) | (tile & 7)
        got = [jnp.zeros((8, 128), F32)] * FEATS
        for row in range(ROWS):
            same = high == row
            for feature in range(FEATS):
                value = pick(feats_ref[feature, row : row + 1, :], low)
                got[feature] = jnp.where(same, value, got[feature])
        for feature in range(FEATS):
            put_feature(table_ref, block, feature, got[feature])
        return carry

    lax.fori_loop(0, 5, gather_block, 0)
    expand_feats(
        table_ref,
        lambda number, start: (shift_ref[number], line_ref[number], start),
        out_ref,
        strips,
        lambda number: number * 6,
    )


def pull_kernel(focal, centre_x, centre_y):
    def kernel(
        camera_ref, count_ref, spot_ref, params_ref, place_ref, chunks_ref, out_ref,
        table_ref, wide_ref, local_ref, grads_ref, sems, out_sems,
    ):
        copies = fetch_params(params_ref, local_ref, sems)
        strips = chunks_ref.shape[0] // 6
        wide_ref[0 : strips * 6, :] = chunks_ref[...]
        compact_feats(
            wide_ref,
            lambda number, chunk, start: (
                start & 127,
                (start >> 7) * GAP,
                (start & 127) + count_ref[number] >= 128,
                start + count_ref[number],
            ),
            table_ref,
            strips,
            lambda number: spot_ref[number],
        )
        bounds = run_bounds(count_ref, strips)

        def gather(block):
            place = place_ref[pl.ds(block * 8, 8), :]
            high = place >> 7
            low = place & 127
            got = [jnp.zeros((8, 128), F32)] * FEATS
            for row in range(ROWS):
                same = high == row
                for feature in range(FEATS):
                    value = pick(table_line(table_ref, row, feature), low)
                    got[feature] = jnp.where(same, value, got[feature])
            return tuple(got)

        def grads(block, got):
            camera = select_camera(camera_ref, place_ref[pl.ds(block * 8, 8), :], bounds)
            params = [
                local_ref[pl.ds(block * (8 * PLACE) + number, 8, stride=PLACE), :]
                for number in range(59)
            ]
            ignored, pull = jax.vjp(
                lambda values: project(values, camera, focal, centre_x, centre_y), params
            )
            for number, grad in enumerate(pull(list(got[:8]))[0]):
                if number == 10:
                    grad = got[8] / (1.0 + jnp.exp(params[10]))
                grads_ref[pl.ds(block * (8 * PLACE) + number, 8, stride=PLACE), :] = grad
            for tile in range(8):
                result(block * 8 + tile).start()

        def block_grads(block, got):
            coming = gather(block + 1)
            grads(block, got)
            return coming

        def result(tile):
            return pltpu.make_async_copy(
                grads_ref.at[pl.ds(pl.multiple_of(tile * PLACE, 8), 59), :],
                out_ref.at[:, pl.ds(pl.multiple_of(tile * 128, 128), 128)],
                out_sems.at[tile],
            )

        for copy in copies:
            copy.wait()
        grads(4, lax.fori_loop(0, 4, block_grads, gather(0)))
        for tile in range(ROWS):
            result(tile).wait()

    return kernel


def shape(*dims, dtype=F32):
    return jax.ShapeDtypeStruct(dims, dtype)


def device_of(strip):
    core = strip & 1
    z, y, x = (strip >> 1) & 3, (strip >> 3) & 3, strip >> 5
    z = z + (y & 1) * (3 - 2 * z)
    y = y + (x & 1) * (3 - 2 * y)
    return ((x * 4 + y) * 4 + z) * 2 + core


def strip_of(device):
    core = device & 1
    z, y, x = (device >> 1) & 3, (device >> 3) & 3, device >> 5
    y = y + (x & 1) * (3 - 2 * y)
    z = z + (y & 1) * (3 - 2 * z)
    return ((x * 4 + y) * 4 + z) * 2 + core


def position_of(strips):
    return lax.rem(strip_of(lax.axis_index("strip")) + strips // VIEWS // 2, strips)


def keeps(strips):
    per_view = strips // VIEWS
    place = lax.rem(position_of(strips), per_view)
    return (place != 0).astype(F32), (place != per_view - 1).astype(F32)


def exchange(chunks, strips):
    sent = chunks.reshape(strips, 1, 768)
    got = lax.all_to_all(sent, "strip", split_axis=0, concat_axis=0, tiled=True)
    return got.reshape(strips * 6, 128)


def per_device(params, camera, send_index, send_count, tile_list, target):
    strips = lax.axis_size("strip")
    per_view = strips // VIEWS
    rows_strip = target.shape[1]
    width = target.shape[2]
    focal = 0.5 * width
    centre_y = 0.5 * rows_strip * per_view
    spots = [device_of(strip) for strip in range(strips)]
    spot_rows = jnp.asarray(np.array(spots, np.int32) * 6)
    ahead = [(spots[i], spots[(i + 1) % strips]) for i in range(strips)]
    behind = [(spots[(i + 1) % strips], spots[i]) for i in range(strips)]

    chunks, place, pack = pl.pallas_call(
        owner_kernel(focal, 0.5 * width, centre_y),
        out_shape=(
            shape(strips * 6, 128),
            shape(ROWS, 128, dtype=jnp.int32),
            shape(280, 128),
        ),
        in_specs=[SMEM, SMEM, SMEM, ANY, VMEM, VMEM, VMEM],
        scratch_shapes=[
            pltpu.VMEM((strips, 128), jnp.int32),
            pltpu.VMEM((ROWS + 8, 128), jnp.int32),
            pltpu.VMEM((FEATS, ROWS, 128), F32),
            pltpu.VMEM(((ROWS + 2) * GAP, 128), F32),
            pltpu.VMEM(((ROWS + 1) * PLACE, 128), F32),
            pltpu.SemaphoreType.DMA((ROWS,)),
        ],
        name="owner",
    )(camera, send_count, spot_rows, params, send_index.T, target, tile_list)
    arrived = exchange(chunks, strips)
    moved = lax.ppermute(pack, "strip", list(enumerate(spots)))

    listed = pl.pallas_call(
        invert_kernel,
        out_shape=shape(ROWS, 128, dtype=jnp.int32),
        scratch_shapes=[pltpu.VMEM((ROWS, 128), jnp.int32)],
        compiler_params=pltpu.CompilerParams(vmem_limit_bytes=8 << 20),
        name="listed",
    )(moved)
    image, first, last, entries, colour, shifts, places, alphas, weights = pl.pallas_call(
        render_kernel,
        out_shape=(
            shape(3, 5, 16, 128),
            shape(300, 128),
            shape(300, 128),
            shape(5, ROWS, 128),
            shape(3, ROWS, 128),
            shape(strips, dtype=jnp.int32),
            shape(strips, dtype=jnp.int32),
            shape(2, 5120, 128),
            shape(2, 640 * STEP + 16, 128),
        ),
        in_specs=[VMEM, VMEM],
        out_specs=(VMEM, VMEM, VMEM, VMEM, VMEM, SMEM, SMEM, VMEM, VMEM),
        scratch_shapes=[
            pltpu.VMEM(((ROWS + 2) * GAP, 128), F32),
            pltpu.VMEM((ROWS, 128), jnp.int32),
            pltpu.VMEM(((ROWS + 5) * 24, 128), F32),
            pltpu.VMEM((640, 256), F32),
            pltpu.VMEM((640, 256), F32),
            pltpu.VMEM(((ROWS + 1) * GAP, 128), F32),
            pltpu.VMEM((2, (ROWS + 1) * GAP, 128), F32),
        ],
        compiler_params=pltpu.CompilerParams(vmem_limit_bytes=24 << 20),
        name="render",
    )(arrived, moved)
    above = lax.ppermute(last, "strip", ahead)
    below = lax.ppermute(first, "strip", behind)
    grads = pl.pallas_call(
        gradient_kernel,
        out_shape=shape(strips * 6, 128),
        in_specs=[SMEM, SMEM] + [VMEM] * 9,
        scratch_shapes=[
            pltpu.VMEM((5, 128, 128), F32),
            pltpu.VMEM((5, 128, 128), F32),
            pltpu.VMEM((5, 128, 128), F32),
            pltpu.VMEM((5, 128, 128), F32),
            pltpu.VMEM((5, 128, 128), F32),
            pltpu.VMEM((128, 128), F32),
            pltpu.VMEM((5, 656, 128), F32),
            pltpu.VMEM((3, 656, 128), F32),
            pltpu.VMEM((640, 256), F32),
            pltpu.VMEM((640, 256), F32),
            pltpu.VMEM((30, 8, 128), F32),
            pltpu.VMEM((2, (ROWS + 1) * GAP, 128), F32),
            pltpu.VMEM((ROWS * 8 + 40, 128), F32),
            pltpu.VMEM(((ROWS + 1) * GAP, 128), F32),
            pltpu.VMEM((FEATS, ROWS, 128), F32),
            pltpu.VMEM(((ROWS + 2) * GAP, 128), F32),
        ],
        compiler_params=pltpu.CompilerParams(vmem_limit_bytes=24 << 20),
        name="gradient",
    )(
        shifts, places, image, above, below, moved,
        entries, colour, listed, alphas, weights,
    )
    returned = exchange(grads, strips)
    return pl.pallas_call(
        pull_kernel(focal, 0.5 * width, centre_y),
        out_shape=shape(59, ROWS * 128),
        in_specs=[SMEM] * 3 + [ANY, VMEM, VMEM],
        out_specs=ANY,
        scratch_shapes=[
            pltpu.VMEM(((ROWS + 2) * GAP, 128), F32),
            pltpu.VMEM((strips * 6 + 8, 128), F32),
            pltpu.VMEM(((ROWS + 1) * PLACE, 128), F32),
            pltpu.VMEM(((ROWS + 1) * PLACE, 128), F32),
            pltpu.SemaphoreType.DMA((ROWS,)),
            pltpu.SemaphoreType.DMA((ROWS,)),
        ],
        compiler_params=pltpu.CompilerParams(vmem_limit_bytes=16 << 20),
        name="pull",
    )(camera, send_count, spot_rows, params, place, returned)


def solution(mesh):
    return jax.shard_map(
        per_device,
        mesh=mesh,
        in_specs=(
            P(None, "strip"),
            P(),
            P("strip", None),
            P("strip"),
            P("strip", None),
            P(None, "strip", None),
        ),
        out_specs=P(None, "strip"),
        check_vma=False,
    )
```

```python
import numpy as np

import jax
import jax.numpy as jnp
from jax import lax
from jax.experimental import pallas as pl
from jax.experimental.pallas import tpu as pltpu
from jax.sharding import PartitionSpec as P

VIEWS = 4
ROWS = 40
FEATS = 9
GAP = 24
PLACE = 72
STEP = 9
LOG2E = 1.4426950408889634
harmonic_zero = 0.28209479177387814
harmonic_one = 0.4886025119029199
harmonic_two = (
    1.0925484305920792,
    -1.0925484305920792,
    0.31539156525252005,
    -1.0925484305920792,
    0.5462742152960396,
)
harmonic_three = (
    -0.5900435899266435,
    2.890611442640554,
    -0.4570457994644658,
    0.3731763325901154,
    -0.4570457994644658,
    1.445305721320277,
    -0.5900435899266435,
)
light_term = 0.0001
contrast_term = 0.0009
F32 = jnp.float32
BF16 = jnp.bfloat16
SMEM = pl.BlockSpec(memory_space=pltpu.SMEM)
VMEM = pl.BlockSpec(memory_space=pltpu.VMEM)
ANY = pl.BlockSpec(memory_space=pl.ANY)


def iota(shape, axis):
    return lax.broadcasted_iota(jnp.int32, shape, axis)


def dot_nt(a, b):
    return lax.dot_general(a, b, (((1,), (1,)), ((), ())), preferred_element_type=F32)


def rounded(x):
    return x.astype(BF16).astype(F32)


def pick(row, lanes):
    return jnp.take_along_axis(
        jnp.broadcast_to(row, lanes.shape), lanes, axis=1, mode="promise_in_bounds"
    )


def harmonics(along_x, along_y, along_z):
    square_x = along_x * along_x
    square_y = along_y * along_y
    square_z = along_z * along_z
    return [
        harmonic_zero + 0.0 * along_x,
        -harmonic_one * along_y,
        harmonic_one * along_z,
        -harmonic_one * along_x,
        harmonic_two[0] * along_x * along_y,
        harmonic_two[1] * along_y * along_z,
        harmonic_two[2] * (2.0 * square_z - square_x - square_y),
        harmonic_two[3] * along_x * along_z,
        harmonic_two[4] * (square_x - square_y),
        harmonic_three[0] * along_y * (3.0 * square_x - square_y),
        harmonic_three[1] * along_x * along_y * along_z,
        harmonic_three[2] * along_y * (4.0 * square_z - square_x - square_y),
        harmonic_three[3] * along_z * (2.0 * square_z - 3.0 * square_x - 3.0 * square_y),
        harmonic_three[4] * along_x * (4.0 * square_z - square_x - square_y),
        harmonic_three[5] * along_z * (square_x - square_y),
        harmonic_three[6] * along_x * (square_x - 3.0 * square_y),
    ]


def project(params, camera, focal, centre_x, centre_y):
    rotation = [[camera[3 * row + col] for col in range(3)] for row in range(3)]
    mean = [params[axis] for axis in range(3)]
    placed = [
        rotation[row][0] * mean[0]
        + rotation[row][1] * mean[1]
        + rotation[row][2] * mean[2]
        + camera[9 + row]
        for row in range(3)
    ]
    depth = placed[2]
    inverse = 1.0 / depth
    screen_x = focal * placed[0] * inverse + centre_x
    screen_y = focal * placed[1] * inverse + centre_y
    quaternion = params[6:10]
    scale = lax.rsqrt(
        quaternion[0] * quaternion[0]
        + quaternion[1] * quaternion[1]
        + quaternion[2] * quaternion[2]
        + quaternion[3] * quaternion[3]
    )
    real, imag_x, imag_y, imag_z = [part * scale for part in quaternion]
    turn = [
        [
            1.0 - 2.0 * (imag_y * imag_y + imag_z * imag_z),
            2.0 * (imag_x * imag_y - real * imag_z),
            2.0 * (imag_x * imag_z + real * imag_y),
        ],
        [
            2.0 * (imag_x * imag_y + real * imag_z),
            1.0 - 2.0 * (imag_x * imag_x + imag_z * imag_z),
            2.0 * (imag_y * imag_z - real * imag_x),
        ],
        [
            2.0 * (imag_x * imag_z - real * imag_y),
            2.0 * (imag_y * imag_z + real * imag_x),
            1.0 - 2.0 * (imag_x * imag_x + imag_y * imag_y),
        ],
    ]
    scales = [jnp.exp(part) for part in params[3:6]]
    near = focal * inverse
    slant = [-near * placed[0] * inverse, -near * placed[1] * inverse]
    facing = [
        [near * rotation[row][col] + slant[row] * rotation[2][col] for col in range(3)]
        for row in range(2)
    ]
    stretch = [
        [
            (
                facing[row][0] * turn[0][col]
                + facing[row][1] * turn[1][col]
                + facing[row][2] * turn[2][col]
            )
            * scales[col]
            for col in range(3)
        ]
        for row in range(2)
    ]
    cov_xx = (
        stretch[0][0] * stretch[0][0]
        + stretch[0][1] * stretch[0][1]
        + stretch[0][2] * stretch[0][2]
        + 0.3
    )
    cov_xy = (
        stretch[0][0] * stretch[1][0]
        + stretch[0][1] * stretch[1][1]
        + stretch[0][2] * stretch[1][2]
    )
    cov_yy = (
        stretch[1][0] * stretch[1][0]
        + stretch[1][1] * stretch[1][1]
        + stretch[1][2] * stretch[1][2]
        + 0.3
    )
    over = 1.0 / (cov_xx * cov_yy - cov_xy * cov_xy)
    shrink = 1.0 / jnp.sqrt(placed[0] * placed[0] + placed[1] * placed[1] + depth * depth)
    heading = [
        (
            rotation[0][col] * placed[0]
            + rotation[1][col] * placed[1]
            + rotation[2][col] * placed[2]
        )
        * shrink
        for col in range(3)
    ]
    basis = harmonics(heading[0], heading[1], heading[2])
    colour = []
    for channel in range(3):
        total = 0.5 + basis[0] * params[11 + channel]
        for k in range(1, 16):
            total = total + basis[k] * params[11 + 3 * k + channel]
        colour.append(total)
    return [
        screen_x,
        screen_y,
        cov_yy * over,
        -cov_xy * over,
        cov_xx * over,
        colour[0],
        colour[1],
        colour[2],
    ]


def log_sigmoid(logit):
    return jnp.minimum(logit, 0.0) - jnp.log(1.0 + jnp.exp(-jnp.abs(logit)))


def send_views(count_ref, strips):
    per_view = strips // VIEWS
    offset = per_view // 2
    runs = []
    for strip in range(strips):
        view = (strip + offset) % strips // per_view
        if not runs or runs[-1][1] != view:
            runs.append([strip, view])
    return runs


def compact_ints(chunk_ref, count_ref, out_ref, steps):
    lane = iota((1, 128), 1)

    def step(number, carry):
        start, held = carry
        live = count_ref[number]
        shift = start & 127
        row = start >> 7
        chunk = pltpu.roll(chunk_ref[pl.ds(number, 1), :], shift, axis=1)
        held = jnp.where(lane >= shift, chunk, held)
        out_ref[pl.ds(row, 1), :] = held
        held = jnp.where(shift + live >= 128, chunk, held)
        return start + live, held

    lax.fori_loop(0, steps, step, (jnp.int32(0), jnp.zeros((1, 128), jnp.int32)), unroll=64)


def compact_feats(chunk_ref, place_of, table_ref, steps, spot=None):
    lane = iota((8, 128), 1)

    def step(number, carry):
        start, held, last = carry
        if spot is not None:
            chunk = chunk_ref[pl.ds(spot(number), 8), :]
        elif isinstance(number, int) and number == steps - 1:
            chunk = pltpu.roll(chunk_ref[number * 6 - 2 : number * 6 + 6, :], 6, axis=0)
        else:
            chunk = chunk_ref[pl.ds(number * 6, 8), :]
        shift, line, crossed, start = place_of(number, chunk, start)
        even = pltpu.roll(chunk, (shift + 48) & 127, axis=1)
        odd = pltpu.roll(chunk, (shift + 96) & 127, axis=1)
        chunk = pltpu.roll(chunk, shift, axis=1)
        rest = jnp.where(((lane - shift) & 127) < 48, even, pltpu.roll(odd, 7, axis=0))
        fresh = lane >= shift
        held = jnp.where(fresh, chunk, held)
        last = jnp.where(fresh, rest, last)
        base = pl.multiple_of(line, 8)
        table_ref[pl.ds(base, 8), :] = held
        table_ref[pl.ds(base + 8, 8), :] = last
        held = jnp.where(crossed, chunk, held)
        last = jnp.where(crossed, rest, last)
        return start, held, last

    zero = jnp.zeros((8, 128), F32)
    carry = lax.fori_loop(0, steps - 16, step, (jnp.int32(0), zero, zero), unroll=56)
    for number in range(steps - 16, steps):
        carry = step(number, carry)


def expand_feats(table_ref, place_of, out_ref, steps, spot, count_ref=None):
    lane = iota((8, 128), 1)
    sub = iota((8, 128), 0)
    even = (sub & 1) == 0
    mark = (sub == 1) & (lane == 127)

    def step(number, start):
        shift, line, start = place_of(number, start)
        back = 128 - shift
        base = pl.multiple_of(line, 8)
        here = lane < back
        main = jnp.where(
            here,
            pltpu.roll(table_ref[pl.ds(base, 8), :], back, axis=1),
            pltpu.roll(table_ref[pl.ds(base + GAP, 8), :], back, axis=1),
        )
        rest = jnp.where(
            here,
            pltpu.roll(table_ref[pl.ds(base + 8, 8), :], back, axis=1),
            pltpu.roll(table_ref[pl.ds(base + GAP + 8, 8), :], back, axis=1),
        )
        tail = jnp.where(even, pltpu.roll(rest, 80, axis=1), pltpu.roll(rest, 32, axis=1))
        if count_ref is not None:
            tail = jnp.where(mark, count_ref[number].astype(F32), tail)
        out_ref[pl.ds(spot(number), 6), :] = jnp.where(lane < 80, main, tail)[0:6]
        return start

    lax.fori_loop(0, steps, step, jnp.int32(0), unroll=16)


def line_of(feature):
    return feature if feature < 6 else 8 + 2 * (feature - 6)


def put_feature(table_ref, block, feature, value):
    line = line_of(feature)
    table_ref[pl.ds(block * (8 * GAP) + line, 8, stride=GAP), :] = value
    if feature >= 6:
        table_ref[pl.ds(block * (8 * GAP) + line + 1, 8, stride=GAP), :] = value


def table_line(table_ref, row, feature):
    line = row * GAP + line_of(feature)
    return table_ref[line : line + 1, :]


def fetch_params(params_ref, local_ref, sems):
    copies = [
        pltpu.make_async_copy(
            params_ref.at[:, pl.ds(tile * 128, 128)],
            local_ref.at[pl.ds(tile * PLACE, 59), :],
            sems.at[tile],
        )
        for tile in range(ROWS)
    ]
    for copy in copies:
        copy.start()
    return copies


def invert(rows_ref, out_ref):
    high = iota((ROWS, 128), 0)
    low = iota((128, 128), 0)
    lane = iota((ROWS, 128), 1).astype(F32)
    total = jnp.zeros((2 * ROWS, 128), F32)
    for pair in range(ROWS // 2):
        lefts = []
        rights = []
        for row in (2 * pair, 2 * pair + 1):
            number = rows_ref[row : row + 1, :]
            same = high == (number >> 7)
            lefts.append(
                jnp.concatenate([jnp.where(same, float(row), 0.0), jnp.where(same, lane, 0.0)], 0)
            )
            rights.append(jnp.where(low == (number & 127), 1.0, 0.0))
        total = total + dot_nt(
            jnp.concatenate(lefts, 1).astype(BF16), jnp.concatenate(rights, 1).astype(BF16)
        )
    out_ref[...] = (total[:ROWS] * 128.0 + total[ROWS:]).astype(jnp.int32)


def select_camera(camera_ref, place, run_starts):
    values = []
    for entry in range(12):
        value = jnp.full(place.shape, camera_ref[run_starts[0][1], entry], F32)
        for start, view in run_starts[1:]:
            value = jnp.where(place >= start, camera_ref[view, entry], value)
        values.append(value)
    return values


def run_bounds(count_ref, strips):
    runs = send_views(count_ref, strips)
    bounds = [(jnp.int32(0), runs[0][1])]
    for (first, _), (last, view) in zip(runs[:-1], runs[1:]):
        begin = bounds[-1][0]
        total = lax.fori_loop(
            first, last, lambda number, sum_: sum_ + count_ref[number], begin, unroll=True
        )
        bounds.append((total, view))
    return bounds


def owner_kernel(focal, centre_x, centre_y):
    def kernel(
        camera_ref, count_ref, spot_ref, params_ref, index_ref, target_ref, list_ref,
        out_ref, place_ref, pack_ref,
        wide_ref, rows_ref, feats_ref, table_ref, local_ref, sems,
    ):
        copies = fetch_params(params_ref, local_ref, sems)
        for tile in range(5):
            for channel in range(3):
                at = tile * 56 + channel * 16
                pack_ref[at : at + 16, :] = target_ref[channel, :, tile * 128 : tile * 128 + 128]
            pack_ref[tile * 56 + 48 : tile * 56 + 56, :] = list_ref[
                tile * 8 : tile * 8 + 8, :
            ].astype(F32)
        strips = index_ref.shape[1]
        wide_ref[...] = jnp.concatenate(
            [index_ref[...], jnp.zeros((128 - index_ref.shape[0], strips), jnp.int32)], 0
        ).T
        compact_ints(wide_ref, count_ref, rows_ref, strips)
        invert(rows_ref, place_ref)
        bounds = run_bounds(count_ref, strips)
        for copy in copies:
            copy.wait()

        def project_block(block, carry):
            rows = pl.ds(block * 8, 8)
            camera = select_camera(camera_ref, place_ref[rows, :], bounds)
            params = [
                local_ref[pl.ds(block * (8 * PLACE) + number, 8, stride=PLACE), :]
                for number in range(59)
            ]
            feats = project(params, camera, focal, centre_x, centre_y)
            feats.append(log_sigmoid(params[10]))
            for feature in range(FEATS):
                feats_ref[feature, rows, :] = feats[feature]
            return carry

        lax.fori_loop(0, 5, project_block, 0)

        def gather_block(block, carry):
            number = rows_ref[pl.ds(block * 8, 8), :]
            high = number >> 7
            low = number & 127
            got = [jnp.zeros((8, 128), F32)] * FEATS
            for row in range(ROWS):
                same = high == row
                for feature in range(FEATS):
                    value = pick(feats_ref[feature, row : row + 1, :], low)
                    got[feature] = jnp.where(same, value, got[feature])
            for feature in range(FEATS):
                put_feature(table_ref, block, feature, got[feature])
            return carry

        lax.fori_loop(0, 5, gather_block, 0)
        expand_feats(
            table_ref,
            lambda number, start: (start & 127, (start >> 7) * GAP, start + count_ref[number]),
            out_ref,
            strips,
            lambda number: spot_ref[number],
            count_ref,
        )

    return kernel


def pixel_basis(rows, times):
    row = iota((rows, 256), 0)
    pixel = iota((rows, 256), 1)
    x = (pixel & 15).astype(F32) - 7.5
    y = (pixel >> 4).astype(F32) - 7.5
    value = jnp.where(row < 6 * times, y * y, 0.0)
    for number, term in ((5, x * y), (4, x * x), (3, y), (2, x), (1, 1.0)):
        value = jnp.where(row < number * times, term, value)
    return value.astype(BF16)


def swap_tiles(x):
    sub = iota((8, 128), 0)
    group = iota((8, 128), 1) >> 4
    for k in (1, 2, 4):
        up = pltpu.roll(pltpu.roll(x, 8 - k, axis=0), 16 * k, axis=1)
        down = pltpu.roll(pltpu.roll(x, k, axis=0), 128 - 16 * k, axis=1)
        s = (sub & k) != 0
        g = (group & k) != 0
        x = jnp.where(s == g, x, jnp.where(g, up, down))
    return x


def coarse_fine(x):
    coarse = x.astype(BF16)
    return coarse, (x - coarse.astype(F32)).astype(BF16)


def by_entry(x):
    lane = iota((8, 128), 1)
    order = ((lane & 7) << 4) | (lane >> 3)
    return jnp.take_along_axis(swap_tiles(x), order, axis=1, mode="promise_in_bounds")


def by_tile(x):
    lane = iota((8, 128), 1)
    order = ((lane & 15) << 3) | (lane >> 4)
    return swap_tiles(jnp.take_along_axis(x, order, axis=1, mode="promise_in_bounds"))


def tile_rows(ref, half, tile):
    base = (tile >> 3) * (16 * STEP) + (tile & 7)
    return jnp.concatenate(
        [ref[half, pl.ds(base + turn * (80 * STEP), 16, stride=STEP), :] for turn in range(8)], 0
    )


def turned_colours(colour_ref, turn, group):
    return [
        pltpu.roll(
            colour_ref[channel, group * 8 : group * 8 + 8, :], 128 - turn * 16 & 127, axis=1
        )
        for channel in range(3)
    ]


def lit(turned, entry):
    return [jnp.broadcast_to(part[:, entry : entry + 1], (8, 128)) for part in turned]


def render_kernel(
    chunks_ref, moved_ref,
    image_ref, first_ref, last_ref, entries_ref, colour_ref, shift_ref, line_ref,
    alpha_ref, weight_ref,
    table_ref, order_ref, lines_ref, power_a, power_b, tint_ref, shown_ref,
):
    for tile in range(5):
        for channel in range(3):
            at = 150 + (channel * 5 + tile) * 10
            base = tile * 56 + channel * 16
            first_ref[at : at + 10, :] = moved_ref[base : base + 10, :]
            last_ref[at : at + 10, :] = moved_ref[base + 6 : base + 16, :]
    strips = chunks_ref.shape[0] // 6

    def place_of(number, chunk, start):
        live = chunk[1, 127].astype(jnp.int32)
        shift = start & 127
        line = (start >> 7) * GAP
        shift_ref[number] = shift
        line_ref[number] = line
        return shift, line, shift + live >= 128, start + live

    compact_feats(chunks_ref, place_of, table_ref, strips)
    per_view = strips // VIEWS
    top = (lax.rem(position_of(strips), per_view) * 16 + 8).astype(F32)
    for group in range(5):
        rows = slice(group * 8, group * 8 + 8)
        order_ref[rows, :] = by_entry(moved_ref[group * 56 + 48 : group * 56 + 56, :]).astype(
            jnp.int32
        )

    def entry_block(block, carry):
        rows = pl.ds(block * 8, 8)
        number = order_ref[rows, :]
        high = number >> 7
        low = number & 127
        got = [jnp.zeros((8, 128), F32)] * FEATS
        for row in range(ROWS):
            same = high == row
            for feature in range(FEATS):
                value = pick(table_line(table_ref, row, feature), low)
                got[feature] = jnp.where(same, value, got[feature])
        across = (block * 8 + (iota((8, 128), 1) & 7)) * 16 + 8
        x = got[0] - across.astype(F32)
        y = got[1] - top
        a, b, c = got[2:5]
        for slot, value in enumerate((x, y, a, b, c)):
            entries_ref[slot, rows, :] = value
        terms = [
            got[8] - 0.5 * (a * x * x + c * y * y) - b * x * y,
            a * x + b * y,
            c * y + b * x,
            -0.5 * a,
            -b,
            -0.5 * c,
        ]
        for slot, term in enumerate(terms):
            term = term * LOG2E
            for part in range(3):
                piece = rounded(term)
                lines_ref[pl.ds(block * 24 + slot * 3 + part, 8, stride=120), :] = piece
                term = term - piece
        for slot in range(18, 24):
            lines_ref[pl.ds(block * 24 + slot, 8, stride=120), :] = jnp.zeros((8, 128), F32)
        for channel in range(3):
            colour_ref[channel, rows, :] = got[5 + channel]
        return carry

    lax.fori_loop(0, 5, entry_block, 0)
    values = [
        by_tile(colour_ref[channel, group * 8 : group * 8 + 8, :])
        for group in range(5)
        for channel in range(3)
    ]
    for number, value in enumerate(values):
        group, channel = divmod(number, 3)
        colour_ref[channel, group * 8 : group * 8 + 8, :] = value
        for part in range(3):
            piece = rounded(value)
            tint_ref[pl.ds(group * (8 * GAP) + channel * 3 + part, 8, stride=GAP), :] = piece
            value = value - piece
    basis = pixel_basis(24, 3)

    def powers(turn, power_ref):
        for part in range(5):
            lines = lines_ref[pl.ds(pl.multiple_of((turn * 5 + part) * 24, 8), 24), :]
            power_ref[part * 128 : part * 128 + 128, :] = jnp.dot(
                lines.T.astype(BF16), basis, preferred_element_type=F32
            )

    def scan(turn, power_ref, through):
        through = list(through)
        for entry in range(16):
            for group in range(5):
                at = group * 128 + entry * 8
                for half in range(2):
                    slot = group * 2 + half
                    alpha = jnp.exp2(power_ref[at : at + 8, half * 128 : half * 128 + 128])
                    weight = alpha * through[slot]
                    through[slot] = through[slot] - weight
                    alpha_ref[half, pl.ds(turn * 640 + at, 8), :] = alpha
                    spot = pl.ds(turn * (80 * STEP) + (group * 16 + entry) * STEP, 8)
                    weight_ref[half, spot, :] = weight
        return tuple(through)

    def blend(pair, through):
        powers(2 * pair + 1, power_b)
        through = scan(2 * pair, power_a, through)
        powers(jnp.minimum(2 * pair + 2, 7), power_a)
        through = scan(2 * pair + 1, power_b, through)
        return through

    powers(0, power_a)
    lax.fori_loop(0, 4, blend, (jnp.ones((8, 128), F32),) * 10)

    def tints(tile, carry):
        at = pl.ds(pl.multiple_of(tile * GAP, 8), 16)
        tint = tint_ref[at, :].astype(BF16)
        halves = [coarse_fine(tile_rows(weight_ref, half, tile)) for half in range(2)]
        weight = jnp.concatenate(
            [jnp.concatenate([halves[0][part], halves[1][part]], 1) for part in range(2)], 0
        )
        total = jnp.dot(jnp.concatenate([tint, tint], 1), weight, preferred_element_type=F32)
        for half in range(2):
            shown_ref[half, at, :] = total[:, half * 128 : half * 128 + 128]
        return carry

    lax.fori_loop(0, ROWS, tints, 0, unroll=8)
    for group in range(5):
        for channel in range(3):
            for half in range(2):
                parts = [
                    shown_ref[half, pl.ds(group * (8 * GAP) + channel * 3 + part, 8, stride=GAP), :]
                    for part in range(3)
                ]
                image_ref[channel, group, half * 8 : half * 8 + 8, :] = swap_tiles(
                    parts[0] + parts[1] + parts[2]
                )
            at = (channel * 5 + group) * 10
            first_ref[at : at + 10, :] = image_ref[channel, group, 0:10, :]
            last_ref[at : at + 10, :] = image_ref[channel, group, 6:16, :]


def window_weights():
    offsets = np.arange(11, dtype=np.float64) - 5.0
    raw = np.exp(-offsets * offsets / 4.5)
    return [float(value) for value in raw / raw.sum()]


WINDOW = window_weights()


def tap_sum(load):
    total = WINDOW[5] * load(5)
    for k in range(5):
        total = total + WINDOW[k] * (load(k) + load(10 - k))
    return total


def down_rows(field_ref, slot, out_ref):
    for tile in range(5):
        for channel in range(3):
            base = channel * 40
            out_ref[base : base + 32, :] = tap_sum(
                lambda k: field_ref[tile, base + k : base + k + 32, :]
            )
        yield tile, out_ref[...].T


def extend(ext_ref, own, above, below, keep_above, keep_below):
    for tile in range(5):
        for channel in range(3):
            base = channel * 40
            ext_ref[tile, base : base + 10, :] = above(channel, tile) * keep_above
            ext_ref[tile, base + 10 : base + 26, :] = own(channel, tile)
            ext_ref[tile, base + 26 : base + 36, :] = below(channel, tile) * keep_below
            ext_ref[tile, base + 36 : base + 40, :] = jnp.zeros((4, 128), F32)
        ext_ref[tile, 120:128, :] = jnp.zeros((8, 128), F32)


def clear_ends(ref, slot):
    ref[slot, 0:8, :] = jnp.zeros((8, 128), F32)
    ref[slot, 648:656, :] = jnp.zeros((8, 128), F32)


def invert_kernel(moved_ref, out_ref, rows_ref):
    for group in range(5):
        rows_ref[group * 8 : group * 8 + 8, :] = moved_ref[
            group * 56 + 48 : group * 56 + 56, :
        ].astype(jnp.int32)
    invert(rows_ref, out_ref)


def gradient_kernel(
    shift_ref, line_ref, image_ref, above_ref, below_ref, moved_ref,
    entries_ref, colour_ref, place_ref, alpha_ref, weight_ref,
    out_ref,
    ext_ref, square_ref, cross_ref, truth_ref, ideal_ref, rows_ref, cols_ref, parts_ref,
    pull_a, pull_b, light_ref, split_ref, sums_ref, tint_ref, feats_ref, table_ref,
):
    strips = out_ref.shape[0] // 6
    keep_above, keep_below = keeps(strips)
    def rim(base):
        return lambda ref: lambda channel, tile: ref[
            base + (channel * 5 + tile) * 10 : base + (channel * 5 + tile) * 10 + 10, :
        ]

    extend(
        ext_ref,
        lambda channel, tile: image_ref[channel, tile],
        rim(0)(above_ref),
        rim(0)(below_ref),
        keep_above,
        keep_below,
    )
    extend(
        truth_ref,
        lambda channel, tile: moved_ref[tile * 56 + channel * 16 : tile * 56 + channel * 16 + 16, :],
        rim(150)(above_ref),
        rim(150)(below_ref),
        keep_above,
        keep_below,
    )
    for tile in range(5):
        square_ref[tile] = ext_ref[tile] * ext_ref[tile]
        cross_ref[tile] = ext_ref[tile] * truth_ref[tile]
        ideal_ref[tile] = truth_ref[tile] * truth_ref[tile]
    rows_ref[...] = jnp.zeros((128, 128), F32)
    for slot in range(3):
        clear_ends(parts_ref, slot)
    for slot, source in enumerate((ext_ref, square_ref, cross_ref, truth_ref, ideal_ref)):
        clear_ends(cols_ref, slot)
        for tile, turned in down_rows(source, slot, rows_ref):
            cols_ref[slot, 8 + tile * 128 : 136 + tile * 128, :] = turned
    lane = iota((8, 128), 1)
    row = lane - jnp.where(lane >= 80, 80, jnp.where(lane >= 40, 40, 0))
    live = jnp.where(row < 5, keep_above, jnp.where(row >= 21, keep_below, 1.0))
    live = jnp.where((row < 26) & (lane < 120), live, 0.0)[0:1, :]

    def similarity(step, carry):
        base = step * 32
        mean_x, power_x, cross, mean_y, power_y = [
            tap_sum(lambda k: cols_ref[slot, pl.ds(base + 3 + k, 32), :]) for slot in range(5)
        ]
        both = mean_x * mean_y
        squares = mean_x * mean_x + mean_y * mean_y
        light_up = 2.0 * both + light_term
        light_down = squares + light_term
        sharp_up = 2.0 * (cross - both) + contrast_term
        sharp_down = power_x + power_y - squares + contrast_term
        over = 1.0 / (light_down * sharp_down)
        score = light_up * sharp_up * over
        scale = live * over
        cross_grad = -2.0 * light_up * scale
        power_grad = score * light_down * scale
        mean_grad = (
            -2.0 * mean_y * (sharp_up - light_up) + 2.0 * mean_x * score * (sharp_down - light_down)
        ) * scale
        at = pl.ds(base + 8, 32)
        parts_ref[0, at, :] = mean_grad
        parts_ref[1, at, :] = power_grad
        parts_ref[2, at, :] = cross_grad
        return carry

    lax.fori_loop(0, 20, similarity, 0, unroll=5)
    for tile in range(5):
        for slot in range(3):
            turned = tap_sum(
                lambda k: parts_ref[slot, tile * 128 + 3 + k : tile * 128 + 131 + k, :]
            ).T
            (square_ref, cross_ref, cols_ref)[slot][0, 0:128, :] = turned
        for channel in range(3):
            base = channel * 40
            down = [
                tap_sum(lambda k: (square_ref, cross_ref, cols_ref)[slot][0, base + k : base + k + 16, :])
                for slot in range(3)
            ]
            own = image_ref[channel, tile]
            truth = truth_ref[tile, base + 10 : base + 26, :]
            pull = down[0] + 2.0 * own * down[1] + truth * down[2]
            for half in range(2):
                value = swap_tiles(pull[half * 8 : half * 8 + 8])
                light_ref[tile * 6 + half * 3 + channel] = value
                for part in range(3):
                    piece = rounded(value)
                    split_ref[half, pl.ds(tile * (8 * GAP) + channel * 3 + part, 8, stride=GAP), :] = piece
                    value = value - piece
    moments = pixel_basis(16, 1)

    def scan(turn, pull_ref, behind):
        behind = list(behind)
        turned = [
            [
                pltpu.roll(
                    colour_ref[channel, group * 8 : group * 8 + 8, :], 128 - turn * 16 & 127, axis=1
                )
                for channel in range(3)
            ]
            for group in range(5)
        ]
        for entry in range(15, -1, -1):
            for group in range(5):
                at = group * 128 + entry * 8
                rows = pl.ds(turn * 640 + at, 8)
                spot = pl.ds(turn * (80 * STEP) + (group * 16 + entry) * STEP, 8)
                colour = [
                    jnp.broadcast_to(turned[group][channel][:, entry : entry + 1], (8, 128))
                    for channel in range(3)
                ]
                for half in range(2):
                    slot = group * 2 + half
                    light = group * 6 + half * 3
                    value = (
                        colour[0] * light_ref[light]
                        + colour[1] * light_ref[light + 1]
                        + colour[2] * light_ref[light + 2]
                    )
                    delta = value - behind[slot]
                    behind[slot] = behind[slot] + alpha_ref[half, rows, :] * delta
                    pull_ref[at : at + 8, half * 128 : half * 128 + 128] = (
                        weight_ref[half, spot, :] * delta
                    )
        return tuple(behind)

    def reduce(turn, pull_ref):
        for part in range(5):
            coarse, fine = coarse_fine(pull_ref[part * 128 : part * 128 + 128, :])
            total = dot_nt(moments, coarse) + dot_nt(moments, fine)
            sums_ref[pl.ds(pl.multiple_of((turn * 5 + part) * 8, 8), 8), :] = total[0:8]

    def backward(count, behind):
        turn = 7 - 2 * count
        reduce(turn + 1, pull_b)
        behind = scan(turn, pull_a, behind)
        reduce(turn, pull_a)
        return scan(turn - 1, pull_b, behind)

    pull_b[...] = jnp.zeros((640, 256), F32)
    lax.fori_loop(0, 4, backward, (jnp.zeros((8, 128), F32),) * 10)
    reduce(0, pull_b)

    def tints(tile, carry):
        at = pl.ds(pl.multiple_of(tile * GAP, 8), 16)
        halves = [coarse_fine(tile_rows(weight_ref, half, tile)) for half in range(2)]
        weight = jnp.concatenate(
            [jnp.concatenate([halves[0][part], halves[1][part]], 1) for part in range(2)], 0
        )
        light = jnp.concatenate([split_ref[half, at, :].astype(BF16) for half in range(2)], 1)
        total = dot_nt(light, weight)
        total = total[:, 0:128] + total[:, 128:256]
        tint_ref[at, :] = total
        return carry

    lax.fori_loop(0, ROWS, tints, 0, unroll=8)

    def entry_grads(block, carry):
        rows = pl.ds(block * 8, 8)
        zeroth, by_x, by_y, by_xx, by_xy, by_yy = [
            sums_ref[pl.ds(block * 8 + slot, 8, stride=40), :] for slot in range(6)
        ]
        x, y, a, b, c = [entries_ref[slot, rows, :] for slot in range(5)]
        off_x = by_x - x * zeroth
        off_y = by_y - y * zeroth
        feats_ref[0, rows, :] = a * off_x + b * off_y
        feats_ref[1, rows, :] = c * off_y + b * off_x
        feats_ref[2, rows, :] = -0.5 * (by_xx - x * (by_x + off_x))
        feats_ref[3, rows, :] = x * by_y + y * off_x - by_xy
        feats_ref[4, rows, :] = -0.5 * (by_yy - y * (by_y + off_y))
        feats_ref[8, rows, :] = zeroth
        for channel in range(3):
            feats_ref[5 + channel, rows, :] = (
                tint_ref[pl.ds(block * (8 * GAP) + channel * 3, 8, stride=GAP), :]
                + tint_ref[pl.ds(block * (8 * GAP) + channel * 3 + 1, 8, stride=GAP), :]
                + tint_ref[pl.ds(block * (8 * GAP) + channel * 3 + 2, 8, stride=GAP), :]
            )
        return carry

    lax.fori_loop(0, 5, entry_grads, 0)
    values = [
        by_entry(feats_ref[5 + channel, group * 8 : group * 8 + 8, :])
        for group in range(5)
        for channel in range(3)
    ]
    for number, value in enumerate(values):
        group, channel = divmod(number, 3)
        feats_ref[5 + channel, group * 8 : group * 8 + 8, :] = value

    def gather_block(block, carry):
        place = place_ref[pl.ds(block * 8, 8), :]
        tile = place >> 7
        entry = place & 127
        high = (tile & 56) | (entry >> 4)
        low = ((entry & 15) << 3) | (tile & 7)
        got = [jnp.zeros((8, 128), F32)] * FEATS
        for row in range(ROWS):
            same = high == row
            for feature in range(FEATS):
                value = pick(feats_ref[feature, row : row + 1, :], low)
                got[feature] = jnp.where(same, value, got[feature])
        for feature in range(FEATS):
            put_feature(table_ref, block, feature, got[feature])
        return carry

    lax.fori_loop(0, 5, gather_block, 0)
    expand_feats(
        table_ref,
        lambda number, start: (shift_ref[number], line_ref[number], start),
        out_ref,
        strips,
        lambda number: number * 6,
    )


def pull_kernel(focal, centre_x, centre_y):
    def kernel(
        camera_ref, count_ref, spot_ref, params_ref, place_ref, chunks_ref, out_ref,
        table_ref, wide_ref, local_ref, grads_ref, sems, out_sems,
    ):
        copies = fetch_params(params_ref, local_ref, sems)
        strips = chunks_ref.shape[0] // 6
        wide_ref[0 : strips * 6, :] = chunks_ref[...]
        compact_feats(
            wide_ref,
            lambda number, chunk, start: (
                start & 127,
                (start >> 7) * GAP,
                (start & 127) + count_ref[number] >= 128,
                start + count_ref[number],
            ),
            table_ref,
            strips,
            lambda number: spot_ref[number],
        )
        bounds = run_bounds(count_ref, strips)

        def gather(block):
            place = place_ref[pl.ds(block * 8, 8), :]
            high = place >> 7
            low = place & 127
            got = [jnp.zeros((8, 128), F32)] * FEATS
            for row in range(ROWS):
                same = high == row
                for feature in range(FEATS):
                    value = pick(table_line(table_ref, row, feature), low)
                    got[feature] = jnp.where(same, value, got[feature])
            return tuple(got)

        def grads(block, got):
            camera = select_camera(camera_ref, place_ref[pl.ds(block * 8, 8), :], bounds)
            params = [
                local_ref[pl.ds(block * (8 * PLACE) + number, 8, stride=PLACE), :]
                for number in range(59)
            ]
            ignored, pull = jax.vjp(
                lambda values: project(values, camera, focal, centre_x, centre_y), params
            )
            for number, grad in enumerate(pull(list(got[:8]))[0]):
                if number == 10:
                    grad = got[8] / (1.0 + jnp.exp(params[10]))
                grads_ref[pl.ds(block * (8 * PLACE) + number, 8, stride=PLACE), :] = grad
            for tile in range(8):
                result(block * 8 + tile).start()

        def block_grads(block, got):
            coming = gather(block + 1)
            grads(block, got)
            return coming

        def result(tile):
            return pltpu.make_async_copy(
                grads_ref.at[pl.ds(pl.multiple_of(tile * PLACE, 8), 59), :],
                out_ref.at[:, pl.ds(pl.multiple_of(tile * 128, 128), 128)],
                out_sems.at[tile],
            )

        for copy in copies:
            copy.wait()
        grads(4, lax.fori_loop(0, 4, block_grads, gather(0)))
        for tile in range(ROWS):
            result(tile).wait()

    return kernel


def shape(*dims, dtype=F32):
    return jax.ShapeDtypeStruct(dims, dtype)


def device_of(strip):
    core = strip & 1
    z, y, x = (strip >> 1) & 3, (strip >> 3) & 3, strip >> 5
    z = z + (y & 1) * (3 - 2 * z)
    y = y + (x & 1) * (3 - 2 * y)
    return ((x * 4 + y) * 4 + z) * 2 + core


def strip_of(device):
    core = device & 1
    z, y, x = (device >> 1) & 3, (device >> 3) & 3, device >> 5
    y = y + (x & 1) * (3 - 2 * y)
    z = z + (y & 1) * (3 - 2 * z)
    return ((x * 4 + y) * 4 + z) * 2 + core


def position_of(strips):
    return lax.rem(strip_of(lax.axis_index("strip")) + strips // VIEWS // 2, strips)


def keeps(strips):
    per_view = strips // VIEWS
    place = lax.rem(position_of(strips), per_view)
    return (place != 0).astype(F32), (place != per_view - 1).astype(F32)


def exchange(chunks, strips):
    sent = chunks.reshape(strips, 1, 768)
    got = lax.all_to_all(sent, "strip", split_axis=0, concat_axis=0, tiled=True)
    return got.reshape(strips * 6, 128)


def per_device(params, camera, send_index, send_count, tile_list, target):
    strips = lax.axis_size("strip")
    per_view = strips // VIEWS
    rows_strip = target.shape[1]
    width = target.shape[2]
    focal = 0.5 * width
    centre_y = 0.5 * rows_strip * per_view
    spots = [device_of(strip) for strip in range(strips)]
    spot_rows = jnp.asarray(np.array(spots, np.int32) * 6)
    ahead = [(spots[i], spots[(i + 1) % strips]) for i in range(strips)]
    behind = [(spots[(i + 1) % strips], spots[i]) for i in range(strips)]

    chunks, place, pack = pl.pallas_call(
        owner_kernel(focal, 0.5 * width, centre_y),
        out_shape=(
            shape(strips * 6, 128),
            shape(ROWS, 128, dtype=jnp.int32),
            shape(280, 128),
        ),
        in_specs=[SMEM, SMEM, SMEM, ANY, VMEM, VMEM, VMEM],
        scratch_shapes=[
            pltpu.VMEM((strips, 128), jnp.int32),
            pltpu.VMEM((ROWS + 8, 128), jnp.int32),
            pltpu.VMEM((FEATS, ROWS, 128), F32),
            pltpu.VMEM(((ROWS + 2) * GAP, 128), F32),
            pltpu.VMEM(((ROWS + 1) * PLACE, 128), F32),
            pltpu.SemaphoreType.DMA((ROWS,)),
        ],
        name="owner",
    )(camera, send_count, spot_rows, params, send_index.T, target, tile_list)
    arrived = exchange(chunks, strips)
    moved = lax.ppermute(pack, "strip", list(enumerate(spots)))

    listed = pl.pallas_call(
        invert_kernel,
        out_shape=shape(ROWS, 128, dtype=jnp.int32),
        scratch_shapes=[pltpu.VMEM((ROWS, 128), jnp.int32)],
        compiler_params=pltpu.CompilerParams(vmem_limit_bytes=8 << 20),
        name="listed",
    )(moved)
    image, first, last, entries, colour, shifts, places, alphas, weights = pl.pallas_call(
        render_kernel,
        out_shape=(
            shape(3, 5, 16, 128),
            shape(300, 128),
            shape(300, 128),
            shape(5, ROWS, 128),
            shape(3, ROWS, 128),
            shape(strips, dtype=jnp.int32),
            shape(strips, dtype=jnp.int32),
            shape(2, 5120, 128),
            shape(2, 640 * STEP + 16, 128),
        ),
        in_specs=[VMEM, VMEM],
        out_specs=(VMEM, VMEM, VMEM, VMEM, VMEM, SMEM, SMEM, VMEM, VMEM),
        scratch_shapes=[
            pltpu.VMEM(((ROWS + 2) * GAP, 128), F32),
            pltpu.VMEM((ROWS, 128), jnp.int32),
            pltpu.VMEM(((ROWS + 5) * 24, 128), F32),
            pltpu.VMEM((640, 256), F32),
            pltpu.VMEM((640, 256), F32),
            pltpu.VMEM(((ROWS + 1) * GAP, 128), F32),
            pltpu.VMEM((2, (ROWS + 1) * GAP, 128), F32),
        ],
        compiler_params=pltpu.CompilerParams(vmem_limit_bytes=24 << 20),
        name="render",
    )(arrived, moved)
    above = lax.ppermute(last, "strip", ahead)
    below = lax.ppermute(first, "strip", behind)
    grads = pl.pallas_call(
        gradient_kernel,
        out_shape=shape(strips * 6, 128),
        in_specs=[SMEM, SMEM] + [VMEM] * 9,
        scratch_shapes=[
            pltpu.VMEM((5, 128, 128), F32),
            pltpu.VMEM((5, 128, 128), F32),
            pltpu.VMEM((5, 128, 128), F32),
            pltpu.VMEM((5, 128, 128), F32),
            pltpu.VMEM((5, 128, 128), F32),
            pltpu.VMEM((128, 128), F32),
            pltpu.VMEM((5, 656, 128), F32),
            pltpu.VMEM((3, 656, 128), F32),
            pltpu.VMEM((640, 256), F32),
            pltpu.VMEM((640, 256), F32),
            pltpu.VMEM((30, 8, 128), F32),
            pltpu.VMEM((2, (ROWS + 1) * GAP, 128), F32),
            pltpu.VMEM((ROWS * 8 + 40, 128), F32),
            pltpu.VMEM(((ROWS + 1) * GAP, 128), F32),
            pltpu.VMEM((FEATS, ROWS, 128), F32),
            pltpu.VMEM(((ROWS + 2) * GAP, 128), F32),
        ],
        compiler_params=pltpu.CompilerParams(vmem_limit_bytes=24 << 20),
        name="gradient",
    )(
        shifts, places, image, above, below, moved,
        entries, colour, listed, alphas, weights,
    )
    returned = exchange(grads, strips)
    return pl.pallas_call(
        pull_kernel(focal, 0.5 * width, centre_y),
        out_shape=shape(59, ROWS * 128),
        in_specs=[SMEM] * 3 + [ANY, VMEM, VMEM],
        out_specs=ANY,
        scratch_shapes=[
            pltpu.VMEM(((ROWS + 2) * GAP, 128), F32),
            pltpu.VMEM((strips * 6 + 8, 128), F32),
            pltpu.VMEM(((ROWS + 1) * PLACE, 128), F32),
            pltpu.VMEM(((ROWS + 1) * PLACE, 128), F32),
            pltpu.SemaphoreType.DMA((ROWS,)),
            pltpu.SemaphoreType.DMA((ROWS,)),
        ],
        compiler_params=pltpu.CompilerParams(vmem_limit_bytes=16 << 20),
        name="pull",
    )(camera, send_count, spot_rows, params, place, returned)


def solution(mesh):
    return jax.shard_map(
        per_device,
        mesh=mesh,
        in_specs=(
            P(None, "strip"),
            P(),
            P("strip", None),
            P("strip"),
            P("strip", None),
            P(None, "strip", None),
        ),
        out_specs=P(None, "strip"),
        check_vma=False,
    )
```
